32 devices in a mesh: grp: 2 (over y), freq: 16 (over z, x, core).
Axes of the slice: x: 2, y: 2, z: 4, core: 2. Of those that a mesh axis runs over, the one named last changes fastest.
Arguments:
- source_field: bfloat16 [4, 16, 512, 256], P('grp', 'freq'), parts along dimension 0, may hold values from -6 to 6
- receiver_field: bfloat16 [4, 16, 512, 256], P('grp', 'freq'), parts along dimension 0, may hold values from -6 to 6
- slowness_slabs: bfloat16 [32, 768, 512], P(('grp', 'freq')), parts along dimension 0, may hold values from 0.3984375 to 1.1953125
- slab_map: int32 [4], P('grp'), parts along dimension 0, may hold values from 0 to 15
- reference_gaps: float32 [4, 3], P('grp'), parts along dimension 0, may hold values from 0.1 to 0.3
- reference_index: int32 [4, 512, 256], P('grp'), parts along dimension 0, may hold values from 0 to 1
- frequency_bins: int32 [16], replicated, may hold values from 10 to 120
- shot_corner: int32 [4], P('grp'), parts along dimension 0, may hold values from 0 to 256
Outputs:
- image: float32 [4, 512, 256, 256], P('grp', 'freq'), parts along dimension 0
The draws below stay inside these ranges and needn't reach their ends.
There are 2 independent parts, one for each index of `grp`. The reference program is written for one: setup_inputs(seed, part) draws one part's arguments, and reference() takes and returns one part's arrays. A program takes and returns all parts, laid end to end along the dimension named above; an argument that names none is the same for every part. Nothing has to cross between parts.
All inputs are finite; a program needn't handle non-finite values.
Results may differ from the reference program's by a relative error of at most 0.014.
Values may be sent and summed in bfloat16 or wider, within the bound.
A program may use at most 128 MiB of HBM per device.

```python
import math
import jax
import jax.numpy as jnp
from jax import lax

NX = 512
NY = 256
LAGS = 256
NREF = 3
DEPTHS = 2
SPAN = 256
NW = 16
SLABS = 16
MX = 768
MY = 512


def place_ends(values, key, smallest, high):
    dims = values.shape
    spot = [jax.random.randint(jax.random.fold_in(key, axis), (), 0, dims[axis]) for axis in range(len(dims))]
    values = values.at[tuple(spot)].set(smallest)
    longest = dims.index(max(dims))
    spot[longest] = (spot[longest] + 1) % dims[longest]
    return values.at[tuple(spot)].set(high)


def steps_of(key, dims, pieces, low, largest):
    level = 1.0
    for dim, blocks in pieces:
        steps = jax.random.uniform(jax.random.fold_in(jax.random.fold_in(key, 6), dim), (blocks,), jnp.float32, low / len(pieces), largest / len(pieces))
        level = level * jnp.repeat(jnp.exp(steps), dims[dim] // blocks).reshape((-1,) + (1,) * (len(dims) - 1 - dim))
    return level


def normal_values(stream_key, shape, spread, reach, shards=(), held_as=jnp.bfloat16):
    level = steps_of(stream_key, shape, shards, -0.22, 0.18) if shards else 1.0
    result = jax.random.normal(stream_key, shape, jnp.float32) * spread * level
    return jnp.minimum(jnp.maximum(result, -reach), reach).astype(held_as)


def setup_inputs(seed: int = 0, part: int = 0) -> dict:
    keys = jax.random.split(jax.random.key(seed), 9)
    part_splits = jax.random.split(jax.random.fold_in(keys[8], part), 9)
    source_field = normal_values(part_splits[0], (2, NW, NX, NY), 1.0, 6.0, ((1, 16),))
    receiver_field = normal_values(part_splits[1], (2, NW, NX, NY), 1.0, 6.0, ((1, 16),))
    slowness_slabs = jnp.clip(0.3984375 + 0.796875 * jax.random.uniform(part_splits[2], (SLABS, MX, MY), jnp.float32) ** steps_of(part_splits[2], (SLABS, MX, MY), ((0, 16),), -0.2, 0.2), 0.3984375, 1.1953125).astype(jnp.bfloat16)
    slab_map = jax.random.randint(part_splits[3], (DEPTHS,), 0, SLABS).astype(jnp.int32)
    reference_gaps = jnp.clip(jnp.exp(jax.random.uniform(part_splits[4], (DEPTHS, NREF), jnp.float32, math.log(0.1), math.log(0.3))), 0.1, 0.3)
    reference_index = place_ends(jax.random.randint(part_splits[5], (DEPTHS, NX, NY), 0, NREF - 1), jax.random.fold_in(part_splits[5], 1), 0, (NREF - 1) - 1).astype(jnp.int32)
    frequency_bins = place_ends(jax.random.randint(keys[6], (NW,), 10, 121), jax.random.fold_in(keys[6], 1), 10, 120).astype(jnp.int32)
    shot_corner = jax.random.randint(part_splits[7], (2,), 0, SPAN + 1).astype(jnp.int32)
    return {"source_field": source_field, "receiver_field": receiver_field, "slowness_slabs": slowness_slabs, "slab_map": slab_map, "reference_gaps": reference_gaps, "reference_index": reference_index, "frequency_bins": frequency_bins, "shot_corner": shot_corner}


cell_width = 0.0125
layer_thick = 0.0125
bin_hertz = 0.5
period_bins = 500
slow_base = 0.3

def transform_table(length, forward):
    grid_steps = jnp.arange(length, dtype=jnp.int32)
    phases = jnp.mod(grid_steps[:, None] * grid_steps[None, :], length).astype(jnp.float32)
    angles = phases * (2.0 * math.pi / length)
    norm_scale = 1.0 / math.sqrt(length)
    cosine = jnp.cos(angles) * norm_scale
    sine_part = jnp.sin(angles) * norm_scale
    if forward:
        cross_term = -sine_part
    else:
        cross_term = sine_part
    return jnp.stack([jnp.stack([cosine, cross_term]), jnp.stack([-cross_term, cosine])]).astype(jnp.bfloat16)

def wave_numbers(length):
    grid_steps = jnp.arange(length, dtype=jnp.int32)
    folded = jnp.where(grid_steps < length // 2, grid_steps, grid_steps - length).astype(jnp.float32)
    return folded * (2.0 * math.pi / (length * cell_width))

def lag_table(frequency_bins, lag_count):
    offsets = jnp.arange(lag_count, dtype=jnp.int32) - lag_count // 2
    cycles = jnp.mod(frequency_bins[:, None] * offsets[None, :], period_bins).astype(jnp.float32)
    angles = cycles * (2.0 * math.pi / period_bins)
    return jnp.stack([jnp.cos(angles), -jnp.sin(angles)]).astype(jnp.bfloat16)

def phase_factors(angular, references, squares):
    radicand = (angular * references[:, None, None]) ** 2 - squares[None]
    vertical = jnp.sqrt(jnp.maximum(radicand, 0.0))
    fading = jnp.exp(-jnp.sqrt(jnp.maximum(-radicand, 0.0)) * layer_thick)
    return (fading * jnp.cos(vertical * layer_thick), fading * jnp.sin(vertical * layer_thick))

def rotate(field_pair, turn_angle):
    return jnp.stack([jnp.cos(turn_angle) * field_pair[0] - jnp.sin(turn_angle) * field_pair[1], jnp.cos(turn_angle) * field_pair[1] + jnp.sin(turn_angle) * field_pair[0]])

def extrapolate(field, angular, slowness, references, bracket, direction, tables, squares):
    forward_x, forward_y, inverse_x, inverse_y = tables
    half_done = jnp.einsum('cxy,cdyk->dxk', field.astype(jnp.float32), forward_y).astype(jnp.bfloat16)
    spectrum = jnp.einsum('cdxk,cxy->dky', forward_x, half_done.astype(jnp.float32))
    cos_part, sin_part = phase_factors(angular, references, squares)
    sin_part = direction * sin_part
    shifted = jnp.stack([cos_part * spectrum[0] - sin_part * spectrum[1], cos_part * spectrum[1] + sin_part * spectrum[0]], axis=1).astype(jnp.bfloat16)
    returned = jnp.einsum('cdxk,jcxy->jdky', inverse_x, shifted.astype(jnp.float32)).astype(jnp.bfloat16)
    refocused = jnp.einsum('jcxy,cdyk->jdxk', returned.astype(jnp.float32), inverse_y)
    lower_pair = bracket == 0
    lower_field = jnp.where(lower_pair[None], refocused[0], refocused[1])
    upper_field = jnp.where(lower_pair[None], refocused[1], refocused[2])
    slow_low = jnp.where(lower_pair, references[0], references[1])
    slow_high = jnp.where(lower_pair, references[1], references[2])
    weight = jnp.clip((slowness - slow_low) / (slow_high - slow_low), 0.0, 1.0)
    turn_low = direction * angular * layer_thick * (slowness - slow_low)
    turn_high = direction * angular * layer_thick * (slowness - slow_high)
    mixed = (1.0 - weight) * rotate(lower_field, turn_low) + weight * rotate(upper_field, turn_high)
    return mixed.astype(jnp.bfloat16)

def reference(source_field, receiver_field, slowness_slabs, slab_map, reference_gaps, reference_index, frequency_bins, shot_corner):
    tables = (transform_table(NX, True).astype(jnp.float32), transform_table(NY, True).astype(jnp.float32), transform_table(NX, False).astype(jnp.float32), transform_table(NY, False).astype(jnp.float32))
    wave_x = wave_numbers(NX)
    wave_y = wave_numbers(NY)
    squares = wave_x[:, None] ** 2 + wave_y[None, :] ** 2
    omegas = frequency_bins.astype(jnp.float32) * (2.0 * math.pi * bin_hertz)
    slow_list = []
    ref_list = []
    for depth_step in range(DEPTHS):
        slab = lax.dynamic_index_in_dim(slowness_slabs, slab_map[depth_step].astype(jnp.int32), 0, keepdims=False)
        window = lax.dynamic_slice(slab, (shot_corner[0].astype(jnp.int32), shot_corner[1].astype(jnp.int32)), (NX, NY))
        slow_list.append(window.astype(jnp.float32))
        ref_list.append(slow_base + jnp.cumsum(reference_gaps[depth_step]))

    def one_frequency(inputs):
        source, receiver, angular = inputs
        crosses = []
        for depth_step in range(DEPTHS):
            source = extrapolate(source, angular, slow_list[depth_step], ref_list[depth_step], reference_index[depth_step], 1.0, tables, squares)
            receiver = extrapolate(receiver, angular, slow_list[depth_step], ref_list[depth_step], reference_index[depth_step], -1.0, tables, squares)
            src_values = source.astype(jnp.float32)
            rec_values = receiver.astype(jnp.float32)
            real_part = src_values[0] * rec_values[0] + src_values[1] * rec_values[1]
            imag_part = src_values[0] * rec_values[1] - src_values[1] * rec_values[0]
            crosses.append(jnp.stack([real_part, imag_part]).astype(jnp.bfloat16))
        return jnp.stack(crosses)
    crosses = lax.map(one_frequency, (jnp.moveaxis(source_field, 1, 0), jnp.moveaxis(receiver_field, 1, 0), omegas))
    lag_weights = lag_table(frequency_bins, LAGS).astype(jnp.float32)
    images = []
    for depth_step in range(DEPTHS):
        summed = jnp.einsum('wcxy,cwl->xyl', crosses[:, depth_step].astype(jnp.float32), lag_weights)
        images.append(summed * NW ** (-0.5))
    return jnp.stack(images)
```

```python
import functools
import math

import jax
import jax.numpy as jnp
import numpy as np
from jax import lax
from jax.experimental import pallas as pl
from jax.experimental.pallas import tpu as pltpu
from jax.sharding import PartitionSpec as P

LAGS = 256

cell_width = 0.0125
layer_thick = 0.0125
bin_hertz = 0.5
period_bins = 500
slow_base = 0.3
chunk = 16
tile = 256


def spectral_order(length):
    half = length // 2
    return np.concatenate([np.arange(half), [half], np.arange(length - 1, half, -1)])


def parts_of(length):
    steps = np.arange(length, dtype=np.int64)
    phases = np.mod(steps[:, None] * steps[None, :], length).astype(np.float32)
    angles = phases * np.float32(2.0 * math.pi / length)
    scale = np.float32(1.0 / math.sqrt(length))
    return np.cos(angles) * scale, np.sin(angles) * scale


def transform_block(length):
    cosine, sine = parts_of(length)
    return np.block([[cosine, -sine], [sine, cosine]]).astype(jnp.bfloat16)


def transform_pair(length):
    cosine, sine = parts_of(length)
    order = spectral_order(length)
    return (
        np.concatenate([cosine[order], sine[order]], axis=1).astype(jnp.bfloat16),
        np.concatenate([cosine[:, order], sine[:, order]], axis=1).astype(jnp.bfloat16),
    )


def sin_cos(angle):
    turns = jnp.floor(angle * (2.0 / math.pi) + 0.5)
    rest = angle - turns * 1.5707855224609375
    rest = rest - turns * 1.0804334124e-05
    quarter = turns.astype(jnp.int32)
    square = rest * rest
    sine = rest + rest * square * (
        -1.6666654611e-1 + square * (8.3321608736e-3 + square * -1.9515295891e-4)
    )
    cosine = (
        1.0
        - 0.5 * square
        + square * square
        * (4.166664568298827e-2 + square * (-1.388731625493765e-3 + square * 2.443315711809948e-5))
    )
    odd = (quarter & 1) == 1
    sine_out = jnp.where(odd, cosine, sine)
    cosine_out = jnp.where(odd, sine, cosine)
    sine_out = jnp.where((quarter & 2) == 2, -sine_out, sine_out)
    cosine_out = jnp.where(((quarter + 1) & 2) == 2, -cosine_out, cosine_out)
    return sine_out, cosine_out


def window_kernel(
    devices, bins, gaps, slab_map, corner, slab_in, source_in, table_y_in, receiver_in,
    table_f_in, table_i_in, bracket_in,
    received, weights,
    slab, source, table_y, receiver, table_f, table_i, bracket,
    half, spectrum, shifted_a, shifted_b, shifted_c, returned, refocused, fields, cross,
    wide, windows, pair, part, parts, total, slow, phase_rows,
    load_sems, pair_sems, scatter_sems, gather_sems, cross_sems,
):
    depths, rows_x, cols_y = bracket.shape
    slab_count, rows_all, cols_all = slab.shape
    chips = devices // 2
    me = lax.axis_index("freq")
    grp = lax.axis_index("grp")
    core = lax.rem(me, 2)
    chip = me // 2
    other = 1 - core
    share_rows = rows_x // devices
    signs = (1.0, -1.0)
    middle = rows_x // 2
    tiles = rows_x // tile
    group = max(share_rows, chunk)
    groups = tile // group
    shifted = (shifted_a, shifted_b, shifted_c)
    angular = bins[me].astype(jnp.float32) * (2.0 * math.pi * bin_hertz)
    references = []
    for d in range(depths):
        first = gaps[d, 0]
        second = first + gaps[d, 1]
        third = second + gaps[d, 2]
        references.append((slow_base + first, slow_base + second, slow_base + third))

    loads = [
        pltpu.make_async_copy(far, near, load_sems.at[place])
        for place, (far, near) in enumerate((
            (slab_in, slab), (source_in, source), (table_y_in, table_y), (receiver_in, receiver),
            (table_f_in, table_f), (bracket_in, bracket), (table_i_in, table_i),
        ))
    ]

    def lanes(which):
        return pl.ds(which * cols_y, cols_y)

    def remote(source_ref, target_ref, sems, place):
        return pltpu.make_async_remote_copy(
            src_ref=source_ref, dst_ref=target_ref, send_sem=sems[0], recv_sem=sems[1],
            device_id=(grp, place), device_id_type=pl.DeviceIdType.MESH,
        )

    def hop_to(hop):
        return lax.rem(chip + hop, chips)

    def swap_first(d):
        return remote(
            windows.at[d, other], pair.at[d], (pair_sems.at[d, 0], pair_sems.at[d, 1]),
            chip * 2 + other,
        )

    def scatter(d, hop):
        return remote(
            part.at[d, hop_to(hop)], parts.at[d, hop],
            (scatter_sems.at[d, 0, hop], scatter_sems.at[d, 1, hop]), hop_to(hop) * 2 + core,
        )

    def gather(d, hop):
        return remote(
            total.at[d], slow.at[d, core, chip],
            (gather_sems.at[d, 0, hop], gather_sems.at[d, 1, hop]), hop_to(hop) * 2 + core,
        )

    def swap_last(d):
        return remote(
            slow.at[d, core], slow.at[d, core], (pair_sems.at[d, 2], pair_sems.at[d, 3]),
            chip * 2 + other,
        )

    def send_cross(d, hop):
        to = lax.rem(me + hop, devices)
        return remote(
            cross.at[d, to], received.at[d, me],
            (cross_sems.at[d, 0, hop], cross_sems.at[d, 1, hop]), to,
        )

    def begin_scatter(d):
        swap_first(d).wait()
        part[d] = windows[d, core] + pair[d]

        @pl.loop(1, chips)
        def _(hop):
            scatter(d, hop).start()

    def begin_gather(d):
        @pl.loop(1, chips)
        def _(hop):
            scatter(d, hop).wait()

        summed = part[d, chip]
        for hop in range(1, chips):
            summed = summed + parts[d, hop]
        total[d] = summed
        slow[d, core, chip] = summed

        @pl.loop(1, chips)
        def _(hop):
            gather(d, hop).start()

    def begin_last(d):
        @pl.loop(1, chips)
        def _(hop):
            gather(d, hop).wait()

        swap_last(d).start()

    barrier = pltpu.get_barrier_semaphore()

    @pl.loop(1, devices)
    def _(hop):
        pl.semaphore_signal(
            barrier, inc=1, device_id=(grp, lax.rem(me + hop, devices)),
            device_id_type=pl.DeviceIdType.MESH,
        )

    for load in loads:
        load.start()

    def one_hot(sizes, offset):
        ahead = lax.broadcasted_iota(jnp.int32, sizes, 0) - lax.broadcasted_iota(
            jnp.int32, sizes, 1
        )
        return jnp.where(ahead == offset, 1.0, 0.0).astype(jnp.bfloat16)

    def cut_slab(which):
        pick = one_hot((cols_all, cols_y), corner[1])
        for start in range(0, rows_all, tile):
            size = min(tile, rows_all - start)
            wide[pl.ds(start, size), :] = jnp.dot(
                slab[which, pl.ds(start, size), :], pick, preferred_element_type=jnp.float32
            ).astype(jnp.bfloat16)

    def put_windows(steps):
        kept = []
        for d in steps:
            apart = jnp.abs(lax.div(slab_map[d], slab_count) - me)
            kept.append((1 - jnp.minimum(apart, 1)).astype(jnp.float32))
        size = max(share_rows, chunk)

        @pl.loop(0, rows_x // size)
        def _(number):
            start = number * size
            pick = one_hot((size, rows_all), -(corner[0] + start))
            values = jnp.dot(pick, wide[...], preferred_element_type=jnp.float32)
            for d, keep in zip(steps, kept):
                held = (values * keep).astype(jnp.bfloat16)
                for piece in range(size // share_rows):
                    block = start // share_rows + piece
                    windows[d, block // chips, lax.rem(block, chips)] = held[
                        piece * share_rows : (piece + 1) * share_rows
                    ]

    loads[0].wait()
    if slab_count == 1:
        cut_slab(0)
        put_windows(range(depths))
    else:
        for d in range(depths):
            cut_slab(lax.rem(slab_map[d], slab_count))
            put_windows((d,))
    pl.semaphore_wait(barrier, devices - 1)
    for d in range(depths):
        swap_first(d).start()

    columns = lax.broadcasted_iota(jnp.int32, (chunk, cols_y), 1)
    wave_y = jnp.where(columns < cols_y // 2, columns, cols_y - columns).astype(jnp.float32) * (
        2.0 * math.pi / (cols_y * cell_width)
    )
    squares_y = wave_y * wave_y

    def phases(d, ref, magnitude):
        wave_x = magnitude.astype(jnp.float32) * (2.0 * math.pi / (rows_x * cell_width))
        reach = angular * references[d][ref]
        radicand = reach * reach - (wave_x * wave_x + squares_y)
        depth = jnp.sqrt(jnp.abs(radicand)) * layer_thick
        moving = radicand > 0.0
        fading = jnp.exp(jnp.where(moving, 0.0, -depth))
        sine, cosine = sin_cos(jnp.where(moving, depth, 0.0) - reach * layer_thick)
        return fading * cosine, fading * sine

    def apply_phase(target, cosine, sine, start):
        rows = pl.ds(start, chunk)
        low_rows = pl.ds(rows_x + start, chunk)
        for which in range(2):
            turned = signs[which] * sine
            real = spectrum[rows, lanes(which)]
            imag = spectrum[low_rows, lanes(which)]
            new_real = (cosine * real - turned * imag).astype(jnp.bfloat16)
            target[rows, lanes(which)] = new_real
            target[low_rows, lanes(which)] = (-(cosine * imag + turned * real)).astype(jnp.bfloat16)
            target[pl.ds(2 * rows_x + start, chunk), lanes(which)] = -new_real

    counted = lax.broadcasted_iota(jnp.int32, (chunk, cols_y), 0)

    def shift_chunk(d, ref, target, start):
        cosine, sine = phases(d, ref, counted + start)
        apply_phase(target, cosine, sine, start)
        apply_phase(target, cosine, sine, pl.multiple_of(middle + start, chunk))

    def shift_edge(d, ref, target):
        cosine, sine = phases(d, ref, jnp.where(counted == 0, middle, counted))
        apply_phase(target, cosine, sine, middle)

    def multiply(table, values, rows):
        block = table[rows, :]
        real = jnp.dot(block, values[: 2 * rows_x, :], preferred_element_type=jnp.float32)
        imag = jnp.dot(block, values[rows_x:, :], preferred_element_type=jnp.float32)
        return real, imag

    def slow_rows(d, start):
        if share_rows >= chunk:
            block = start // share_rows
            inner = pl.multiple_of(lax.rem(start, share_rows), chunk)
            return slow[d, block // chips, lax.rem(block, chips), pl.ds(inner, chunk), :].astype(
                jnp.float32
            )
        pieces = []
        for piece in range(chunk // share_rows):
            block = start // share_rows + piece
            pieces.append(
                slow[d, block // chips, lax.rem(block, chips)].astype(jnp.float32)
            )
        return jnp.concatenate(pieces, axis=0)

    def store_cross(d, start, which, values):
        if share_rows >= chunk:
            inner = pl.multiple_of(lax.rem(start, share_rows), chunk)
            cross[d, start // share_rows, which, pl.ds(inner, chunk), :] = values.astype(
                jnp.bfloat16
            )
        else:
            for piece in range(chunk // share_rows):
                cross[d, start // share_rows + piece, which] = values[
                    piece * share_rows : (piece + 1) * share_rows
                ].astype(jnp.bfloat16)

    def mix(d, turn, inside, start):
        local = pl.ds(inside, chunk)
        rows = pl.ds(start, chunk)
        slowness = slow_rows(d, start)
        lower = bracket[d, rows, :] == 0
        slow_low = jnp.where(lower, references[d][0], references[d][1])
        slow_gap = jnp.where(
            lower, references[d][1] - references[d][0], references[d][2] - references[d][1]
        )
        weight = jnp.clip((slowness - slow_low) / slow_gap, 0.0, 1.0)
        sine, cosine = sin_cos((angular * layer_thick) * slowness)
        rounded = []
        for which in range(2):
            mixed = []
            for side in range(2):
                first = refocused[turn, 0, which, local, lanes(side)]
                second = refocused[turn, 1, which, local, lanes(side)]
                third = refocused[turn, 2, which, local, lanes(side)]
                low = jnp.where(lower, first, second)
                high = jnp.where(lower, second, third)
                mixed.append((1.0 - weight) * low + weight * high)
            turned = signs[which] * sine
            real = (cosine * mixed[0] + turned * mixed[1]).astype(jnp.bfloat16)
            imag = (turned * mixed[0] - cosine * mixed[1]).astype(jnp.bfloat16)
            if d < depths - 1:
                fields[which, 0, rows, :] = real
                fields[which, 1, rows, :] = imag
            rounded.append((real.astype(jnp.float32), imag.astype(jnp.float32)))
        (sr, si), (rr, ri) = rounded
        store_cross(d, start, 0, sr * rr + si * ri)
        store_cross(d, start, 1, sr * ri - si * rr)

    def forward_y(which, field):
        for start in range(0, rows_x, tile):
            rows = pl.ds(start, tile)
            both = jnp.concatenate([field[0, rows, :], field[1, rows, :]], axis=1)
            out = jnp.dot(both, table_y[...], preferred_element_type=jnp.float32)
            out = out.astype(jnp.bfloat16)
            half[rows, lanes(which)] = out[:, :cols_y]
            half[pl.ds(rows_x + start, tile), lanes(which)] = out[:, cols_y:]
            half[pl.ds(2 * rows_x + start, tile), lanes(which)] = -out[:, :cols_y]

    def forward_x():
        @pl.loop(0, rows_x // tile)
        def _(number):
            start = pl.multiple_of(number * tile, tile)
            real, imag = multiply(table_f, half, pl.ds(start, tile))
            spectrum[pl.ds(start, tile), :] = real
            spectrum[pl.ds(rows_x + start, tile), :] = imag

    def shift_first(d):
        @pl.loop(0, middle // chunk)
        def _(number):
            shift_chunk(d, 0, shifted[0], pl.multiple_of(number * chunk, chunk))

        shift_edge(d, 0, shifted[0])

    def inverse(d, turn, ref, tile_start):
        if turn == 0 and ref < 2:
            part_rows = tile // 2

            @pl.loop(0, 2)
            def _(side):
                inner = pl.multiple_of(side * part_rows, part_rows)
                real, imag = multiply(table_i, shifted[ref], pl.ds(tile_start + inner, part_rows))
                returned[pl.ds(inner, part_rows), :] = real.astype(jnp.bfloat16)
                returned[pl.ds(tile + inner, part_rows), :] = imag.astype(jnp.bfloat16)
                for each in range(middle // chunk // 2):
                    shift_chunk(
                        d, ref + 1, shifted[ref + 1],
                        pl.multiple_of(side * (middle // 2) + each * chunk, chunk),
                    )

            shift_edge(d, ref + 1, shifted[ref + 1])
        else:
            real, imag = multiply(table_i, shifted[ref], pl.ds(tile_start, tile))
            returned[:tile, :] = real.astype(jnp.bfloat16)
            returned[tile:, :] = imag.astype(jnp.bfloat16)
        for which in range(2):
            both = jnp.concatenate(
                [returned[:tile, lanes(which)], returned[tile:, lanes(which)]], axis=1
            )
            refocused[turn, ref, which] = jnp.dot(
                both, table_y[...], preferred_element_type=jnp.float32
            )

    def send_group(d, tile_start, index):
        for each in range(group // share_rows):
            to = (tile_start + index * group) // share_rows + each
            hop = lax.rem(to - me + devices, devices)

            @pl.when(hop != 0)
            def _():
                send_cross(d, hop).start()

    own_tile = me * share_rows // tile
    own_group = lax.rem(me * share_rows, tile) // group

    def turn_index(number):
        return lax.rem(own_group + 1 + number, groups)

    def mix_tile(d, turn, tile_start):
        @pl.loop(0, groups)
        def _(number):
            for each in range(group // chunk):
                inside = pl.multiple_of(turn_index(number) * group + each * chunk, chunk)
                mix(d, turn, inside, pl.multiple_of(tile_start + inside, chunk))

            @pl.when(number > 0)
            def _():
                send_group(d, tile_start, turn_index(number - 1))

        send_group(d, tile_start, turn_index(groups - 1))

    def lag_table():
        lag_count = weights.shape[1]
        offsets = (
            lax.broadcasted_iota(jnp.int32, (1, lag_count), 1) - lag_count // 2
        ).astype(jnp.float32)

        @pl.loop(0, devices)
        def _(slot):
            turned = bins[slot].astype(jnp.float32) * offsets
            phase_rows[pl.ds(2 * slot, 1), :] = turned
            phase_rows[pl.ds(2 * slot + 1, 1), :] = turned

        counts = phase_rows[...]
        wraps = jnp.floor((counts + 0.5) * (1.0 / period_bins))
        sine, cosine = sin_cos((counts - wraps * period_bins) * (2.0 * math.pi / period_bins))
        odd = lax.broadcasted_iota(jnp.int32, counts.shape, 0) % 2 == 1
        weights[...] = jnp.where(odd, -sine, cosine).astype(jnp.bfloat16)

    tile_starts = [
        pl.multiple_of(lax.rem(own_tile + 1 + turn, tiles) * tile, tile) for turn in range(tiles)
    ]
    for d in range(depths):
        if d == 0:
            loads[1].wait()
            loads[2].wait()
            forward_y(0, source)
            begin_scatter(0)
            loads[3].wait()
            forward_y(1, receiver)
            loads[4].wait()
            forward_x()
            shift_first(0)
            begin_gather(0)
            for later in range(1, depths):
                begin_scatter(later)
            loads[5].wait()
            loads[6].wait()
            for turn in range(tiles):
                for ref in range(3):
                    if turn == tiles - 1 and ref == 2:
                        begin_last(0)
                        for later in range(1, depths):
                            begin_gather(later)
                    inverse(0, turn, ref, tile_starts[turn])
            lag_table()
            swap_last(0).wait()
            for turn in range(tiles):
                mix_tile(0, turn, tile_starts[turn])
            for later in range(1, depths):
                begin_last(later)
        else:
            forward_y(0, fields.at[0])
            forward_y(1, fields.at[1])
            forward_x()
            shift_first(d)
            for turn in range(tiles):
                for ref in range(3):
                    inverse(d, turn, ref, tile_starts[turn])
                if turn == 0:
                    swap_last(d).wait()
                mix_tile(d, turn, tile_starts[turn])
        received[d, me] = cross[d, me]
    for d in range(depths):
        @pl.loop(1, devices)
        def _(hop):
            send_cross(d, hop).wait()


def cross_spectra(
    devices, bins, gaps, slab_map, corner, source, receiver, slabs, bracket
):
    depths, rows_x, cols_y = bracket.shape
    slab_count, rows_all, cols_all = slabs.shape
    chips = devices // 2
    share_rows = rows_x // devices
    table_f, table_i = transform_pair(rows_x)
    table_y = transform_block(cols_y)
    vmem = pl.BlockSpec(memory_space=pltpu.VMEM)
    flops = 16 * rows_x * (2 * rows_x + 2 * cols_y) * 2 * cols_y * depths
    dma = pltpu.SemaphoreType.DMA
    held = (depths, chips, share_rows, cols_y)
    field = pltpu.VMEM((2, rows_x, cols_y), jnp.bfloat16)
    return pl.pallas_call(
        functools.partial(window_kernel, devices),
        out_shape=(
            jax.ShapeDtypeStruct((depths, devices, 2, share_rows, cols_y), jnp.bfloat16),
            jax.ShapeDtypeStruct((2 * devices, LAGS), jnp.bfloat16),
        ),
        in_specs=[pl.BlockSpec(memory_space=pltpu.SMEM)] * 4
        + [pl.BlockSpec(memory_space=pltpu.HBM)] * 7,
        out_specs=(vmem, vmem),
        scratch_shapes=[
            pltpu.VMEM(slabs.shape, jnp.bfloat16),
            field,
            pltpu.VMEM(table_y.shape, jnp.bfloat16),
            field,
            pltpu.VMEM(table_f.shape, jnp.bfloat16),
            pltpu.VMEM(table_i.shape, jnp.bfloat16),
            pltpu.VMEM(bracket.shape, jnp.int32),
            pltpu.VMEM((3 * rows_x, 2 * cols_y), jnp.bfloat16),
            pltpu.VMEM((2 * rows_x, 2 * cols_y), jnp.float32),
            pltpu.VMEM((3 * rows_x, 2 * cols_y), jnp.bfloat16),
            pltpu.VMEM((3 * rows_x, 2 * cols_y), jnp.bfloat16),
            pltpu.VMEM((3 * rows_x, 2 * cols_y), jnp.bfloat16),
            pltpu.VMEM((2 * tile, 2 * cols_y), jnp.bfloat16),
            pltpu.VMEM((rows_x // tile, 3, 2, tile, 2 * cols_y), jnp.float32),
            pltpu.VMEM((2, 2, rows_x, cols_y), jnp.bfloat16),
            pltpu.VMEM((depths, devices, 2, share_rows, cols_y), jnp.bfloat16),
            pltpu.VMEM((rows_all, cols_y), jnp.bfloat16),
            pltpu.VMEM((depths, 2, chips, share_rows, cols_y), jnp.bfloat16),
            pltpu.VMEM(held, jnp.bfloat16),
            pltpu.VMEM(held, jnp.bfloat16),
            pltpu.VMEM(held, jnp.bfloat16),
            pltpu.VMEM((depths, share_rows, cols_y), jnp.bfloat16),
            pltpu.VMEM((depths, 2, chips, share_rows, cols_y), jnp.bfloat16),
            pltpu.VMEM((2 * devices, LAGS), jnp.float32),
            dma((7,)),
            dma((depths, 4)),
            dma((depths, 2, chips)),
            dma((depths, 2, chips)),
            dma((depths, 2, devices)),
        ],
        cost_estimate=pl.CostEstimate(
            flops=4 * flops, bytes_accessed=8 * 1024 * 1024, transcendentals=0
        ),
        compiler_params=pltpu.CompilerParams(
            collective_id=0, has_side_effects=True, vmem_limit_bytes=44 * 1024 * 1024
        ),
    )(
        *[
            pltpu.with_memory_space_constraint(value, pltpu.HBM)
            for value in (
                bins, gaps, slab_map, corner, slabs, source, jnp.asarray(table_y), receiver,
                jnp.asarray(table_f), jnp.asarray(table_i), bracket,
            )
        ]
    )


def image_kernel(scale, crosses, weights, out):
    _, slots, _, _, cols_y = crosses.shape
    _, rows, _, _ = out.shape
    step = pl.multiple_of(pl.program_id(1) * rows, rows)
    values = crosses[pl.program_id(0), :, :, pl.ds(step, rows), :]
    values = values.astype(jnp.float32).reshape(2 * slots, rows, cols_y)
    values = jnp.swapaxes(values, 0, 1).astype(jnp.bfloat16)
    for row in range(rows):
        out[0, row] = scale * lax.dot_general(
            values[row], weights[...], (((0,), (0,)), ((), ())),
            preferred_element_type=jnp.float32,
        )


def lag_image(crosses, weights):
    depths, slots, _, rows, cols_y = crosses.shape
    lag_count = weights.shape[1]
    step = min(8, rows)
    whole = pl.BlockSpec(memory_space=pltpu.VMEM)
    return pl.pallas_call(
        functools.partial(image_kernel, slots ** (-0.5)),
        out_shape=jax.ShapeDtypeStruct((depths, rows, cols_y, lag_count), jnp.float32),
        grid=(depths, rows // step),
        in_specs=[whole, whole],
        out_specs=pl.BlockSpec((1, step, cols_y, lag_count), lambda d, r: (d, r, 0, 0)),
        compiler_params=pltpu.CompilerParams(vmem_limit_bytes=24 * 1024 * 1024),
    )(crosses, weights)


def shards(
    devices,
    source_field,
    receiver_field,
    slowness_slabs,
    slab_map,
    reference_gaps,
    reference_index,
    frequency_bins,
    shot_corner,
):
    crosses, weights = cross_spectra(
        devices, frequency_bins, reference_gaps, slab_map, shot_corner, source_field[:, 0],
        receiver_field[:, 0], slowness_slabs, reference_index,
    )
    return lag_image(crosses, weights)


def solution(mesh):
    placed = (
        P("grp", "freq", None, None),
        P("grp", "freq", None, None),
        P(("grp", "freq"), None, None),
        P("grp"),
        P("grp", None),
        P("grp", None, None),
        P(),
        P("grp"),
    )
    return jax.shard_map(
        functools.partial(shards, mesh.shape["freq"]),
        mesh=mesh,
        in_specs=placed,
        out_specs=P("grp", "freq", None, None),
        check_vma=False,
    )
```

```python
import functools
import math

import jax
import jax.numpy as jnp
import numpy as np
from jax import lax
from jax.experimental import pallas as pl
from jax.experimental.pallas import tpu as pltpu
from jax.sharding import PartitionSpec as P

LAGS = 256

cell_width = 0.0125
layer_thick = 0.0125
bin_hertz = 0.5
period_bins = 500
slow_base = 0.3
chunk = 16
tile = 256


def parts_of(length):
    steps = np.arange(length, dtype=np.int64)
    phases = np.mod(steps[:, None] * steps[None, :], length).astype(np.float32)
    angles = phases * np.float32(2.0 * math.pi / length)
    scale = np.float32(1.0 / math.sqrt(length))
    return np.cos(angles) * scale, np.sin(angles) * scale


def real_transform(length):
    cosine, sine = (part.astype(jnp.bfloat16) for part in parts_of(length))
    half = length // 2
    basis = np.concatenate([cosine[: half + 1], sine[1:half]], axis=0)
    twice = np.full((length, 1), 2.0, np.float32)
    twice[0] = twice[half] = 1.0
    return (basis.astype(np.float32) * twice).astype(jnp.bfloat16), basis.T


def sin_cos(angle):
    turns = jnp.floor(angle * (2.0 / math.pi) + 0.5)
    rest = angle - turns * 1.5707855224609375
    rest = rest - turns * 1.0804334124e-05
    quarter = turns.astype(jnp.int32)
    square = rest * rest
    sine = rest + rest * square * (
        -1.6666654611e-1 + square * (8.3321608736e-3 + square * -1.9515295891e-4)
    )
    cosine = (
        1.0
        - 0.5 * square
        + square * square
        * (4.166664568298827e-2 + square * (-1.388731625493765e-3 + square * 2.443315711809948e-5))
    )
    odd = (quarter & 1) == 1
    sine_out = jnp.where(odd, cosine, sine)
    cosine_out = jnp.where(odd, sine, cosine)
    sine_out = jnp.where((quarter & 2) == 2, -sine_out, sine_out)
    cosine_out = jnp.where(((quarter + 1) & 2) == 2, -cosine_out, cosine_out)
    return sine_out, cosine_out


def window_kernel(
    devices, bins, gaps, slab_map, corner, slab_in, source_in, table_y_in, receiver_in,
    table_f_in, table_i_in, bracket_in, table_z_in,
    received, weights,
    slab, source, table_y, receiver, table_f, table_i, bracket, table_z,
    half, spectrum, phases, shifted, returned, refocused, fields, cross,
    wide, windows, pair, part, parts, total, slow, phase_rows,
    load_sems, pair_sems, scatter_sems, gather_sems, cross_sems,
):
    depths, rows_x, cols_y = bracket.shape
    slab_count, rows_all, cols_all = slab.shape
    chips = devices // 2
    me = lax.axis_index("freq")
    grp = lax.axis_index("grp")
    core = lax.rem(me, 2)
    chip = me // 2
    other = 1 - core
    share_rows = rows_x // devices
    signs = (1.0, -1.0)
    middle = rows_x // 2
    tiles = rows_x // tile
    group = max(share_rows, chunk)
    groups = tile // group
    angular = bins[me].astype(jnp.float32) * (2.0 * math.pi * bin_hertz)
    references = []
    for d in range(depths):
        first = gaps[d, 0]
        second = first + gaps[d, 1]
        third = second + gaps[d, 2]
        references.append((slow_base + first, slow_base + second, slow_base + third))

    loads = [
        pltpu.make_async_copy(far, near, load_sems.at[place])
        for place, (far, near) in enumerate((
            (slab_in, slab), (source_in, source), (table_y_in, table_y), (receiver_in, receiver),
            (table_f_in, table_f), (bracket_in, bracket), (table_i_in, table_i), (table_z_in, table_z),
        ))
    ]

    def lanes(which, side):
        return pl.ds((2 * which + side) * cols_y, cols_y)

    def remote(source_ref, target_ref, sems, place):
        return pltpu.make_async_remote_copy(
            src_ref=source_ref, dst_ref=target_ref, send_sem=sems[0], recv_sem=sems[1],
            device_id=(grp, place), device_id_type=pl.DeviceIdType.MESH,
        )

    def hop_to(hop):
        return lax.rem(chip + hop, chips)

    def swap_first(d):
        return remote(
            windows.at[d, other], pair.at[d], (pair_sems.at[d, 0], pair_sems.at[d, 1]),
            chip * 2 + other,
        )

    def scatter(d, hop):
        return remote(
            part.at[d, hop_to(hop)], parts.at[d, hop],
            (scatter_sems.at[d, 0, hop], scatter_sems.at[d, 1, hop]), hop_to(hop) * 2 + core,
        )

    def gather(d, hop):
        return remote(
            total.at[d], slow.at[d, core, chip],
            (gather_sems.at[d, 0, hop], gather_sems.at[d, 1, hop]), hop_to(hop) * 2 + core,
        )

    def swap_last(d):
        return remote(
            slow.at[d, core], slow.at[d, core], (pair_sems.at[d, 2], pair_sems.at[d, 3]),
            chip * 2 + other,
        )

    def send_cross(d, hop):
        to = lax.rem(me + hop, devices)
        return remote(
            cross.at[d, to], received.at[d, me],
            (cross_sems.at[d, 0, hop], cross_sems.at[d, 1, hop]), to,
        )

    def begin_scatter(d):
        swap_first(d).wait()
        part[d] = windows[d, core] + pair[d]

        @pl.loop(1, chips)
        def _(hop):
            scatter(d, hop).start()

    def begin_gather(d):
        @pl.loop(1, chips)
        def _(hop):
            scatter(d, hop).wait()

        summed = part[d, chip]
        for hop in range(1, chips):
            summed = summed + parts[d, hop]
        total[d] = summed
        slow[d, core, chip] = summed

        @pl.loop(1, chips)
        def _(hop):
            gather(d, hop).start()

    def begin_last(d):
        @pl.loop(1, chips)
        def _(hop):
            gather(d, hop).wait()

        swap_last(d).start()

    barrier = pltpu.get_barrier_semaphore()

    @pl.loop(1, devices)
    def _(hop):
        pl.semaphore_signal(
            barrier, inc=1, device_id=(grp, lax.rem(me + hop, devices)),
            device_id_type=pl.DeviceIdType.MESH,
        )

    for load in loads:
        load.start()

    def one_hot(sizes, offset):
        ahead = lax.broadcasted_iota(jnp.int32, sizes, 0) - lax.broadcasted_iota(
            jnp.int32, sizes, 1
        )
        return jnp.where(ahead == offset, 1.0, 0.0).astype(jnp.bfloat16)

    def cut_slab(which):
        pick = one_hot((cols_all, cols_y), corner[1])
        for start in range(0, rows_all, tile):
            size = min(tile, rows_all - start)
            wide[pl.ds(start, size), :] = jnp.dot(
                slab[which, pl.ds(start, size), :], pick, preferred_element_type=jnp.float32
            ).astype(jnp.bfloat16)

    def put_windows(steps):
        kept = []
        for d in steps:
            apart = jnp.abs(lax.div(slab_map[d], slab_count) - me)
            kept.append((1 - jnp.minimum(apart, 1)).astype(jnp.float32))
        size = max(share_rows, chunk)

        @pl.loop(0, rows_x // size)
        def _(number):
            start = number * size
            pick = one_hot((size, rows_all), -(corner[0] + start))
            values = jnp.dot(pick, wide[...], preferred_element_type=jnp.float32)
            for d, keep in zip(steps, kept):
                held = (values * keep).astype(jnp.bfloat16)
                for piece in range(size // share_rows):
                    block = start // share_rows + piece
                    windows[d, block // chips, lax.rem(block, chips)] = held[
                        piece * share_rows : (piece + 1) * share_rows
                    ]

    loads[0].wait()
    if slab_count == 1:
        cut_slab(0)
        put_windows(range(depths))
    else:
        for d in range(depths):
            cut_slab(lax.rem(slab_map[d], slab_count))
            put_windows((d,))
    pl.semaphore_wait(barrier, devices - 1)
    for d in range(depths):
        swap_first(d).start()

    columns = lax.broadcasted_iota(jnp.int32, (chunk, cols_y), 1)
    wave_y = jnp.where(columns <= cols_y // 2, columns, columns - cols_y // 2).astype(
        jnp.float32
    ) * (2.0 * math.pi / (cols_y * cell_width))
    squares_y = wave_y * wave_y
    counted = lax.broadcasted_iota(jnp.int32, (chunk, cols_y), 0)

    def phase_chunk(d, ref, start, magnitude):
        wave_x = magnitude.astype(jnp.float32) * (2.0 * math.pi / (rows_x * cell_width))
        reach = angular * references[d][ref]
        radicand = reach * reach - (wave_x * wave_x + squares_y)
        depth = jnp.sqrt(jnp.abs(radicand)) * layer_thick
        moving = radicand > 0.0
        fading = jnp.exp(jnp.where(moving, 0.0, -depth))
        sine, cosine = sin_cos(jnp.where(moving, depth, 0.0) - reach * layer_thick)
        phases[d, ref, 0, pl.ds(start, chunk), :] = fading * cosine
        phases[d, ref, 1, pl.ds(start, chunk), :] = fading * sine

    def phase_table(d, ref):
        @pl.loop(0, middle // chunk)
        def _(number):
            start = pl.multiple_of(number * chunk, chunk)
            phase_chunk(d, ref, start, counted + start)

        phase_chunk(d, ref, middle, jnp.where(counted == 0, middle, counted))

    def apply_phase(d, ref, start, place):
        rows = pl.ds(start, chunk)
        cosine = phases[d, ref, 0, pl.ds(place, chunk), :]
        sine = phases[d, ref, 1, pl.ds(place, chunk), :]
        for which in range(2):
            turned = signs[which] * sine
            real = spectrum[rows, lanes(which, 0)]
            imag = spectrum[rows, lanes(which, 1)]
            shifted[ref, rows, lanes(which, 0)] = (cosine * real - turned * imag).astype(
                jnp.bfloat16
            )
            shifted[ref, rows, lanes(which, 1)] = (cosine * imag + turned * real).astype(
                jnp.bfloat16
            )

    def shift_chunk(d, ref, start):
        apply_phase(d, ref, start, start)
        apply_phase(d, ref, pl.multiple_of(middle + start, chunk), start)

    def shift_edge(d, ref):
        apply_phase(d, ref, 0, 0)
        apply_phase(d, ref, middle, middle)

    def shift(d, ref):
        @pl.loop(1, middle // chunk)
        def _(number):
            shift_chunk(d, ref, pl.multiple_of(number * chunk, chunk))

        shift_edge(d, ref)

    def slow_rows(d, start):
        if share_rows >= chunk:
            block = start // share_rows
            inner = pl.multiple_of(lax.rem(start, share_rows), chunk)
            return slow[d, block // chips, lax.rem(block, chips), pl.ds(inner, chunk), :].astype(
                jnp.float32
            )
        pieces = []
        for piece in range(chunk // share_rows):
            block = start // share_rows + piece
            pieces.append(
                slow[d, block // chips, lax.rem(block, chips)].astype(jnp.float32)
            )
        return jnp.concatenate(pieces, axis=0)

    def store_cross(d, start, which, values):
        if share_rows >= chunk:
            inner = pl.multiple_of(lax.rem(start, share_rows), chunk)
            cross[d, start // share_rows, which, pl.ds(inner, chunk), :] = values.astype(
                jnp.bfloat16
            )
        else:
            for piece in range(chunk // share_rows):
                cross[d, start // share_rows + piece, which] = values[
                    piece * share_rows : (piece + 1) * share_rows
                ].astype(jnp.bfloat16)

    def mix(d, turn, inside, start):
        local = pl.ds(inside, chunk)
        rows = pl.ds(start, chunk)
        slowness = slow_rows(d, start)
        lower = bracket[d, rows, :] == 0
        slow_low = jnp.where(lower, references[d][0], references[d][1])
        slow_gap = jnp.where(
            lower, references[d][1] - references[d][0], references[d][2] - references[d][1]
        )
        weight = jnp.clip((slowness - slow_low) / slow_gap, 0.0, 1.0)
        sine, cosine = sin_cos((angular * layer_thick) * slowness)
        rounded = []
        for which in range(2):
            mixed = []
            for side in range(2):
                first = refocused[turn, 0, local, lanes(which, side)]
                second = refocused[turn, 1, local, lanes(which, side)]
                third = refocused[turn, 2, local, lanes(which, side)]
                low = jnp.where(lower, first, second)
                high = jnp.where(lower, second, third)
                mixed.append((1.0 - weight) * low + weight * high)
            turned = signs[which] * sine
            real = (cosine * mixed[0] - turned * mixed[1]).astype(jnp.bfloat16)
            imag = (turned * mixed[0] + cosine * mixed[1]).astype(jnp.bfloat16)
            if d < depths - 1:
                fields[which, 0, rows, :] = real
                fields[which, 1, rows, :] = imag
            rounded.append((real.astype(jnp.float32), imag.astype(jnp.float32)))
        (sr, si), (rr, ri) = rounded
        store_cross(d, start, 0, sr * rr + si * ri)
        store_cross(d, start, 1, sr * ri - si * rr)

    def forward_y(which, field):
        for side in range(2):
            for start in range(0, rows_x, tile):
                rows = pl.ds(start, tile)
                half[rows, lanes(which, side)] = jnp.dot(
                    field[side, rows, :], table_y[...], preferred_element_type=jnp.float32
                ).astype(jnp.bfloat16)

    def forward_x():
        @pl.loop(0, rows_x // tile)
        def _(number):
            rows = pl.ds(pl.multiple_of(number * tile, tile), tile)
            spectrum[rows, :] = jnp.dot(
                table_f[rows, :], half[...], preferred_element_type=jnp.float32
            )

    def inverse(turn, ref, tile_start):
        returned[...] = jnp.dot(
            table_i[pl.ds(tile_start, tile), :], shifted[ref], preferred_element_type=jnp.float32
        ).astype(jnp.bfloat16)
        for which in range(2):
            for side in range(2):
                refocused[turn, ref, :, lanes(which, side)] = jnp.dot(
                    returned[:, lanes(which, side)], table_z[...],
                    preferred_element_type=jnp.float32,
                )

    def send_group(d, tile_start, index):
        for each in range(group // share_rows):
            to = (tile_start + index * group) // share_rows + each
            hop = lax.rem(to - me + devices, devices)

            @pl.when(hop != 0)
            def _():
                send_cross(d, hop).start()

    own_tile = me * share_rows // tile
    own_group = lax.rem(me * share_rows, tile) // group

    def turn_index(number):
        return lax.rem(own_group + 1 + number, groups)

    def mix_tile(d, turn, tile_start):
        @pl.loop(0, groups)
        def _(number):
            for each in range(group // chunk):
                inside = pl.multiple_of(turn_index(number) * group + each * chunk, chunk)
                mix(d, turn, inside, pl.multiple_of(tile_start + inside, chunk))

            @pl.when(number > 0)
            def _():
                send_group(d, tile_start, turn_index(number - 1))

        send_group(d, tile_start, turn_index(groups - 1))

    def lag_table():
        lag_count = weights.shape[1]
        offsets = (
            lax.broadcasted_iota(jnp.int32, (1, lag_count), 1) - lag_count // 2
        ).astype(jnp.float32)

        @pl.loop(0, devices)
        def _(slot):
            turned = bins[slot].astype(jnp.float32) * offsets
            phase_rows[pl.ds(2 * slot, 1), :] = turned
            phase_rows[pl.ds(2 * slot + 1, 1), :] = turned

        counts = phase_rows[...]
        wraps = jnp.floor((counts + 0.5) * (1.0 / period_bins))
        sine, cosine = sin_cos((counts - wraps * period_bins) * (2.0 * math.pi / period_bins))
        odd = lax.broadcasted_iota(jnp.int32, counts.shape, 0) % 2 == 1
        weights[...] = jnp.where(odd, -sine, cosine).astype(jnp.bfloat16)

    tile_starts = [
        pl.multiple_of(lax.rem(own_tile + 1 + turn, tiles) * tile, tile) for turn in range(tiles)
    ]
    for d in range(depths):
        if d == 0:
            loads[1].wait()
            loads[2].wait()
            forward_y(0, source)
            loads[3].wait()
            forward_y(1, receiver)
            begin_scatter(0)
            loads[4].wait()
            forward_x()
            for ref in range(3):
                phase_table(0, ref)
                shift(0, ref)
            begin_gather(0)
            for later in range(1, depths):
                begin_scatter(later)
            loads[5].wait()
            loads[6].wait()
            loads[7].wait()
            for turn in range(tiles):
                for ref in range(3):
                    inverse(turn, ref, tile_starts[turn])
            for later in range(1, depths):
                for ref in range(3):
                    phase_table(later, ref)
            begin_last(0)
            for later in range(1, depths):
                begin_gather(later)
            lag_table()
            swap_last(0).wait()
            for turn in range(tiles):
                mix_tile(0, turn, tile_starts[turn])
            for later in range(1, depths):
                begin_last(later)
        else:
            forward_y(0, fields.at[0])
            forward_y(1, fields.at[1])
            forward_x()
            for ref in range(3):
                shift(d, ref)
            for turn in range(tiles):
                for ref in range(3):
                    inverse(turn, ref, tile_starts[turn])
                if turn == 0:
                    swap_last(d).wait()
                mix_tile(d, turn, tile_starts[turn])
        received[d, me] = cross[d, me]
    for d in range(depths):
        @pl.loop(1, devices)
        def _(hop):
            send_cross(d, hop).wait()


def cross_spectra(
    devices, bins, gaps, slab_map, corner, source, receiver, slabs, bracket
):
    depths, rows_x, cols_y = bracket.shape
    slab_count, rows_all, cols_all = slabs.shape
    chips = devices // 2
    share_rows = rows_x // devices
    table_f, table_i = real_transform(rows_x)
    table_y, table_z = (table.T for table in real_transform(cols_y))
    vmem = pl.BlockSpec(memory_space=pltpu.VMEM)
    flops = 8 * rows_x * (rows_x + cols_y) * 4 * cols_y * depths
    dma = pltpu.SemaphoreType.DMA
    held = (depths, chips, share_rows, cols_y)
    field = pltpu.VMEM((2, rows_x, cols_y), jnp.bfloat16)
    return pl.pallas_call(
        functools.partial(window_kernel, devices),
        out_shape=(
            jax.ShapeDtypeStruct((depths, devices, 2, share_rows, cols_y), jnp.bfloat16),
            jax.ShapeDtypeStruct((2 * devices, LAGS), jnp.bfloat16),
        ),
        in_specs=[pl.BlockSpec(memory_space=pltpu.SMEM)] * 4
        + [pl.BlockSpec(memory_space=pltpu.HBM)] * 8,
        out_specs=(vmem, vmem),
        scratch_shapes=[
            pltpu.VMEM(slabs.shape, jnp.bfloat16),
            field,
            pltpu.VMEM(table_y.shape, jnp.bfloat16),
            field,
            pltpu.VMEM(table_f.shape, jnp.bfloat16),
            pltpu.VMEM(table_i.shape, jnp.bfloat16),
            pltpu.VMEM(bracket.shape, jnp.int32),
            pltpu.VMEM(table_z.shape, jnp.bfloat16),
            pltpu.VMEM((rows_x, 4 * cols_y), jnp.bfloat16),
            pltpu.VMEM((rows_x, 4 * cols_y), jnp.float32),
            pltpu.VMEM((depths, 3, 2, rows_x // 2 + chunk, cols_y), jnp.float32),
            pltpu.VMEM((3, rows_x, 4 * cols_y), jnp.bfloat16),
            pltpu.VMEM((tile, 4 * cols_y), jnp.bfloat16),
            pltpu.VMEM((rows_x // tile, 3, tile, 4 * cols_y), jnp.float32),
            pltpu.VMEM((2, 2, rows_x, cols_y), jnp.bfloat16),
            pltpu.VMEM((depths, devices, 2, share_rows, cols_y), jnp.bfloat16),
            pltpu.VMEM((rows_all, cols_y), jnp.bfloat16),
            pltpu.VMEM((depths, 2, chips, share_rows, cols_y), jnp.bfloat16),
            pltpu.VMEM(held, jnp.bfloat16),
            pltpu.VMEM(held, jnp.bfloat16),
            pltpu.VMEM(held, jnp.bfloat16),
            pltpu.VMEM((depths, share_rows, cols_y), jnp.bfloat16),
            pltpu.VMEM((depths, 2, chips, share_rows, cols_y), jnp.bfloat16),
            pltpu.VMEM((2 * devices, LAGS), jnp.float32),
            dma((8,)),
            dma((depths, 4)),
            dma((depths, 2, chips)),
            dma((depths, 2, chips)),
            dma((depths, 2, devices)),
        ],
        cost_estimate=pl.CostEstimate(
            flops=flops, bytes_accessed=8 * 1024 * 1024, transcendentals=0
        ),
        compiler_params=pltpu.CompilerParams(
            collective_id=0, has_side_effects=True, vmem_limit_bytes=44 * 1024 * 1024
        ),
    )(
        *[
            pltpu.with_memory_space_constraint(value, pltpu.HBM)
            for value in (
                bins, gaps, slab_map, corner, slabs, source, jnp.asarray(table_y), receiver,
                jnp.asarray(table_f), jnp.asarray(table_i), bracket, jnp.asarray(table_z),
            )
        ]
    )


def image_kernel(scale, crosses, weights, out):
    _, slots, _, _, cols_y = crosses.shape
    _, rows, _, _ = out.shape
    step = pl.multiple_of(pl.program_id(1) * rows, rows)
    values = crosses[pl.program_id(0), :, :, pl.ds(step, rows), :]
    values = values.astype(jnp.float32).reshape(2 * slots, rows, cols_y)
    values = jnp.swapaxes(values, 0, 1).astype(jnp.bfloat16)
    for row in range(rows):
        out[0, row] = scale * lax.dot_general(
            values[row], weights[...], (((0,), (0,)), ((), ())),
            preferred_element_type=jnp.float32,
        )


def lag_image(crosses, weights):
    depths, slots, _, rows, cols_y = crosses.shape
    lag_count = weights.shape[1]
    step = min(8, rows)
    whole = pl.BlockSpec(memory_space=pltpu.VMEM)
    return pl.pallas_call(
        functools.partial(image_kernel, slots ** (-0.5)),
        out_shape=jax.ShapeDtypeStruct((depths, rows, cols_y, lag_count), jnp.float32),
        grid=(depths, rows // step),
        in_specs=[whole, whole],
        out_specs=pl.BlockSpec((1, step, cols_y, lag_count), lambda d, r: (d, r, 0, 0)),
        compiler_params=pltpu.CompilerParams(vmem_limit_bytes=24 * 1024 * 1024),
    )(crosses, weights)


def shards(
    devices,
    source_field,
    receiver_field,
    slowness_slabs,
    slab_map,
    reference_gaps,
    reference_index,
    frequency_bins,
    shot_corner,
):
    crosses, weights = cross_spectra(
        devices, frequency_bins, reference_gaps, slab_map, shot_corner, source_field[:, 0],
        receiver_field[:, 0], slowness_slabs, reference_index,
    )
    return lag_image(crosses, weights)


def solution(mesh):
    placed = (
        P("grp", "freq", None, None),
        P("grp", "freq", None, None),
        P(("grp", "freq"), None, None),
        P("grp"),
        P("grp", None),
        P("grp", None, None),
        P(),
        P("grp"),
    )
    return jax.shard_map(
        functools.partial(shards, mesh.shape["freq"]),
        mesh=mesh,
        in_specs=placed,
        out_specs=P("grp", "freq", None, None),
        check_vma=False,
    )
```

```python
import functools
import math

import jax
import jax.numpy as jnp
import numpy as np
from jax import lax
from jax.experimental import pallas as pl
from jax.experimental.pallas import tpu as pltpu
from jax.sharding import PartitionSpec as P

LAGS = 256

cell_width = 0.0125
layer_thick = 0.0125
bin_hertz = 0.5
period_bins = 500
slow_base = 0.3
chunk = 16
tile = 256


def parts_of(length):
    steps = np.arange(length, dtype=np.int64)
    phases = np.mod(steps[:, None] * steps[None, :], length).astype(np.float32)
    angles = phases * np.float32(2.0 * math.pi / length)
    scale = np.float32(1.0 / math.sqrt(length))
    return np.cos(angles) * scale, np.sin(angles) * scale


def real_transform(length):
    cosine, sine = (part.astype(jnp.bfloat16) for part in parts_of(length))
    half = length // 2
    basis = np.concatenate([cosine[: half + 1], sine[1:half]], axis=0)
    twice = np.full((length, 1), 2.0, np.float32)
    twice[0] = twice[half] = 1.0
    return (basis.astype(np.float32) * twice).astype(jnp.bfloat16), basis.T


def sin_cos(angle):
    turns = jnp.floor(angle * (2.0 / math.pi) + 0.5)
    rest = angle - turns * 1.5707855224609375
    rest = rest - turns * 1.0804334124e-05
    quarter = turns.astype(jnp.int32)
    square = rest * rest
    sine = rest + rest * square * (
        -1.6666654611e-1 + square * (8.3321608736e-3 + square * -1.9515295891e-4)
    )
    cosine = (
        1.0
        - 0.5 * square
        + square * square
        * (4.166664568298827e-2 + square * (-1.388731625493765e-3 + square * 2.443315711809948e-5))
    )
    odd = (quarter & 1) == 1
    sine_out = jnp.where(odd, cosine, sine)
    cosine_out = jnp.where(odd, sine, cosine)
    sine_out = jnp.where((quarter & 2) == 2, -sine_out, sine_out)
    cosine_out = jnp.where(((quarter + 1) & 2) == 2, -cosine_out, cosine_out)
    return sine_out, cosine_out


def window_kernel(
    devices, bins, gaps, slab_map, corner, slab_in, source_in, table_y_in, receiver_in,
    table_f_in, table_i_in, bracket_in, table_z_in,
    received, weights,
    slab, source, table_y, receiver, table_f, table_i, bracket, table_z,
    half, spectrum, phases, shifted, returned, refocused, fields, cross,
    wide, windows, pair, part, parts, total, slow, phase_rows,
    load_sems, pair_sems, scatter_sems, gather_sems, trade_sems, cross_sems,
):
    depths, rows_x, cols_y = bracket.shape
    slab_count, rows_all, cols_all = slab.shape
    chips = devices // 2
    me = lax.axis_index("freq")
    grp = lax.axis_index("grp")
    core = lax.rem(me, 2)
    chip = me // 2
    other = 1 - core
    share_rows = rows_x // devices
    signs = (1.0, -1.0)
    middle = rows_x // 2
    tiles = rows_x // tile
    group = max(share_rows, chunk)
    groups = tile // group
    angular = bins[me].astype(jnp.float32) * (2.0 * math.pi * bin_hertz)
    references = []
    for d in range(depths):
        first = gaps[d, 0]
        second = first + gaps[d, 1]
        third = second + gaps[d, 2]
        references.append((slow_base + first, slow_base + second, slow_base + third))

    loads = [
        pltpu.make_async_copy(far, near, load_sems.at[place])
        for place, (far, near) in enumerate((
            (slab_in, slab), (source_in, source), (table_y_in, table_y), (receiver_in, receiver),
            (table_f_in, table_f), (bracket_in, bracket), (table_i_in, table_i), (table_z_in, table_z),
        ))
    ]

    def lanes(which, side):
        return pl.ds((2 * which + side) * cols_y, cols_y)

    def remote(source_ref, target_ref, sems, place):
        return pltpu.make_async_remote_copy(
            src_ref=source_ref, dst_ref=target_ref, send_sem=sems[0], recv_sem=sems[1],
            device_id=(grp, place), device_id_type=pl.DeviceIdType.MESH,
        )

    def hop_to(hop):
        return lax.rem(chip + hop, chips)

    def swap_first(d):
        return remote(
            windows.at[d, other], pair.at[d], (pair_sems.at[d, 0], pair_sems.at[d, 1]),
            chip * 2 + other,
        )

    def scatter(d, hop):
        return remote(
            part.at[d, hop_to(hop)], parts.at[d, hop],
            (scatter_sems.at[d, 0, hop], scatter_sems.at[d, 1, hop]), hop_to(hop) * 2 + core,
        )

    def gather(d, hop):
        return remote(
            total.at[d], slow.at[d, core, chip],
            (gather_sems.at[d, 0, hop], gather_sems.at[d, 1, hop]), hop_to(hop) * 2 + core,
        )

    def swap_last(d):
        return remote(
            slow.at[d, core], slow.at[d, core], (pair_sems.at[d, 2], pair_sems.at[d, 3]),
            chip * 2 + other,
        )

    def send_cross(d, hop):
        to = lax.rem(me + hop, devices)
        return remote(
            cross.at[d, to], received.at[d, me],
            (cross_sems.at[d, 0, hop], cross_sems.at[d, 1, hop]), to,
        )

    levels = chips.bit_length() - 1

    def bit_of(level):
        return lax.rem(chip // 2**level, 2)

    def lowest(level):
        return sum((bit_of(below) * (chips >> (below + 1)) for below in range(level)), 0 * chip)

    def trade(d, step, source_ref, target_ref):
        level = step if step < levels else 2 * levels - 2 - step
        place = chip + (1 - 2 * bit_of(level)) * 2**level
        return remote(
            source_ref, target_ref, (trade_sems.at[d, 0, step], trade_sems.at[d, 1, step]),
            place * 2 + core,
        )

    def halve(d, level):
        size = chips >> (level + 1)
        sent = lowest(level) + (1 - bit_of(level)) * size
        return trade(
            d, level, part.at[d, pl.ds(sent, size)],
            parts.at[d, pl.ds(chips - (chips >> level), size)],
        )

    def add_half(d, level):
        size = chips >> (level + 1)
        kept = pl.ds(lowest(level + 1), size)
        part[d, kept] = part[d, kept] + parts[d, pl.ds(chips - (chips >> level), size)]

    def exchange(d):
        kept = pl.ds(lowest(levels - 1), 2)
        return trade(d, levels - 1, part.at[d, kept], parts.at[d, pl.ds(chips - 2, 2)])

    def double(d, level):
        ready = pl.ds(lowest(level + 1), chips >> (level + 1))
        return trade(
            d, 2 * levels - 2 - level, slow.at[d, core, ready], slow.at[d, core, ready]
        )

    def relay(d):
        swap_first(d).wait()
        part[d] = windows[d, core] + pair[d]
        for level in range(levels - 1):
            halve(d, level).start()
            yield
            halve(d, level).wait()
            add_half(d, level)
        exchange(d).start()
        yield
        exchange(d).wait()
        kept = pl.ds(lowest(levels - 1), 2)
        slow[d, core, kept] = part[d, kept] + parts[d, pl.ds(chips - 2, 2)]
        for level in reversed(range(levels - 1)):
            double(d, level).start()
            yield
            double(d, level).wait()
        swap_last(d).start()

    relays = [relay(d) for d in range(1, depths)]

    def advance():
        for each in relays:
            next(each, None)

    def begin_scatter(d):
        swap_first(d).wait()
        part[d] = windows[d, core] + pair[d]

        @pl.loop(1, chips)
        def _(hop):
            scatter(d, hop).start()

    def begin_gather(d):
        @pl.loop(1, chips)
        def _(hop):
            scatter(d, hop).wait()

        summed = part[d, chip]
        for hop in range(1, chips):
            summed = summed + parts[d, hop]
        total[d] = summed
        slow[d, core, chip] = summed

        @pl.loop(1, chips)
        def _(hop):
            gather(d, hop).start()

    def begin_last(d):
        @pl.loop(1, chips)
        def _(hop):
            gather(d, hop).wait()

        swap_last(d).start()

    barrier = pltpu.get_barrier_semaphore()

    @pl.loop(1, devices)
    def _(hop):
        pl.semaphore_signal(
            barrier, inc=1, device_id=(grp, lax.rem(me + hop, devices)),
            device_id_type=pl.DeviceIdType.MESH,
        )

    loads[0].start()

    def one_hot(sizes, offset):
        ahead = lax.broadcasted_iota(jnp.int32, sizes, 0) - lax.broadcasted_iota(
            jnp.int32, sizes, 1
        )
        return jnp.where(ahead == offset, 1.0, 0.0).astype(jnp.bfloat16)

    def cut_slab(which):
        pick = one_hot((cols_all, cols_y), corner[1])
        for start in range(0, rows_all, tile):
            size = min(tile, rows_all - start)
            wide[pl.ds(start, size), :] = jnp.dot(
                slab[which, pl.ds(start, size), :], pick, preferred_element_type=jnp.float32
            ).astype(jnp.bfloat16)

    def put_windows(steps):
        kept = []
        for d in steps:
            apart = jnp.abs(lax.div(slab_map[d], slab_count) - me)
            kept.append((1 - jnp.minimum(apart, 1)).astype(jnp.float32))
        reach = tile + rows_all - rows_x
        pick = one_hot((tile, reach), -corner[0])
        for start in range(0, rows_x, tile):
            values = jnp.dot(
                pick, wide[pl.ds(start, reach), :], preferred_element_type=jnp.float32
            )
            for d, keep in zip(steps, kept):
                held = (values * keep).astype(jnp.bfloat16)
                for piece in range(tile // share_rows):
                    block = start // share_rows + piece
                    windows[d, block // chips, block % chips] = held[
                        piece * share_rows : (piece + 1) * share_rows
                    ]

    loads[0].wait()
    for load in loads[1:]:
        load.start()
    if slab_count == 1:
        cut_slab(0)
        put_windows(range(depths))
    else:
        for d in range(depths):
            cut_slab(lax.rem(slab_map[d], slab_count))
            put_windows((d,))
    pl.semaphore_wait(barrier, devices - 1)
    for d in range(depths):
        swap_first(d).start()

    columns = lax.broadcasted_iota(jnp.int32, (chunk, cols_y), 1)
    wave_y = jnp.where(columns <= cols_y // 2, columns, columns - cols_y // 2).astype(
        jnp.float32
    ) * (2.0 * math.pi / (cols_y * cell_width))
    squares_y = wave_y * wave_y
    counted = lax.broadcasted_iota(jnp.int32, (chunk, cols_y), 0)

    def phase_chunk(d, ref, start, magnitude):
        wave_x = magnitude.astype(jnp.float32) * (2.0 * math.pi / (rows_x * cell_width))
        reach = angular * references[d][ref]
        radicand = reach * reach - (wave_x * wave_x + squares_y)
        depth = jnp.sqrt(jnp.abs(radicand)) * layer_thick
        moving = radicand > 0.0
        fading = jnp.exp(jnp.where(moving, 0.0, -depth))
        sine, cosine = sin_cos(jnp.where(moving, depth, 0.0) - reach * layer_thick)
        phases[d, ref, 0, pl.ds(start, chunk), :] = fading * cosine
        phases[d, ref, 1, pl.ds(start, chunk), :] = fading * sine

    def phase_table(d, ref):
        @pl.loop(0, middle // chunk)
        def _(number):
            start = pl.multiple_of(number * chunk, chunk)
            phase_chunk(d, ref, start, counted + start)

        phase_chunk(d, ref, middle, jnp.where(counted == 0, middle, counted))

    def apply_phase(d, ref, start, place):
        rows = pl.ds(start, chunk)
        cosine = phases[d, ref, 0, pl.ds(place, chunk), :]
        sine = phases[d, ref, 1, pl.ds(place, chunk), :]
        for which in range(2):
            turned = signs[which] * sine
            real = spectrum[rows, lanes(which, 0)]
            imag = spectrum[rows, lanes(which, 1)]
            shifted[ref, rows, lanes(which, 0)] = (cosine * real - turned * imag).astype(
                jnp.bfloat16
            )
            shifted[ref, rows, lanes(which, 1)] = (cosine * imag + turned * real).astype(
                jnp.bfloat16
            )

    def shift_chunk(d, ref, start):
        apply_phase(d, ref, start, start)
        apply_phase(d, ref, pl.multiple_of(middle + start, chunk), start)

    def shift_edge(d, ref):
        apply_phase(d, ref, 0, 0)
        apply_phase(d, ref, middle, middle)

    def shift(d, ref):
        @pl.loop(1, middle // chunk)
        def _(number):
            shift_chunk(d, ref, pl.multiple_of(number * chunk, chunk))

        shift_edge(d, ref)

    def slow_rows(d, start):
        if share_rows >= chunk:
            block = start // share_rows
            inner = pl.multiple_of(lax.rem(start, share_rows), chunk)
            return slow[d, block // chips, lax.rem(block, chips), pl.ds(inner, chunk), :].astype(
                jnp.float32
            )
        pieces = []
        for piece in range(chunk // share_rows):
            block = start // share_rows + piece
            pieces.append(
                slow[d, block // chips, lax.rem(block, chips)].astype(jnp.float32)
            )
        return jnp.concatenate(pieces, axis=0)

    def store_cross(d, start, which, values):
        if share_rows >= chunk:
            inner = pl.multiple_of(lax.rem(start, share_rows), chunk)
            cross[d, start // share_rows, which, pl.ds(inner, chunk), :] = values.astype(
                jnp.bfloat16
            )
        else:
            for piece in range(chunk // share_rows):
                cross[d, start // share_rows + piece, which] = values[
                    piece * share_rows : (piece + 1) * share_rows
                ].astype(jnp.bfloat16)

    def mix(d, turn, inside, start):
        local = pl.ds(inside, chunk)
        rows = pl.ds(start, chunk)
        slowness = slow_rows(d, start)
        lower = bracket[d, rows, :] == 0
        slow_low = jnp.where(lower, references[d][0], references[d][1])
        slow_gap = jnp.where(
            lower, references[d][1] - references[d][0], references[d][2] - references[d][1]
        )
        weight = jnp.clip((slowness - slow_low) / slow_gap, 0.0, 1.0)
        sine, cosine = sin_cos((angular * layer_thick) * slowness)
        rounded = []
        for which in range(2):
            mixed = []
            for side in range(2):
                first = refocused[turn, 0, local, lanes(which, side)]
                second = refocused[turn, 1, local, lanes(which, side)]
                third = refocused[turn, 2, local, lanes(which, side)]
                low = jnp.where(lower, first, second)
                high = jnp.where(lower, second, third)
                mixed.append((1.0 - weight) * low + weight * high)
            turned = signs[which] * sine
            real = (cosine * mixed[0] - turned * mixed[1]).astype(jnp.bfloat16)
            imag = (turned * mixed[0] + cosine * mixed[1]).astype(jnp.bfloat16)
            if d < depths - 1:
                fields[which, 0, rows, :] = real
                fields[which, 1, rows, :] = imag
            rounded.append((real.astype(jnp.float32), imag.astype(jnp.float32)))
        (sr, si), (rr, ri) = rounded
        store_cross(d, start, 0, sr * rr + si * ri)
        store_cross(d, start, 1, sr * ri - si * rr)

    def forward_y(which, field):
        for side in range(2):
            for start in range(0, rows_x, tile):
                rows = pl.ds(start, tile)
                half[rows, lanes(which, side)] = jnp.dot(
                    field[side, rows, :], table_y[...], preferred_element_type=jnp.float32
                ).astype(jnp.bfloat16)

    def forward_x():
        @pl.loop(0, rows_x // tile)
        def _(number):
            rows = pl.ds(pl.multiple_of(number * tile, tile), tile)
            spectrum[rows, :] = jnp.dot(
                table_f[rows, :], half[...], preferred_element_type=jnp.float32
            )

    def inverse(turn, ref, tile_start):
        returned[...] = jnp.dot(
            table_i[pl.ds(tile_start, tile), :], shifted[ref], preferred_element_type=jnp.float32
        ).astype(jnp.bfloat16)
        for which in range(2):
            for side in range(2):
                refocused[turn, ref, :, lanes(which, side)] = jnp.dot(
                    returned[:, lanes(which, side)], table_z[...],
                    preferred_element_type=jnp.float32,
                )

    def send_group(d, tile_start, index):
        for each in range(group // share_rows):
            to = (tile_start + index * group) // share_rows + each
            hop = lax.rem(to - me + devices, devices)

            @pl.when(hop != 0)
            def _():
                send_cross(d, hop).start()

    own_tile = me * share_rows // tile
    own_group = lax.rem(me * share_rows, tile) // group

    def turn_index(number):
        return lax.rem(own_group + 1 + number, groups)

    def mix_tile(d, turn, tile_start):
        @pl.loop(0, groups)
        def _(number):
            for each in range(group // chunk):
                inside = pl.multiple_of(turn_index(number) * group + each * chunk, chunk)
                mix(d, turn, inside, pl.multiple_of(tile_start + inside, chunk))

            @pl.when(number > 0)
            def _():
                send_group(d, tile_start, turn_index(number - 1))

        send_group(d, tile_start, turn_index(groups - 1))

    def lag_table():
        lag_count = weights.shape[1]
        offsets = (
            lax.broadcasted_iota(jnp.int32, (1, lag_count), 1) - lag_count // 2
        ).astype(jnp.float32)

        @pl.loop(0, devices)
        def _(slot):
            turned = bins[slot].astype(jnp.float32) * offsets
            phase_rows[pl.ds(2 * slot, 1), :] = turned
            phase_rows[pl.ds(2 * slot + 1, 1), :] = turned

        counts = phase_rows[...]
        wraps = jnp.floor((counts + 0.5) * (1.0 / period_bins))
        sine, cosine = sin_cos((counts - wraps * period_bins) * (2.0 * math.pi / period_bins))
        odd = lax.broadcasted_iota(jnp.int32, counts.shape, 0) % 2 == 1
        weights[...] = jnp.where(odd, -sine, cosine).astype(jnp.bfloat16)

    first_tiles = (core * (tiles // 2),) + (own_tile + 1,) * (depths - 1)
    for d in range(depths):
        tile_starts = [
            pl.multiple_of(lax.rem(first_tiles[d] + turn, tiles) * tile, tile)
            for turn in range(tiles)
        ]
        if d == 0:
            loads[1].wait()
            loads[2].wait()
            forward_y(0, source)
            begin_scatter(0)
            advance()
            loads[3].wait()
            forward_y(1, receiver)
            loads[4].wait()
            forward_x()
            for ref in range(3):
                phase_table(0, ref)
            advance()
            for ref in range(3):
                shift(0, ref)
            begin_gather(0)
            loads[5].wait()
            loads[6].wait()
            loads[7].wait()
            for turn in range(tiles):
                for ref in range(3):
                    inverse(turn, ref, tile_starts[turn])
                if turn == 0:
                    advance()
            for later in range(1, depths):
                for ref in range(3):
                    phase_table(later, ref)
            advance()
            lag_table()
            begin_last(0)
            for turn in range(tiles // 2):
                mix_tile(0, turn, tile_starts[turn])
            swap_last(0).wait()
            advance()
            for turn in range(tiles // 2, tiles):
                mix_tile(0, turn, tile_starts[turn])
        else:
            forward_y(0, fields.at[0])
            forward_y(1, fields.at[1])
            forward_x()
            if d == 1:
                for _ in range(2 * levels):
                    advance()
            for ref in range(3):
                shift(d, ref)
            for turn in range(tiles):
                for ref in range(3):
                    inverse(turn, ref, tile_starts[turn])
                if turn == 0:
                    swap_last(d).wait()
                mix_tile(d, turn, tile_starts[turn])
        received[d, me] = cross[d, me]
    for d in range(depths):
        @pl.loop(1, devices)
        def _(hop):
            send_cross(d, hop).wait()


def cross_spectra(
    devices, bins, gaps, slab_map, corner, source, receiver, slabs, bracket
):
    depths, rows_x, cols_y = bracket.shape
    slab_count, rows_all, cols_all = slabs.shape
    chips = devices // 2
    share_rows = rows_x // devices
    table_f, table_i = real_transform(rows_x)
    table_y, table_z = (table.T for table in real_transform(cols_y))
    vmem = pl.BlockSpec(memory_space=pltpu.VMEM)
    flops = 8 * rows_x * (rows_x + cols_y) * 4 * cols_y * depths
    dma = pltpu.SemaphoreType.DMA
    held = (depths, chips, share_rows, cols_y)
    field = pltpu.VMEM((2, rows_x, cols_y), jnp.bfloat16)
    return pl.pallas_call(
        functools.partial(window_kernel, devices),
        out_shape=(
            jax.ShapeDtypeStruct((depths, devices, 2, share_rows, cols_y), jnp.bfloat16),
            jax.ShapeDtypeStruct((2 * devices, LAGS), jnp.bfloat16),
        ),
        in_specs=[pl.BlockSpec(memory_space=pltpu.SMEM)] * 4
        + [pl.BlockSpec(memory_space=pltpu.HBM)] * 8,
        out_specs=(vmem, vmem),
        scratch_shapes=[
            pltpu.VMEM(slabs.shape, jnp.bfloat16),
            field,
            pltpu.VMEM(table_y.shape, jnp.bfloat16),
            field,
            pltpu.VMEM(table_f.shape, jnp.bfloat16),
            pltpu.VMEM(table_i.shape, jnp.bfloat16),
            pltpu.VMEM(bracket.shape, jnp.int32),
            pltpu.VMEM(table_z.shape, jnp.bfloat16),
            pltpu.VMEM((rows_x, 4 * cols_y), jnp.bfloat16),
            pltpu.VMEM((rows_x, 4 * cols_y), jnp.float32),
            pltpu.VMEM((depths, 3, 2, rows_x // 2 + chunk, cols_y), jnp.float32),
            pltpu.VMEM((3, rows_x, 4 * cols_y), jnp.bfloat16),
            pltpu.VMEM((tile, 4 * cols_y), jnp.bfloat16),
            pltpu.VMEM((rows_x // tile, 3, tile, 4 * cols_y), jnp.float32),
            pltpu.VMEM((2, 2, rows_x, cols_y), jnp.bfloat16),
            pltpu.VMEM((depths, devices, 2, share_rows, cols_y), jnp.bfloat16),
            pltpu.VMEM((rows_all, cols_y), jnp.bfloat16),
            pltpu.VMEM((depths, 2, chips, share_rows, cols_y), jnp.bfloat16),
            pltpu.VMEM(held, jnp.bfloat16),
            pltpu.VMEM(held, jnp.bfloat16),
            pltpu.VMEM(held, jnp.bfloat16),
            pltpu.VMEM((depths, share_rows, cols_y), jnp.bfloat16),
            pltpu.VMEM((depths, 2, chips, share_rows, cols_y), jnp.bfloat16),
            pltpu.VMEM((2 * devices, LAGS), jnp.float32),
            dma((8,)),
            dma((depths, 4)),
            dma((depths, 2, chips)),
            dma((depths, 2, chips)),
            dma((depths, 2, 2 * chips.bit_length() - 3)),
            dma((depths, 2, devices)),
        ],
        cost_estimate=pl.CostEstimate(
            flops=flops, bytes_accessed=8 * 1024 * 1024, transcendentals=0
        ),
        compiler_params=pltpu.CompilerParams(
            collective_id=0, has_side_effects=True, vmem_limit_bytes=44 * 1024 * 1024
        ),
    )(
        *[
            pltpu.with_memory_space_constraint(value, pltpu.HBM)
            for value in (
                bins, gaps, slab_map, corner, slabs, source, jnp.asarray(table_y), receiver,
                jnp.asarray(table_f), jnp.asarray(table_i), bracket, jnp.asarray(table_z),
            )
        ]
    )


def image_kernel(scale, crosses, weights, out):
    _, slots, _, _, cols_y = crosses.shape
    _, rows, _, _ = out.shape
    step = pl.multiple_of(pl.program_id(1) * rows, rows)
    values = crosses[pl.program_id(0), :, :, pl.ds(step, rows), :]
    values = values.astype(jnp.float32).reshape(2 * slots, rows, cols_y)
    values = jnp.swapaxes(values, 0, 1).astype(jnp.bfloat16)
    for row in range(rows):
        out[0, row] = scale * lax.dot_general(
            values[row], weights[...], (((0,), (0,)), ((), ())),
            preferred_element_type=jnp.float32,
        )


def lag_image(crosses, weights):
    depths, slots, _, rows, cols_y = crosses.shape
    lag_count = weights.shape[1]
    step = min(16, rows)
    whole = pl.BlockSpec(memory_space=pltpu.VMEM)
    return pl.pallas_call(
        functools.partial(image_kernel, slots ** (-0.5)),
        out_shape=jax.ShapeDtypeStruct((depths, rows, cols_y, lag_count), jnp.float32),
        grid=(depths, rows // step),
        in_specs=[whole, whole],
        out_specs=pl.BlockSpec((1, step, cols_y, lag_count), lambda d, r: (d, r, 0, 0)),
        compiler_params=pltpu.CompilerParams(vmem_limit_bytes=24 * 1024 * 1024),
    )(crosses, weights)


def shards(
    devices,
    source_field,
    receiver_field,
    slowness_slabs,
    slab_map,
    reference_gaps,
    reference_index,
    frequency_bins,
    shot_corner,
):
    crosses, weights = cross_spectra(
        devices, frequency_bins, reference_gaps, slab_map, shot_corner, source_field[:, 0],
        receiver_field[:, 0], slowness_slabs, reference_index,
    )
    return lag_image(crosses, weights)


def solution(mesh):
    placed = (
        P("grp", "freq", None, None),
        P("grp", "freq", None, None),
        P(("grp", "freq"), None, None),
        P("grp"),
        P("grp", None),
        P("grp", None, None),
        P(),
        P("grp"),
    )
    return jax.shard_map(
        functools.partial(shards, mesh.shape["freq"]),
        mesh=mesh,
        in_specs=placed,
        out_specs=P("grp", "freq", None, None),
        check_vma=False,
    )
```

```python
import functools
import math

import jax
import jax.numpy as jnp
import numpy as np
from jax import lax
from jax.experimental import pallas as pl
from jax.experimental.pallas import tpu as pltpu
from jax.sharding import PartitionSpec as P

LAGS = 256

cell_width = 0.0125
layer_thick = 0.0125
bin_hertz = 0.5
period_bins = 500
slow_base = 0.3
chunk = 16
tile = 256


def parts_of(length):
    steps = np.arange(length, dtype=np.int64)
    phases = np.mod(steps[:, None] * steps[None, :], length).astype(np.float32)
    angles = phases * np.float32(2.0 * math.pi / length)
    scale = np.float32(1.0 / math.sqrt(length))
    return np.cos(angles) * scale, np.sin(angles) * scale


def real_transform(length):
    cosine, sine = (part.astype(jnp.bfloat16) for part in parts_of(length))
    half = length // 2
    basis = np.concatenate([cosine[: half + 1], sine[1:half]], axis=0)
    twice = np.full((length, 1), 2.0, np.float32)
    twice[0] = twice[half] = 1.0
    return (basis.astype(np.float32) * twice).astype(jnp.bfloat16), basis.T


def sin_cos(angle):
    turns = jnp.floor(angle * (2.0 / math.pi) + 0.5)
    rest = angle - turns * 1.5707855224609375
    rest = rest - turns * 1.0804334124e-05
    quarter = turns.astype(jnp.int32)
    square = rest * rest
    sine = rest + rest * square * (
        -1.6666654611e-1 + square * (8.3321608736e-3 + square * -1.9515295891e-4)
    )
    cosine = (
        1.0
        - 0.5 * square
        + square * square
        * (4.166664568298827e-2 + square * (-1.388731625493765e-3 + square * 2.443315711809948e-5))
    )
    odd = (quarter & 1) == 1
    sine_out = jnp.where(odd, cosine, sine)
    cosine_out = jnp.where(odd, sine, cosine)
    sine_out = jnp.where((quarter & 2) == 2, -sine_out, sine_out)
    cosine_out = jnp.where(((quarter + 1) & 2) == 2, -cosine_out, cosine_out)
    return sine_out, cosine_out


def window_kernel(
    devices, bins, gaps, slab_map, corner, slab_in, source_in, table_y_in, receiver_in,
    table_f_in, table_i_in, bracket_in, table_z_in,
    received, weights,
    slab, source, table_y, receiver, table_f, table_i, bracket, table_z,
    half, spectrum, phases, shifted, returned, refocused, fields, cross,
    wide, windows, pair, part, parts, total, slow, phase_rows,
    load_sems, pair_sems, scatter_sems, gather_sems, cross_sems,
):
    depths, rows_x, cols_y = bracket.shape
    slab_count, rows_all, cols_all = slab.shape
    chips = devices // 2
    me = lax.axis_index("freq")
    grp = lax.axis_index("grp")
    core = lax.rem(me, 2)
    chip = me // 2
    other = 1 - core
    share_rows = rows_x // devices
    signs = (1.0, -1.0)
    middle = rows_x // 2
    tiles = rows_x // tile
    group = max(share_rows, chunk)
    groups = tile // group
    angular = bins[me].astype(jnp.float32) * (2.0 * math.pi * bin_hertz)
    references = []
    for d in range(depths):
        first = gaps[d, 0]
        second = first + gaps[d, 1]
        third = second + gaps[d, 2]
        references.append((slow_base + first, slow_base + second, slow_base + third))

    loads = [
        pltpu.make_async_copy(far, near, load_sems.at[place])
        for place, (far, near) in enumerate((
            (slab_in, slab), (source_in, source), (table_y_in, table_y), (receiver_in, receiver),
            (table_f_in, table_f), (bracket_in, bracket), (table_i_in, table_i), (table_z_in, table_z),
        ))
    ]

    def lanes(which, side):
        return pl.ds((2 * which + side) * cols_y, cols_y)

    def remote(source_ref, target_ref, sems, place):
        return pltpu.make_async_remote_copy(
            src_ref=source_ref, dst_ref=target_ref, send_sem=sems[0], recv_sem=sems[1],
            device_id=(grp, place), device_id_type=pl.DeviceIdType.MESH,
        )

    def hop_to(hop):
        return lax.rem(chip + hop, chips)

    def swap_first(d):
        return remote(
            windows.at[d, other], pair.at[d], (pair_sems.at[d, 0], pair_sems.at[d, 1]),
            chip * 2 + other,
        )

    def scatter(d, hop):
        return remote(
            part.at[d, hop_to(hop)], parts.at[d, hop],
            (scatter_sems.at[d, 0, hop], scatter_sems.at[d, 1, hop]), hop_to(hop) * 2 + core,
        )

    def gather(d, hop):
        return remote(
            total.at[d], slow.at[d, core, chip],
            (gather_sems.at[d, 0, hop], gather_sems.at[d, 1, hop]), hop_to(hop) * 2 + core,
        )

    def swap_last(d):
        return remote(
            slow.at[d, core], slow.at[d, core], (pair_sems.at[d, 2], pair_sems.at[d, 3]),
            chip * 2 + other,
        )

    def send_cross(d, hop):
        to = lax.rem(me + hop, devices)
        return remote(
            cross.at[d, to], received.at[d, me],
            (cross_sems.at[d, 0, hop], cross_sems.at[d, 1, hop]), to,
        )

    def begin_scatter(d):
        swap_first(d).wait()
        part[d] = windows[d, core] + pair[d]

        @pl.loop(1, chips)
        def _(hop):
            scatter(d, hop).start()

    def begin_gather(d):
        @pl.loop(1, chips)
        def _(hop):
            scatter(d, hop).wait()

        summed = part[d, chip]
        for hop in range(1, chips):
            summed = summed + parts[d, hop]
        total[d] = summed
        slow[d, core, chip] = summed

        @pl.loop(1, chips)
        def _(hop):
            gather(d, hop).start()

    def begin_last(d):
        @pl.loop(1, chips)
        def _(hop):
            gather(d, hop).wait()

        swap_last(d).start()

    barrier = pltpu.get_barrier_semaphore()

    @pl.loop(1, devices)
    def _(hop):
        pl.semaphore_signal(
            barrier, inc=1, device_id=(grp, lax.rem(me + hop, devices)),
            device_id_type=pl.DeviceIdType.MESH,
        )

    loads[0].start()

    def one_hot(sizes, offset):
        ahead = lax.broadcasted_iota(jnp.int32, sizes, 0) - lax.broadcasted_iota(
            jnp.int32, sizes, 1
        )
        return jnp.where(ahead == offset, 1.0, 0.0).astype(jnp.bfloat16)

    def cut_slab(which):
        pick = one_hot((cols_all, cols_y), corner[1])
        for start in range(0, rows_all, tile):
            size = min(tile, rows_all - start)
            wide[pl.ds(start, size), :] = jnp.dot(
                slab[which, pl.ds(start, size), :], pick, preferred_element_type=jnp.float32
            ).astype(jnp.bfloat16)

    def put_windows(steps):
        kept = []
        for d in steps:
            apart = jnp.abs(lax.div(slab_map[d], slab_count) - me)
            kept.append((1 - jnp.minimum(apart, 1)).astype(jnp.float32))
        reach = tile + rows_all - rows_x
        pick = one_hot((tile, reach), -corner[0])
        for start in range(0, rows_x, tile):
            values = jnp.dot(
                pick, wide[pl.ds(start, reach), :], preferred_element_type=jnp.float32
            )
            for d, keep in zip(steps, kept):
                held = (values * keep).astype(jnp.bfloat16)
                for piece in range(tile // share_rows):
                    block = start // share_rows + piece
                    windows[d, block // chips, block % chips] = held[
                        piece * share_rows : (piece + 1) * share_rows
                    ]

    loads[0].wait()
    for load in loads[1:]:
        load.start()
    if slab_count == 1:
        cut_slab(0)
        put_windows(range(depths))
    else:
        for d in range(depths):
            cut_slab(lax.rem(slab_map[d], slab_count))
            put_windows((d,))
    pl.semaphore_wait(barrier, devices - 1)
    for d in range(depths):
        swap_first(d).start()

    columns = lax.broadcasted_iota(jnp.int32, (chunk, cols_y), 1)
    wave_y = jnp.where(columns <= cols_y // 2, columns, columns - cols_y // 2).astype(
        jnp.float32
    ) * (2.0 * math.pi / (cols_y * cell_width))
    squares_y = wave_y * wave_y
    counted = lax.broadcasted_iota(jnp.int32, (chunk, cols_y), 0)

    def phase_chunk(d, ref, start, magnitude):
        wave_x = magnitude.astype(jnp.float32) * (2.0 * math.pi / (rows_x * cell_width))
        reach = angular * references[d][ref]
        radicand = reach * reach - (wave_x * wave_x + squares_y)
        depth = jnp.sqrt(jnp.abs(radicand)) * layer_thick
        moving = radicand > 0.0
        fading = jnp.exp(jnp.where(moving, 0.0, -depth))
        sine, cosine = sin_cos(jnp.where(moving, depth, 0.0) - reach * layer_thick)
        phases[d, ref, 0, pl.ds(start, chunk), :] = fading * cosine
        phases[d, ref, 1, pl.ds(start, chunk), :] = fading * sine

    def phase_table(d, ref):
        @pl.loop(0, middle // chunk)
        def _(number):
            start = pl.multiple_of(number * chunk, chunk)
            phase_chunk(d, ref, start, counted + start)

        phase_chunk(d, ref, middle, jnp.where(counted == 0, middle, counted))

    def apply_phase(d, ref, start, place):
        rows = pl.ds(start, chunk)
        cosine = phases[d, ref, 0, pl.ds(place, chunk), :]
        sine = phases[d, ref, 1, pl.ds(place, chunk), :]
        for which in range(2):
            turned = signs[which] * sine
            real = spectrum[rows, lanes(which, 0)]
            imag = spectrum[rows, lanes(which, 1)]
            shifted[ref, rows, lanes(which, 0)] = (cosine * real - turned * imag).astype(
                jnp.bfloat16
            )
            shifted[ref, rows, lanes(which, 1)] = (cosine * imag + turned * real).astype(
                jnp.bfloat16
            )

    def shift_chunk(d, ref, start):
        apply_phase(d, ref, start, start)
        apply_phase(d, ref, pl.multiple_of(middle + start, chunk), start)

    def shift_edge(d, ref):
        apply_phase(d, ref, 0, 0)
        apply_phase(d, ref, middle, middle)

    def shift(d, ref):
        @pl.loop(1, middle // chunk)
        def _(number):
            shift_chunk(d, ref, pl.multiple_of(number * chunk, chunk))

        shift_edge(d, ref)

    def slow_rows(d, start):
        if share_rows >= chunk:
            block = start // share_rows
            inner = pl.multiple_of(lax.rem(start, share_rows), chunk)
            return slow[d, block // chips, lax.rem(block, chips), pl.ds(inner, chunk), :].astype(
                jnp.float32
            )
        pieces = []
        for piece in range(chunk // share_rows):
            block = start // share_rows + piece
            pieces.append(
                slow[d, block // chips, lax.rem(block, chips)].astype(jnp.float32)
            )
        return jnp.concatenate(pieces, axis=0)

    def store_cross(d, start, which, values):
        if share_rows >= chunk:
            inner = pl.multiple_of(lax.rem(start, share_rows), chunk)
            cross[d, start // share_rows, which, pl.ds(inner, chunk), :] = values.astype(
                jnp.bfloat16
            )
        else:
            for piece in range(chunk // share_rows):
                cross[d, start // share_rows + piece, which] = values[
                    piece * share_rows : (piece + 1) * share_rows
                ].astype(jnp.bfloat16)

    def mix(d, turn, inside, start):
        local = pl.ds(inside, chunk)
        rows = pl.ds(start, chunk)
        slowness = slow_rows(d, start)
        lower = bracket[d, rows, :] == 0
        slow_low = jnp.where(lower, references[d][0], references[d][1])
        slow_gap = jnp.where(
            lower, references[d][1] - references[d][0], references[d][2] - references[d][1]
        )
        weight = jnp.clip((slowness - slow_low) / slow_gap, 0.0, 1.0)
        sine, cosine = sin_cos((angular * layer_thick) * slowness)
        rounded = []
        for which in range(2):
            mixed = []
            for side in range(2):
                first = refocused[turn, 0, local, lanes(which, side)]
                second = refocused[turn, 1, local, lanes(which, side)]
                third = refocused[turn, 2, local, lanes(which, side)]
                low = jnp.where(lower, first, second)
                high = jnp.where(lower, second, third)
                mixed.append((1.0 - weight) * low + weight * high)
            turned = signs[which] * sine
            real = (cosine * mixed[0] - turned * mixed[1]).astype(jnp.bfloat16)
            imag = (turned * mixed[0] + cosine * mixed[1]).astype(jnp.bfloat16)
            if d < depths - 1:
                fields[which, 0, rows, :] = real
                fields[which, 1, rows, :] = imag
            rounded.append((real.astype(jnp.float32), imag.astype(jnp.float32)))
        (sr, si), (rr, ri) = rounded
        store_cross(d, start, 0, sr * rr + si * ri)
        store_cross(d, start, 1, sr * ri - si * rr)

    def forward_y(which, field):
        for side in range(2):
            for start in range(0, rows_x, tile):
                rows = pl.ds(start, tile)
                half[rows, lanes(which, side)] = jnp.dot(
                    field[side, rows, :], table_y[...], preferred_element_type=jnp.float32
                ).astype(jnp.bfloat16)

    def forward_x():
        @pl.loop(0, rows_x // tile)
        def _(number):
            rows = pl.ds(pl.multiple_of(number * tile, tile), tile)
            spectrum[rows, :] = jnp.dot(
                table_f[rows, :], half[...], preferred_element_type=jnp.float32
            )

    def inverse(turn, ref, tile_start):
        returned[...] = jnp.dot(
            table_i[pl.ds(tile_start, tile), :], shifted[ref], preferred_element_type=jnp.float32
        ).astype(jnp.bfloat16)
        for which in range(2):
            for side in range(2):
                refocused[turn, ref, :, lanes(which, side)] = jnp.dot(
                    returned[:, lanes(which, side)], table_z[...],
                    preferred_element_type=jnp.float32,
                )

    def send_group(d, tile_start, index):
        for each in range(group // share_rows):
            to = (tile_start + index * group) // share_rows + each
            hop = lax.rem(to - me + devices, devices)

            @pl.when(hop != 0)
            def _():
                send_cross(d, hop).start()

    own_tile = me * share_rows // tile
    own_group = lax.rem(me * share_rows, tile) // group

    def turn_index(number):
        return lax.rem(own_group + 1 + number, groups)

    def mix_tile(d, turn, tile_start):
        @pl.loop(0, groups)
        def _(number):
            for each in range(group // chunk):
                inside = pl.multiple_of(turn_index(number) * group + each * chunk, chunk)
                mix(d, turn, inside, pl.multiple_of(tile_start + inside, chunk))

            @pl.when(number > 0)
            def _():
                send_group(d, tile_start, turn_index(number - 1))

        send_group(d, tile_start, turn_index(groups - 1))

    def lag_table():
        lag_count = weights.shape[1]
        offsets = (
            lax.broadcasted_iota(jnp.int32, (1, lag_count), 1) - lag_count // 2
        ).astype(jnp.float32)

        @pl.loop(0, devices)
        def _(slot):
            turned = bins[slot].astype(jnp.float32) * offsets
            phase_rows[pl.ds(2 * slot, 1), :] = turned
            phase_rows[pl.ds(2 * slot + 1, 1), :] = turned

        counts = phase_rows[...]
        wraps = jnp.floor((counts + 0.5) * (1.0 / period_bins))
        sine, cosine = sin_cos((counts - wraps * period_bins) * (2.0 * math.pi / period_bins))
        odd = lax.broadcasted_iota(jnp.int32, counts.shape, 0) % 2 == 1
        weights[...] = jnp.where(odd, -sine, cosine).astype(jnp.bfloat16)

    first_tiles = (core * (tiles // 2),) + (own_tile + 1,) * (depths - 1)
    for d in range(depths):
        tile_starts = [
            pl.multiple_of(lax.rem(first_tiles[d] + turn, tiles) * tile, tile)
            for turn in range(tiles)
        ]
        if d == 0:
            loads[1].wait()
            loads[2].wait()
            forward_y(0, source)
            begin_scatter(0)
            loads[3].wait()
            forward_y(1, receiver)
            loads[4].wait()
            forward_x()
            for later in range(1, depths):
                begin_scatter(later)
            for ref in range(3):
                phase_table(0, ref)
                shift(0, ref)
            begin_gather(0)
            loads[5].wait()
            loads[6].wait()
            loads[7].wait()
            for turn in range(tiles):
                for ref in range(3):
                    inverse(turn, ref, tile_starts[turn])
            for later in range(1, depths):
                begin_gather(later)
            for later in range(1, depths):
                for ref in range(3):
                    phase_table(later, ref)
            lag_table()
            begin_last(0)
            for turn in range(tiles // 2):
                mix_tile(0, turn, tile_starts[turn])
            swap_last(0).wait()
            for turn in range(tiles // 2, tiles):
                mix_tile(0, turn, tile_starts[turn])
            for later in range(1, depths):
                begin_last(later)
        else:
            forward_y(0, fields.at[0])
            forward_y(1, fields.at[1])
            forward_x()
            for ref in range(3):
                shift(d, ref)
            for turn in range(tiles):
                for ref in range(3):
                    inverse(turn, ref, tile_starts[turn])
                if turn == 0:
                    swap_last(d).wait()
                mix_tile(d, turn, tile_starts[turn])
        received[d, me] = cross[d, me]
    for d in range(depths):
        @pl.loop(1, devices)
        def _(hop):
            send_cross(d, hop).wait()


def cross_spectra(
    devices, bins, gaps, slab_map, corner, source, receiver, slabs, bracket
):
    depths, rows_x, cols_y = bracket.shape
    slab_count, rows_all, cols_all = slabs.shape
    chips = devices // 2
    share_rows = rows_x // devices
    table_f, table_i = real_transform(rows_x)
    table_y, table_z = (table.T for table in real_transform(cols_y))
    vmem = pl.BlockSpec(memory_space=pltpu.VMEM)
    flops = 8 * rows_x * (rows_x + cols_y) * 4 * cols_y * depths
    dma = pltpu.SemaphoreType.DMA
    held = (depths, chips, share_rows, cols_y)
    field = pltpu.VMEM((2, rows_x, cols_y), jnp.bfloat16)
    return pl.pallas_call(
        functools.partial(window_kernel, devices),
        out_shape=(
            jax.ShapeDtypeStruct((depths, devices, 2, share_rows, cols_y), jnp.bfloat16),
            jax.ShapeDtypeStruct((2 * devices, LAGS), jnp.bfloat16),
        ),
        in_specs=[pl.BlockSpec(memory_space=pltpu.SMEM)] * 4
        + [pl.BlockSpec(memory_space=pltpu.HBM)] * 8,
        out_specs=(vmem, vmem),
        scratch_shapes=[
            pltpu.VMEM(slabs.shape, jnp.bfloat16),
            field,
            pltpu.VMEM(table_y.shape, jnp.bfloat16),
            field,
            pltpu.VMEM(table_f.shape, jnp.bfloat16),
            pltpu.VMEM(table_i.shape, jnp.bfloat16),
            pltpu.VMEM(bracket.shape, jnp.int32),
            pltpu.VMEM(table_z.shape, jnp.bfloat16),
            pltpu.VMEM((rows_x, 4 * cols_y), jnp.bfloat16),
            pltpu.VMEM((rows_x, 4 * cols_y), jnp.float32),
            pltpu.VMEM((depths, 3, 2, rows_x // 2 + chunk, cols_y), jnp.float32),
            pltpu.VMEM((3, rows_x, 4 * cols_y), jnp.bfloat16),
            pltpu.VMEM((tile, 4 * cols_y), jnp.bfloat16),
            pltpu.VMEM((rows_x // tile, 3, tile, 4 * cols_y), jnp.float32),
            pltpu.VMEM((2, 2, rows_x, cols_y), jnp.bfloat16),
            pltpu.VMEM((depths, devices, 2, share_rows, cols_y), jnp.bfloat16),
            pltpu.VMEM((rows_all, cols_y), jnp.bfloat16),
            pltpu.VMEM((depths, 2, chips, share_rows, cols_y), jnp.bfloat16),
            pltpu.VMEM(held, jnp.bfloat16),
            pltpu.VMEM(held, jnp.bfloat16),
            pltpu.VMEM(held, jnp.bfloat16),
            pltpu.VMEM((depths, share_rows, cols_y), jnp.bfloat16),
            pltpu.VMEM((depths, 2, chips, share_rows, cols_y), jnp.bfloat16),
            pltpu.VMEM((2 * devices, LAGS), jnp.float32),
            dma((8,)),
            dma((depths, 4)),
            dma((depths, 2, chips)),
            dma((depths, 2, chips)),
            dma((depths, 2, devices)),
        ],
        cost_estimate=pl.CostEstimate(
            flops=flops, bytes_accessed=8 * 1024 * 1024, transcendentals=0
        ),
        compiler_params=pltpu.CompilerParams(
            collective_id=0, has_side_effects=True, vmem_limit_bytes=44 * 1024 * 1024
        ),
    )(
        *[
            pltpu.with_memory_space_constraint(value, pltpu.HBM)
            for value in (
                bins, gaps, slab_map, corner, slabs, source, jnp.asarray(table_y), receiver,
                jnp.asarray(table_f), jnp.asarray(table_i), bracket, jnp.asarray(table_z),
            )
        ]
    )


def image_kernel(scale, crosses, weights, out):
    _, slots, _, _, cols_y = crosses.shape
    _, rows, _, _ = out.shape
    step = pl.multiple_of(pl.program_id(1) * rows, rows)
    values = crosses[pl.program_id(0), :, :, pl.ds(step, rows), :]
    values = values.astype(jnp.float32).reshape(2 * slots, rows, cols_y)
    values = jnp.swapaxes(values, 0, 1).astype(jnp.bfloat16)
    for row in range(rows):
        out[0, row] = scale * lax.dot_general(
            values[row], weights[...], (((0,), (0,)), ((), ())),
            preferred_element_type=jnp.float32,
        )


def lag_image(crosses, weights):
    depths, slots, _, rows, cols_y = crosses.shape
    lag_count = weights.shape[1]
    step = min(16, rows)
    whole = pl.BlockSpec(memory_space=pltpu.VMEM)
    return pl.pallas_call(
        functools.partial(image_kernel, slots ** (-0.5)),
        out_shape=jax.ShapeDtypeStruct((depths, rows, cols_y, lag_count), jnp.float32),
        grid=(depths, rows // step),
        in_specs=[whole, whole],
        out_specs=pl.BlockSpec((1, step, cols_y, lag_count), lambda d, r: (d, r, 0, 0)),
        compiler_params=pltpu.CompilerParams(vmem_limit_bytes=24 * 1024 * 1024),
    )(crosses, weights)


def shards(
    devices,
    source_field,
    receiver_field,
    slowness_slabs,
    slab_map,
    reference_gaps,
    reference_index,
    frequency_bins,
    shot_corner,
):
    crosses, weights = cross_spectra(
        devices, frequency_bins, reference_gaps, slab_map, shot_corner, source_field[:, 0],
        receiver_field[:, 0], slowness_slabs, reference_index,
    )
    return lag_image(crosses, weights)


def solution(mesh):
    placed = (
        P("grp", "freq", None, None),
        P("grp", "freq", None, None),
        P(("grp", "freq"), None, None),
        P("grp"),
        P("grp", None),
        P("grp", None, None),
        P(),
        P("grp"),
    )
    return jax.shard_map(
        functools.partial(shards, mesh.shape["freq"]),
        mesh=mesh,
        in_specs=placed,
        out_specs=P("grp", "freq", None, None),
        check_vma=False,
    )
```

```python
import functools
import math

import jax
import jax.numpy as jnp
import numpy as np
from jax import lax
from jax.experimental import pallas as pl
from jax.experimental.pallas import tpu as pltpu
from jax.sharding import PartitionSpec as P

LAGS = 256

cell_width = 0.0125
layer_thick = 0.0125
bin_hertz = 0.5
period_bins = 500
slow_base = 0.3
chunk = 16
tile = 256
strip = 64


def parts_of(length):
    steps = np.arange(length, dtype=np.int64)
    phases = np.mod(steps[:, None] * steps[None, :], length).astype(np.float32)
    angles = phases * np.float32(2.0 * math.pi / length)
    scale = np.float32(1.0 / math.sqrt(length))
    return np.cos(angles) * scale, np.sin(angles) * scale


def real_transform(length):
    cosine, sine = (part.astype(jnp.bfloat16) for part in parts_of(length))
    half = length // 2
    basis = np.concatenate([cosine[: half + 1], sine[1:half]], axis=0)
    twice = np.full((length, 1), 2.0, np.float32)
    twice[0] = twice[half] = 1.0
    return (basis.astype(np.float32) * twice).astype(jnp.bfloat16), basis.T


def sin_cos(half_angle):
    square = half_angle * half_angle
    sine = half_angle + half_angle * square * (
        -1.6666656999673e-1
        + square * (8.3330149027548e-3 + square * (-1.9806441580e-4 + square * 2.5996687760e-6))
    )
    cosine = 1.0 + square * (
        -4.9999999543840e-1
        + square * (
            4.1666640465459e-2
            + square * (-1.3888399836750e-3 + square * (2.4761687147e-5 + square * -2.6073429763e-7))
        )
    )
    twice = sine + sine
    return -(twice * cosine), twice * sine - 1.0


def window_kernel(
    devices, bins, gaps, slab_map, corner, slab_in, source_in, table_y_in, receiver_in,
    table_f_in, table_i_in, bracket_in, table_z_in,
    received, weights,
    slab, source, table_y, receiver, table_f, table_i, bracket, table_z,
    half, spectrum, squares, edge, phases, shifted, returned, refocused, fields, cross,
    wide, windows, pair, part, parts, traded, total, slow, phase_rows,
    load_sems, pair_sems, scatter_sems, gather_sems, piece_sems, cross_sems,
):
    depths, rows_x, cols_y = bracket.shape
    slab_count, rows_all, cols_all = slab.shape
    chips = devices // 2
    me = lax.axis_index("freq")
    grp = lax.axis_index("grp")
    core = lax.rem(me, 2)
    chip = me // 2
    other = 1 - core
    share_rows = rows_x // devices
    signs = (1.0, -1.0)
    middle = rows_x // 2
    tiles = rows_x // tile
    group = max(share_rows, chunk)
    groups = tile // group
    angular = bins[me].astype(jnp.float32) * (2.0 * math.pi * bin_hertz)
    references = []
    for d in range(depths):
        first = gaps[d, 0]
        second = first + gaps[d, 1]
        third = second + gaps[d, 2]
        references.append((slow_base + first, slow_base + second, slow_base + third))

    loads = [
        pltpu.make_async_copy(far, near, load_sems.at[place])
        for place, (far, near) in enumerate((
            (slab_in, slab), (source_in, source), (table_y_in, table_y), (receiver_in, receiver),
            (table_f_in, table_f), (bracket_in, bracket), (table_i_in, table_i), (table_z_in, table_z),
        ))
    ]

    def lanes(which, side):
        return pl.ds((2 * which + side) * cols_y, cols_y)

    def remote(source_ref, target_ref, sems, place):
        return pltpu.make_async_remote_copy(
            src_ref=source_ref, dst_ref=target_ref, send_sem=sems[0], recv_sem=sems[1],
            device_id=(grp, place), device_id_type=pl.DeviceIdType.MESH,
        )

    levels = chips.bit_length() - 1
    pieced = share_rows >= chunk

    def mate(mask):
        place = 0 * chip
        for level in range(levels):
            flipped = lax.rem(chip // 2**level + mask // 2**level, 2)
            place = place + flipped * 2**level
        return place

    def swap_first(d):
        return remote(
            windows.at[d, other], pair.at[d], (pair_sems.at[d, 0], pair_sems.at[d, 1]),
            chip * 2 + other,
        )

    def scatter(d, mask):
        return remote(
            part.at[d, mate(mask)], parts.at[d, mask],
            (scatter_sems.at[d, 0, mask], scatter_sems.at[d, 1, mask]), mate(mask) * 2 + core,
        )

    def gather(d, mask):
        return remote(
            total.at[d], slow.at[d, core, chip],
            (gather_sems.at[d, 0, mask], gather_sems.at[d, 1, mask]), mate(mask) * 2 + core,
        )

    def swap_piece(d, mask):
        piece = slow.at[d, core, mate(mask)]
        return remote(
            piece, piece, (piece_sems.at[0, mask], piece_sems.at[1, mask]), chip * 2 + other
        )

    def swap_last(d):
        return remote(
            slow.at[d, core], slow.at[d, core], (pair_sems.at[d, 2], pair_sems.at[d, 3]),
            chip * 2 + other,
        )

    def send_cross(d, hop):
        to = lax.rem(me + hop, devices)
        return remote(
            cross.at[d, to], received.at[d, me],
            (cross_sems.at[d, 0, hop], cross_sems.at[d, 1, hop]), to,
        )

    sides = chips // 2
    low = lax.rem(chip, sides)
    pairs = pl.ds(2 * low, 2)
    near_start = chip - low

    def near_mate(mask):
        return lax.rem(mate(mask), sides)

    def near_scatter(d, mask):
        return remote(
            part.at[d, pl.ds(2 * near_mate(mask), 2)], parts.at[d, pl.ds(2 * mask, 2)],
            (scatter_sems.at[d, 0, mask], scatter_sems.at[d, 1, mask]),
            (near_start + near_mate(mask)) * 2 + core,
        )

    def trade(d):
        return remote(
            parts.at[d, pl.ds(0, 2)], traded.at[d],
            (scatter_sems.at[d, 0, 0], scatter_sems.at[d, 1, 0]),
            (sides - near_start + low) * 2 + core,
        )

    def near_gather(d, mask):
        return remote(
            slow.at[d, core, pairs], slow.at[d, core, pairs],
            (gather_sems.at[d, 0, mask], gather_sems.at[d, 1, mask]),
            (near_start + near_mate(mask)) * 2 + core,
        )

    def begin_near_scatter(d):
        swap_first(d).wait()
        part[d] = windows[d, core] + pair[d]

        @pl.loop(1, sides)
        def _(step):
            near_scatter(d, sides - step).start()

    def begin_trade(d):
        @pl.loop(1, sides)
        def _(mask):
            near_scatter(d, mask).wait()

        summed = part[d, pairs]
        for mask in range(1, sides):
            summed = summed + parts[d, pl.ds(2 * mask, 2)]
        parts[d, pl.ds(0, 2)] = summed
        trade(d).start()

    def begin_near_gather(d):
        trade(d).wait()
        slow[d, core, pairs] = parts[d, pl.ds(0, 2)] + traded[d]

        @pl.loop(1, sides)
        def _(step):
            near_gather(d, sides - step).start()

    def begin_near_last(d):
        @pl.loop(1, sides)
        def _(mask):
            near_gather(d, mask).wait()

        swap_last(d).start()

    def begin_scatter(d):
        swap_first(d).wait()
        part[d] = windows[d, core] + pair[d]

        @pl.loop(1, chips)
        def _(step):
            scatter(d, chips - step).start()

    def begin_gather(d):
        @pl.loop(1, chips)
        def _(hop):
            scatter(d, hop).wait()

        summed = part[d, chip]
        for hop in range(1, chips):
            summed = summed + parts[d, hop]
        total[d] = summed
        slow[d, core, chip] = summed

        @pl.loop(1, chips)
        def _(step):
            gather(d, chips - step).start()

    def begin_last(d):
        @pl.loop(1, chips)
        def _(hop):
            gather(d, hop).wait()

        swap_last(d).start()

    barrier = pltpu.get_barrier_semaphore()

    @pl.loop(1, devices)
    def _(hop):
        pl.semaphore_signal(
            barrier, inc=1, device_id=(grp, lax.rem(me + hop, devices)),
            device_id_type=pl.DeviceIdType.MESH,
        )

    loads[0].start()

    def one_hot(sizes, offset):
        ahead = lax.broadcasted_iota(jnp.int32, sizes, 0) - lax.broadcasted_iota(
            jnp.int32, sizes, 1
        )
        return jnp.where(ahead == offset, 1.0, 0.0).astype(jnp.bfloat16)

    def cut_slab(which):
        pick = one_hot((cols_all, cols_y), corner[1])
        for start in range(0, rows_all, tile):
            size = min(tile, rows_all - start)
            wide[pl.ds(start, size), :] = jnp.dot(
                slab[which, pl.ds(start, size), :], pick, preferred_element_type=jnp.float32
            ).astype(jnp.bfloat16)

    def put_windows(steps):
        kept = []
        for d in steps:
            apart = jnp.abs(lax.div(slab_map[d], slab_count) - me)
            kept.append((1 - jnp.minimum(apart, 1)).astype(jnp.float32))
        reach = tile + rows_all - rows_x
        pick = one_hot((tile, reach), -corner[0])
        for start in range(0, rows_x, tile):
            values = jnp.dot(
                pick, wide[pl.ds(start, reach), :], preferred_element_type=jnp.float32
            )
            for d, keep in zip(steps, kept):
                held = (values * keep).astype(jnp.bfloat16)
                for piece in range(tile // share_rows):
                    block = start // share_rows + piece
                    windows[d, block // chips, block % chips] = held[
                        piece * share_rows : (piece + 1) * share_rows
                    ]

    loads[0].wait()
    for load in loads[1:]:
        load.start()
    if slab_count == 1:
        cut_slab(0)
        put_windows(range(depths))
    else:
        for d in range(depths):
            cut_slab(lax.rem(slab_map[d], slab_count))
            put_windows((d,))
    pl.semaphore_wait(barrier, devices - 1)
    for d in range(depths):
        swap_first(d).start()

    half_y = cols_y // 2
    unit = 0.5 * layer_thick
    step_x = unit * 2.0 * math.pi / (rows_x * cell_width)
    step_y = unit * 2.0 * math.pi / (cols_y * cell_width)
    strips = middle // strip + 1
    counted = lax.broadcasted_iota(jnp.int32, (strip, half_y), 0)
    columns = lax.broadcasted_iota(jnp.int32, (strip, half_y), 1)

    def strip_rows(number):
        return pl.ds(pl.multiple_of(number * strip, strip), strip)

    def reach_of(d, ref):
        return angular * references[d][ref] * unit

    def turn_of(reach, square):
        radicand = reach * reach - square
        size = jnp.abs(radicand)
        depth = size * lax.rsqrt(jnp.maximum(size, 1e-30))
        moving = radicand > 0.0
        fading = jnp.exp(jnp.where(moving, 0.0, -2.0 * depth))
        sine, cosine = sin_cos(jnp.where(moving, depth, 0.0) + (0.5 * math.pi - reach))
        return fading * cosine, fading * sine

    def fill_tables():
        reach = jnp.zeros((strip, half_y), jnp.float32)
        for d in range(depths):
            for ref in range(3):
                reach = jnp.where(columns == 3 * d + ref, reach_of(d, ref), reach)

        @pl.loop(0, strips)
        def _(number):
            rows = strip_rows(number)
            index = counted + number * strip
            magnitude = jnp.where(index <= middle, index, index - middle)
            wave_x = magnitude.astype(jnp.float32) * step_x
            wave_y = columns.astype(jnp.float32) * step_y
            squares[rows, :] = wave_x * wave_x + wave_y * wave_y
            real, imag = turn_of(reach, wave_x * wave_x + (half_y * step_y) ** 2)
            edge[0, rows, :] = real
            edge[1, rows, :] = imag

    def phase_table(d, ref):
        @pl.loop(0, strips)
        def _(number):
            rows = strip_rows(number)
            for part, values in enumerate(turn_of(reach_of(d, ref), squares[rows, :])):
                phases[d, ref, part, rows, :half_y] = values
                last = pltpu.roll(edge[part, rows, :], (half_y - 3 * d - ref) % half_y, 1)
                phases[d, ref, part, rows, half_y:] = jnp.where(columns == 0, last, values)

    def apply_phase(d, ref, start, place):
        rows = pl.ds(start, chunk)
        cosine = phases[d, ref, 0, pl.ds(place, chunk), :]
        sine = phases[d, ref, 1, pl.ds(place, chunk), :]
        for which in range(2):
            turned = signs[which] * sine
            real = spectrum[rows, lanes(which, 0)]
            imag = spectrum[rows, lanes(which, 1)]
            shifted[ref, rows, lanes(which, 0)] = (cosine * real - turned * imag).astype(
                jnp.bfloat16
            )
            shifted[ref, rows, lanes(which, 1)] = (cosine * imag + turned * real).astype(
                jnp.bfloat16
            )

    def shift_chunk(d, ref, start):
        apply_phase(d, ref, start, start)
        apply_phase(d, ref, pl.multiple_of(middle + start, chunk), start)

    def shift_edge(d, ref):
        apply_phase(d, ref, 0, 0)
        apply_phase(d, ref, middle, middle)

    def shift(d, ref):
        @pl.loop(1, middle // chunk)
        def _(number):
            shift_chunk(d, ref, pl.multiple_of(number * chunk, chunk))

        shift_edge(d, ref)

    def slow_rows(d, start):
        if share_rows >= chunk:
            block = start // share_rows
            inner = pl.multiple_of(lax.rem(start, share_rows), chunk)
            return slow[d, block // chips, lax.rem(block, chips), pl.ds(inner, chunk), :].astype(
                jnp.float32
            )
        pieces = []
        for piece in range(chunk // share_rows):
            block = start // share_rows + piece
            pieces.append(
                slow[d, block // chips, lax.rem(block, chips)].astype(jnp.float32)
            )
        return jnp.concatenate(pieces, axis=0)

    def store_cross(d, start, which, values):
        if share_rows >= chunk:
            inner = pl.multiple_of(lax.rem(start, share_rows), chunk)
            cross[d, start // share_rows, which, pl.ds(inner, chunk), :] = values.astype(
                jnp.bfloat16
            )
        else:
            for piece in range(chunk // share_rows):
                cross[d, start // share_rows + piece, which] = values[
                    piece * share_rows : (piece + 1) * share_rows
                ].astype(jnp.bfloat16)

    def mix(d, turn, inside, start):
        local = pl.ds(inside, chunk)
        rows = pl.ds(start, chunk)
        slowness = slow_rows(d, start)
        lower = bracket[d, rows, :] == 0
        slow_low = jnp.where(lower, references[d][0], references[d][1])
        slow_scale = jnp.where(
            lower, 1.0 / (references[d][1] - references[d][0]),
            1.0 / (references[d][2] - references[d][1]),
        )
        weight = jnp.clip((slowness - slow_low) * slow_scale, 0.0, 1.0)
        sine, cosine = sin_cos((angular * unit) * slowness - 0.5 * math.pi)
        rounded = []
        for which in range(2):
            mixed = []
            for side in range(2):
                first = refocused[turn, 0, local, lanes(which, side)]
                second = refocused[turn, 1, local, lanes(which, side)]
                third = refocused[turn, 2, local, lanes(which, side)]
                low = jnp.where(lower, first, second)
                high = jnp.where(lower, second, third)
                mixed.append((1.0 - weight) * low + weight * high)
            turned = signs[which] * sine
            real = (cosine * mixed[0] - turned * mixed[1]).astype(jnp.bfloat16)
            imag = (turned * mixed[0] + cosine * mixed[1]).astype(jnp.bfloat16)
            if d < depths - 1:
                fields[which, 0, rows, :] = real
                fields[which, 1, rows, :] = imag
            rounded.append((real.astype(jnp.float32), imag.astype(jnp.float32)))
        (sr, si), (rr, ri) = rounded
        store_cross(d, start, 0, sr * rr + si * ri)
        store_cross(d, start, 1, sr * ri - si * rr)

    def forward_y(which, field):
        for side in range(2):
            for start in range(0, rows_x, tile):
                rows = pl.ds(start, tile)
                half[rows, lanes(which, side)] = jnp.dot(
                    field[side, rows, :], table_y[...], preferred_element_type=jnp.float32
                ).astype(jnp.bfloat16)

    def forward_x():
        @pl.loop(0, rows_x // tile)
        def _(number):
            rows = pl.ds(pl.multiple_of(number * tile, tile), tile)
            spectrum[rows, :] = jnp.dot(
                table_f[rows, :], half[...], preferred_element_type=jnp.float32
            )

    def inverse(turn, ref, tile_start):
        returned[...] = jnp.dot(
            table_i[pl.ds(tile_start, tile), :], shifted[ref], preferred_element_type=jnp.float32
        ).astype(jnp.bfloat16)
        for which in range(2):
            for side in range(2):
                refocused[turn, ref, :, lanes(which, side)] = jnp.dot(
                    returned[:, lanes(which, side)], table_z[...],
                    preferred_element_type=jnp.float32,
                )

    def send_group(d, tile_start, index):
        for each in range(group // share_rows):
            to = (tile_start + index * group) // share_rows + each
            hop = lax.rem(to - me + devices, devices)

            @pl.when(hop != 0)
            def _():
                send_cross(d, hop).start()

    own_tile = me * share_rows // tile
    own_group = lax.rem(me * share_rows, tile) // group

    def turn_index(number):
        return lax.rem(own_group + 1 + number, groups)

    def mix_tile(d, turn, tile_start):
        @pl.loop(0, groups)
        def _(number):
            for each in range(group // chunk):
                inside = pl.multiple_of(turn_index(number) * group + each * chunk, chunk)
                mix(d, turn, inside, pl.multiple_of(tile_start + inside, chunk))

            @pl.when(number > 0)
            def _():
                send_group(d, tile_start, turn_index(number - 1))

        send_group(d, tile_start, turn_index(groups - 1))

    def lag_table():
        lag_count = weights.shape[1]
        offsets = (
            lax.broadcasted_iota(jnp.int32, (1, lag_count), 1) - lag_count // 2
        ).astype(jnp.float32)

        @pl.loop(0, devices)
        def _(slot):
            turned = bins[slot].astype(jnp.float32) * offsets
            phase_rows[pl.ds(2 * slot, 1), :] = turned
            phase_rows[pl.ds(2 * slot + 1, 1), :] = turned

        counts = phase_rows[...]
        wraps = jnp.floor((counts + 0.5) * (1.0 / period_bins))
        sine, cosine = sin_cos(
            (counts - wraps * period_bins) * (math.pi / period_bins) - 0.5 * math.pi
        )
        odd = lax.broadcasted_iota(jnp.int32, counts.shape, 0) % 2 == 1
        weights[...] = jnp.where(odd, -sine, cosine).astype(jnp.bfloat16)

    def mix_piece(d, half, mask):
        block = mate(mask)
        turn = (block * share_rows) // tile
        turn = turn + jnp.where(half == core, 0, tiles // 2)
        inside = lax.rem(block * share_rows, tile)
        to = half * chips + block
        for each in range(share_rows // chunk):
            mix(
                d, turn, pl.multiple_of(inside + each * chunk, chunk),
                pl.multiple_of(to * share_rows + each * chunk, chunk),
            )
        hop = lax.rem(to - me + devices, devices)

        @pl.when(hop != 0)
        def _():
            send_cross(d, hop).start()

    def mix_pieces(d, first, end):
        @pl.loop(first, end)
        def _(mask):
            gather(d, mask).wait()
            swap_piece(d, mask).start()
            mix_piece(d, core, mask)
            swap_piece(d, mask - 1).wait()
            mix_piece(d, other, mask - 1)

    def mix_last_piece(d):
        swap_piece(d, chips - 1).wait()
        mix_piece(d, other, chips - 1)

    first_tiles = (core * (tiles // 2),) + (own_tile + 1,) * (depths - 1)
    for d in range(depths):
        tile_starts = [
            pl.multiple_of(lax.rem(first_tiles[d] + turn, tiles) * tile, tile)
            for turn in range(tiles)
        ]
        if d == 0:
            fill_tables()
            loads[1].wait()
            loads[2].wait()
            forward_y(0, source)
            begin_scatter(0)
            loads[3].wait()
            forward_y(1, receiver)
            loads[4].wait()
            forward_x()
            for later in range(1, depths):
                begin_near_scatter(later)
            for ref in range(3):
                phase_table(0, ref)
                shift(0, ref)
            loads[6].wait()
            loads[7].wait()
            for turn in range(tiles // 2):
                for ref in range(3):
                    inverse(turn, ref, tile_starts[turn])
            begin_gather(0)
            loads[5].wait()
            if pieced:
                swap_piece(0, 0).start()
                mix_piece(0, core, 0)
            for later in range(1, depths):
                begin_trade(later)
            for turn in range(tiles // 2, tiles):
                for ref in range(3):
                    inverse(turn, ref, tile_starts[turn])
            for later in range(1, depths):
                for ref in range(3):
                    phase_table(later, ref)
            if pieced:
                mix_pieces(0, 1, sides)
            for later in range(1, depths):
                begin_near_gather(later)
            if pieced:
                mix_pieces(0, sides, chips)
                mix_last_piece(0)
            else:
                begin_last(0)
                for turn in range(tiles // 2):
                    mix_tile(0, turn, tile_starts[turn])
                swap_last(0).wait()
                for turn in range(tiles // 2, tiles):
                    mix_tile(0, turn, tile_starts[turn])
        else:
            forward_y(0, fields.at[0])
            forward_y(1, fields.at[1])
            forward_x()
            begin_near_last(d)
            for ref in range(3):
                shift(d, ref)
            for turn in range(tiles):
                for ref in range(3):
                    inverse(turn, ref, tile_starts[turn])
                if turn == 0:
                    swap_last(d).wait()
                mix_tile(d, turn, tile_starts[turn])
        received[d, me] = cross[d, me]
    lag_table()
    for d in range(depths):
        @pl.loop(1, devices)
        def _(hop):
            send_cross(d, hop).wait()


def cross_spectra(
    devices, bins, gaps, slab_map, corner, source, receiver, slabs, bracket
):
    depths, rows_x, cols_y = bracket.shape
    slab_count, rows_all, cols_all = slabs.shape
    chips = devices // 2
    share_rows = rows_x // devices
    table_f, table_i = real_transform(rows_x)
    table_y, table_z = (table.T for table in real_transform(cols_y))
    vmem = pl.BlockSpec(memory_space=pltpu.VMEM)
    flops = 8 * rows_x * (rows_x + cols_y) * 4 * cols_y * depths
    dma = pltpu.SemaphoreType.DMA
    held = (depths, chips, share_rows, cols_y)
    field = pltpu.VMEM((2, rows_x, cols_y), jnp.bfloat16)
    return pl.pallas_call(
        functools.partial(window_kernel, devices),
        out_shape=(
            jax.ShapeDtypeStruct((depths, devices, 2, share_rows, cols_y), jnp.bfloat16),
            jax.ShapeDtypeStruct((2 * devices, LAGS), jnp.bfloat16),
        ),
        in_specs=[pl.BlockSpec(memory_space=pltpu.SMEM)] * 4
        + [pl.BlockSpec(memory_space=pltpu.HBM)] * 8,
        out_specs=(vmem, vmem),
        scratch_shapes=[
            pltpu.VMEM(slabs.shape, jnp.bfloat16),
            field,
            pltpu.VMEM(table_y.shape, jnp.bfloat16),
            field,
            pltpu.VMEM(table_f.shape, jnp.bfloat16),
            pltpu.VMEM(table_i.shape, jnp.bfloat16),
            pltpu.VMEM(bracket.shape, jnp.int32),
            pltpu.VMEM(table_z.shape, jnp.bfloat16),
            pltpu.VMEM((rows_x, 4 * cols_y), jnp.bfloat16),
            pltpu.VMEM((rows_x, 4 * cols_y), jnp.float32),
            pltpu.VMEM((rows_x // 2 + strip, cols_y // 2), jnp.float32),
            pltpu.VMEM((2, rows_x // 2 + strip, cols_y // 2), jnp.float32),
            pltpu.VMEM((depths, 3, 2, rows_x // 2 + strip, cols_y), jnp.float32),
            pltpu.VMEM((3, rows_x, 4 * cols_y), jnp.bfloat16),
            pltpu.VMEM((tile, 4 * cols_y), jnp.bfloat16),
            pltpu.VMEM((rows_x // tile, 3, tile, 4 * cols_y), jnp.float32),
            pltpu.VMEM((2, 2, rows_x, cols_y), jnp.bfloat16),
            pltpu.VMEM((depths, devices, 2, share_rows, cols_y), jnp.bfloat16),
            pltpu.VMEM((rows_all, cols_y), jnp.bfloat16),
            pltpu.VMEM((depths, 2, chips, share_rows, cols_y), jnp.bfloat16),
            pltpu.VMEM(held, jnp.bfloat16),
            pltpu.VMEM(held, jnp.bfloat16),
            pltpu.VMEM(held, jnp.bfloat16),
            pltpu.VMEM((depths, 2, share_rows, cols_y), jnp.bfloat16),
            pltpu.VMEM((depths, share_rows, cols_y), jnp.bfloat16),
            pltpu.VMEM((depths, 2, chips, share_rows, cols_y), jnp.bfloat16),
            pltpu.VMEM((2 * devices, LAGS), jnp.float32),
            dma((8,)),
            dma((depths, 4)),
            dma((depths, 2, chips)),
            dma((depths, 2, chips)),
            dma((2, chips)),
            dma((depths, 2, devices)),
        ],
        cost_estimate=pl.CostEstimate(
            flops=flops, bytes_accessed=8 * 1024 * 1024, transcendentals=0
        ),
        compiler_params=pltpu.CompilerParams(
            collective_id=0, has_side_effects=True, vmem_limit_bytes=44 * 1024 * 1024
        ),
    )(
        *[
            pltpu.with_memory_space_constraint(value, pltpu.HBM)
            for value in (
                bins, gaps, slab_map, corner, slabs, source, jnp.asarray(table_y), receiver,
                jnp.asarray(table_f), jnp.asarray(table_i), bracket, jnp.asarray(table_z),
            )
        ]
    )


def image_kernel(scale, crosses, weights, out, held, sems):
    depths, slots, _, rows, cols_y = crosses.shape
    step = min(16, rows)
    part = min(4, step)
    count = depths * (rows // step)

    def block(number, place):
        d = number // (rows // step)
        start = lax.rem(number, rows // step) * step + place * part
        return d, pl.ds(start, part)

    def write(number, place):
        d, local = block(number, place)
        return pltpu.make_async_copy(
            held.at[d, local], out.at[d, local], sems.at[number, place]
        )

    @pl.loop(0, count)
    def _(number):
        d = number // (rows // step)
        start = pl.multiple_of(lax.rem(number, rows // step) * step, step)
        values = crosses[d, :, :, pl.ds(start, step), :]
        values = values.astype(jnp.float32).reshape(2 * slots, step, cols_y)
        values = jnp.swapaxes(values, 0, 1).astype(jnp.bfloat16)
        for row in range(step):
            held[d, start + row] = scale * lax.dot_general(
                values[row], weights[...], (((0,), (0,)), ((), ())),
                preferred_element_type=jnp.float32,
            )
            if row % part == part - 1:
                write(number, row // part).start()

    @pl.loop(0, count)
    def _(number):
        for place in range(step // part):
            write(number, place).wait()


def lag_image(crosses, weights):
    depths, slots, _, rows, cols_y = crosses.shape
    lag_count = weights.shape[1]
    step = min(16, rows)
    whole = pl.BlockSpec(memory_space=pltpu.VMEM)
    image = (depths, rows, cols_y, lag_count)
    return pl.pallas_call(
        functools.partial(image_kernel, slots ** (-0.5)),
        out_shape=jax.ShapeDtypeStruct(image, jnp.float32),
        in_specs=[whole, whole],
        out_specs=pl.BlockSpec(memory_space=pltpu.HBM),
        scratch_shapes=[
            pltpu.VMEM(image, jnp.float32),
            pltpu.SemaphoreType.DMA((depths * (rows // step), step // min(4, step))),
        ],
        compiler_params=pltpu.CompilerParams(vmem_limit_bytes=32 * 1024 * 1024),
    )(crosses, weights)


def shards(
    devices,
    source_field,
    receiver_field,
    slowness_slabs,
    slab_map,
    reference_gaps,
    reference_index,
    frequency_bins,
    shot_corner,
):
    crosses, weights = cross_spectra(
        devices, frequency_bins, reference_gaps, slab_map, shot_corner, source_field[:, 0],
        receiver_field[:, 0], slowness_slabs, reference_index,
    )
    return lag_image(crosses, weights)


def solution(mesh):
    placed = (
        P("grp", "freq", None, None),
        P("grp", "freq", None, None),
        P(("grp", "freq"), None, None),
        P("grp"),
        P("grp", None),
        P("grp", None, None),
        P(),
        P("grp"),
    )
    return jax.shard_map(
        functools.partial(shards, mesh.shape["freq"]),
        mesh=mesh,
        in_specs=placed,
        out_specs=P("grp", "freq", None, None),
        check_vma=False,
    )
```

```python
import functools
import math

import jax
import jax.numpy as jnp
import numpy as np
from jax import lax
from jax.experimental import pallas as pl
from jax.experimental.pallas import tpu as pltpu
from jax.sharding import PartitionSpec as P

LAGS = 256

cell_width = 0.0125
layer_thick = 0.0125
bin_hertz = 0.5
period_bins = 500
slow_base = 0.3
chunk = 16
tile = 256
strip = 64


def parts_of(length):
    steps = np.arange(length, dtype=np.int64)
    phases = np.mod(steps[:, None] * steps[None, :], length).astype(np.float32)
    angles = phases * np.float32(2.0 * math.pi / length)
    scale = np.float32(1.0 / math.sqrt(length))
    return np.cos(angles) * scale, np.sin(angles) * scale


def real_transform(length):
    cosine, sine = (part.astype(jnp.bfloat16) for part in parts_of(length))
    half = length // 2
    basis = np.concatenate([cosine[: half + 1], sine[1:half]], axis=0)
    twice = np.full((length, 1), 2.0, np.float32)
    twice[0] = twice[half] = 1.0
    return (basis.astype(np.float32) * twice).astype(jnp.bfloat16), basis.T


def sin_cos(half_angle):
    square = half_angle * half_angle
    sine = half_angle + half_angle * square * (
        -1.6666656999673e-1
        + square * (8.3330149027548e-3 + square * (-1.9806441580e-4 + square * 2.5996687760e-6))
    )
    cosine = 1.0 + square * (
        -4.9999999543840e-1
        + square * (
            4.1666640465459e-2
            + square * (-1.3888399836750e-3 + square * (2.4761687147e-5 + square * -2.6073429763e-7))
        )
    )
    twice = sine + sine
    return -(twice * cosine), twice * sine - 1.0


def window_kernel(
    devices, bins, gaps, slab_map, corner, slab_in, source_in, table_y_in, receiver_in,
    table_f_in, table_i_in, bracket_in, table_z_in,
    received, weights,
    slab, source, table_y, receiver, table_f, table_i, bracket, table_z,
    half, spectrum, squares, edge, phases, shifted, returned, refocused, fields, cross,
    wide, windows, pair, part, parts, traded, total, slow, phase_rows,
    load_sems, pair_sems, scatter_sems, gather_sems, piece_sems, cross_sems,
):
    depths, rows_x, cols_y = bracket.shape
    slab_count, rows_all, cols_all = slab.shape
    chips = devices // 2
    me = lax.axis_index("freq")
    grp = lax.axis_index("grp")
    core = lax.rem(me, 2)
    chip = me // 2
    other = 1 - core
    share_rows = rows_x // devices
    signs = (1.0, -1.0)
    middle = rows_x // 2
    tiles = rows_x // tile
    group = max(share_rows, chunk)
    groups = tile // group
    angular = bins[me].astype(jnp.float32) * (2.0 * math.pi * bin_hertz)
    references = []
    for d in range(depths):
        first = gaps[d, 0]
        second = first + gaps[d, 1]
        third = second + gaps[d, 2]
        references.append((slow_base + first, slow_base + second, slow_base + third))

    loads = [
        pltpu.make_async_copy(far, near, load_sems.at[place])
        for place, (far, near) in enumerate((
            (slab_in, slab), (source_in, source), (table_y_in, table_y), (receiver_in, receiver),
            (table_f_in, table_f), (bracket_in, bracket), (table_i_in, table_i), (table_z_in, table_z),
        ))
    ]

    def lanes(which, side):
        return pl.ds((2 * which + side) * cols_y, cols_y)

    def remote(source_ref, target_ref, sems, place):
        return pltpu.make_async_remote_copy(
            src_ref=source_ref, dst_ref=target_ref, send_sem=sems[0], recv_sem=sems[1],
            device_id=(grp, place), device_id_type=pl.DeviceIdType.MESH,
        )

    levels = chips.bit_length() - 1
    pieced = share_rows >= chunk

    def mate(mask):
        place = 0 * chip
        for level in range(levels):
            flipped = lax.rem(chip // 2**level + mask // 2**level, 2)
            place = place + flipped * 2**level
        return place

    def swap_first(d):
        return remote(
            windows.at[d, other], pair.at[d], (pair_sems.at[d, 0], pair_sems.at[d, 1]),
            chip * 2 + other,
        )

    def scatter(d, mask):
        return remote(
            part.at[d, mate(mask)], parts.at[d, mask],
            (scatter_sems.at[d, 0, mask], scatter_sems.at[d, 1, mask]), mate(mask) * 2 + core,
        )

    def gather(d, mask):
        return remote(
            total.at[d], slow.at[d, core, chip],
            (gather_sems.at[d, 0, mask], gather_sems.at[d, 1, mask]), mate(mask) * 2 + core,
        )

    def swap_piece(d, mask):
        piece = slow.at[d, core, mate(mask)]
        return remote(
            piece, piece, (piece_sems.at[0, mask], piece_sems.at[1, mask]), chip * 2 + other
        )

    def swap_last(d):
        return remote(
            slow.at[d, core], slow.at[d, core], (pair_sems.at[d, 2], pair_sems.at[d, 3]),
            chip * 2 + other,
        )

    def send_cross(d, hop):
        to = lax.rem(me + hop, devices)
        return remote(
            cross.at[d, to], received.at[d, me],
            (cross_sems.at[d, 0, hop], cross_sems.at[d, 1, hop]), to,
        )

    sides = chips // 2
    low = lax.rem(chip, sides)
    pairs = pl.ds(2 * low, 2)
    near_start = chip - low

    def near_mate(mask):
        return lax.rem(mate(mask), sides)

    def near_scatter(d, mask):
        return remote(
            part.at[d, pl.ds(2 * near_mate(mask), 2)], parts.at[d, pl.ds(2 * mask, 2)],
            (scatter_sems.at[d, 0, mask], scatter_sems.at[d, 1, mask]),
            (near_start + near_mate(mask)) * 2 + core,
        )

    def trade(d):
        return remote(
            parts.at[d, pl.ds(0, 2)], traded.at[d],
            (scatter_sems.at[d, 0, 0], scatter_sems.at[d, 1, 0]),
            (sides - near_start + low) * 2 + core,
        )

    def near_gather(d, mask):
        return remote(
            slow.at[d, core, pairs], slow.at[d, core, pairs],
            (gather_sems.at[d, 0, mask], gather_sems.at[d, 1, mask]),
            (near_start + near_mate(mask)) * 2 + core,
        )

    def begin_near_scatter(d):
        swap_first(d).wait()
        part[d] = windows[d, core] + pair[d]

        @pl.loop(1, sides)
        def _(step):
            near_scatter(d, sides - step).start()

    def begin_trade(d):
        @pl.loop(1, sides)
        def _(mask):
            near_scatter(d, mask).wait()

        summed = part[d, pairs]
        for mask in range(1, sides):
            summed = summed + parts[d, pl.ds(2 * mask, 2)]
        parts[d, pl.ds(0, 2)] = summed
        trade(d).start()

    def begin_near_gather(d):
        trade(d).wait()
        slow[d, core, pairs] = parts[d, pl.ds(0, 2)] + traded[d]

        @pl.loop(1, sides)
        def _(step):
            near_gather(d, sides - step).start()

    def begin_near_last(d):
        @pl.loop(1, sides)
        def _(mask):
            near_gather(d, mask).wait()

        swap_last(d).start()

    def begin_scatter(d):
        swap_first(d).wait()
        part[d] = windows[d, core] + pair[d]

        @pl.loop(1, chips)
        def _(step):
            scatter(d, chips - step).start()

    def begin_gather(d):
        @pl.loop(1, chips)
        def _(hop):
            scatter(d, hop).wait()

        summed = part[d, chip]
        for hop in range(1, chips):
            summed = summed + parts[d, hop]
        total[d] = summed
        slow[d, core, chip] = summed

        @pl.loop(1, chips)
        def _(step):
            gather(d, chips - step).start()

    def begin_last(d):
        @pl.loop(1, chips)
        def _(hop):
            gather(d, hop).wait()

        swap_last(d).start()

    barrier = pltpu.get_barrier_semaphore()

    @pl.loop(1, devices)
    def _(hop):
        pl.semaphore_signal(
            barrier, inc=1, device_id=(grp, lax.rem(me + hop, devices)),
            device_id_type=pl.DeviceIdType.MESH,
        )

    loads[0].start()

    def one_hot(sizes, offset):
        ahead = lax.broadcasted_iota(jnp.int32, sizes, 0) - lax.broadcasted_iota(
            jnp.int32, sizes, 1
        )
        return jnp.where(ahead == offset, 1.0, 0.0).astype(jnp.bfloat16)

    def cut_slab(which):
        pick = one_hot((cols_all, cols_y), corner[1])
        for start in range(0, rows_all, tile):
            size = min(tile, rows_all - start)
            wide[pl.ds(start, size), :] = jnp.dot(
                slab[which, pl.ds(start, size), :], pick, preferred_element_type=jnp.float32
            ).astype(jnp.bfloat16)

    def put_windows(steps):
        kept = []
        for d in steps:
            apart = jnp.abs(lax.div(slab_map[d], slab_count) - me)
            kept.append((1 - jnp.minimum(apart, 1)).astype(jnp.float32))
        reach = tile + rows_all - rows_x
        pick = one_hot((tile, reach), -corner[0])
        for start in range(0, rows_x, tile):
            values = jnp.dot(
                pick, wide[pl.ds(start, reach), :], preferred_element_type=jnp.float32
            )
            for d, keep in zip(steps, kept):
                held = (values * keep).astype(jnp.bfloat16)
                for piece in range(tile // share_rows):
                    block = start // share_rows + piece
                    windows[d, block // chips, block % chips] = held[
                        piece * share_rows : (piece + 1) * share_rows
                    ]

    loads[0].wait()
    for load in loads[1:]:
        load.start()
    if slab_count == 1:
        cut_slab(0)
        put_windows(range(depths))
    else:
        for d in range(depths):
            cut_slab(lax.rem(slab_map[d], slab_count))
            put_windows((d,))
    pl.semaphore_wait(barrier, devices - 1)
    for d in range(depths):
        swap_first(d).start()

    half_y = cols_y // 2
    unit = 0.5 * layer_thick
    step_x = unit * 2.0 * math.pi / (rows_x * cell_width)
    step_y = unit * 2.0 * math.pi / (cols_y * cell_width)
    strips = middle // strip + 1
    counted = lax.broadcasted_iota(jnp.int32, (strip, half_y), 0)
    columns = lax.broadcasted_iota(jnp.int32, (strip, half_y), 1)

    def strip_rows(number):
        return pl.ds(pl.multiple_of(number * strip, strip), strip)

    def reach_of(d, ref):
        return angular * references[d][ref] * unit

    def turn_of(reach, square):
        radicand = reach * reach - square
        size = jnp.abs(radicand)
        depth = size * lax.rsqrt(jnp.maximum(size, 1e-30))
        moving = radicand > 0.0
        fading = jnp.exp(jnp.where(moving, 0.0, -2.0 * depth))
        sine, cosine = sin_cos(jnp.where(moving, depth, 0.0) + (0.5 * math.pi - reach))
        return fading * cosine, fading * sine

    def fill_tables():
        reach = jnp.zeros((strip, half_y), jnp.float32)
        for d in range(depths):
            for ref in range(3):
                reach = jnp.where(columns == 3 * d + ref, reach_of(d, ref), reach)

        @pl.loop(0, strips)
        def _(number):
            rows = strip_rows(number)
            index = counted + number * strip
            magnitude = jnp.where(index <= middle, index, index - middle)
            wave_x = magnitude.astype(jnp.float32) * step_x
            wave_y = columns.astype(jnp.float32) * step_y
            squares[rows, :] = wave_x * wave_x + wave_y * wave_y
            real, imag = turn_of(reach, wave_x * wave_x + (half_y * step_y) ** 2)
            edge[0, rows, :] = real
            edge[1, rows, :] = imag

    def phase_table(d, ref):
        @pl.loop(0, strips)
        def _(number):
            rows = strip_rows(number)
            for part, values in enumerate(turn_of(reach_of(d, ref), squares[rows, :])):
                phases[d, ref, part, rows, :half_y] = values
                last = pltpu.roll(edge[part, rows, :], (half_y - 3 * d - ref) % half_y, 1)
                phases[d, ref, part, rows, half_y:] = jnp.where(columns == 0, last, values)

    def apply_phase(d, ref, start, place):
        rows = pl.ds(start, chunk)
        cosine = phases[d, ref, 0, pl.ds(place, chunk), :]
        sine = phases[d, ref, 1, pl.ds(place, chunk), :]
        for which in range(2):
            turned = signs[which] * sine
            real = spectrum[rows, lanes(which, 0)]
            imag = spectrum[rows, lanes(which, 1)]
            shifted[ref, rows, lanes(which, 0)] = (cosine * real - turned * imag).astype(
                jnp.bfloat16
            )
            shifted[ref, rows, lanes(which, 1)] = (cosine * imag + turned * real).astype(
                jnp.bfloat16
            )

    def shift_chunk(d, ref, start):
        apply_phase(d, ref, start, start)
        apply_phase(d, ref, pl.multiple_of(middle + start, chunk), start)

    def shift_edge(d, ref):
        apply_phase(d, ref, 0, 0)
        apply_phase(d, ref, middle, middle)

    def shift(d, ref):
        @pl.loop(1, middle // chunk)
        def _(number):
            shift_chunk(d, ref, pl.multiple_of(number * chunk, chunk))

        shift_edge(d, ref)

    def slow_rows(d, start):
        if share_rows >= chunk:
            block = start // share_rows
            inner = pl.multiple_of(lax.rem(start, share_rows), chunk)
            return slow[d, block // chips, lax.rem(block, chips), pl.ds(inner, chunk), :].astype(
                jnp.float32
            )
        pieces = []
        for piece in range(chunk // share_rows):
            block = start // share_rows + piece
            pieces.append(
                slow[d, block // chips, lax.rem(block, chips)].astype(jnp.float32)
            )
        return jnp.concatenate(pieces, axis=0)

    def store_cross(d, start, which, values):
        if share_rows >= chunk:
            inner = pl.multiple_of(lax.rem(start, share_rows), chunk)
            cross[d, start // share_rows, which, pl.ds(inner, chunk), :] = values.astype(
                jnp.bfloat16
            )
        else:
            for piece in range(chunk // share_rows):
                cross[d, start // share_rows + piece, which] = values[
                    piece * share_rows : (piece + 1) * share_rows
                ].astype(jnp.bfloat16)

    def mix(d, turn, inside, start):
        local = pl.ds(inside, chunk)
        rows = pl.ds(start, chunk)
        slowness = slow_rows(d, start)
        lower = bracket[d, rows, :] == 0
        slow_low = jnp.where(lower, references[d][0], references[d][1])
        slow_scale = jnp.where(
            lower, 1.0 / (references[d][1] - references[d][0]),
            1.0 / (references[d][2] - references[d][1]),
        )
        weight = jnp.clip((slowness - slow_low) * slow_scale, 0.0, 1.0)
        sine, cosine = sin_cos((angular * unit) * slowness - 0.5 * math.pi)
        rounded = []
        for which in range(2):
            mixed = []
            for side in range(2):
                first = refocused[turn, 0, local, lanes(which, side)]
                second = refocused[turn, 1, local, lanes(which, side)]
                third = refocused[turn, 2, local, lanes(which, side)]
                low = jnp.where(lower, first, second)
                high = jnp.where(lower, second, third)
                mixed.append((1.0 - weight) * low + weight * high)
            turned = signs[which] * sine
            real = (cosine * mixed[0] - turned * mixed[1]).astype(jnp.bfloat16)
            imag = (turned * mixed[0] + cosine * mixed[1]).astype(jnp.bfloat16)
            if d < depths - 1:
                fields[which, 0, rows, :] = real
                fields[which, 1, rows, :] = imag
            rounded.append((real.astype(jnp.float32), imag.astype(jnp.float32)))
        (sr, si), (rr, ri) = rounded
        store_cross(d, start, 0, sr * rr + si * ri)
        store_cross(d, start, 1, sr * ri - si * rr)

    def forward_y(which, field):
        for side in range(2):
            for start in range(0, rows_x, tile):
                rows = pl.ds(start, tile)
                half[rows, lanes(which, side)] = jnp.dot(
                    field[side, rows, :], table_y[...], preferred_element_type=jnp.float32
                ).astype(jnp.bfloat16)

    def forward_x():
        @pl.loop(0, rows_x // tile)
        def _(number):
            rows = pl.ds(pl.multiple_of(number * tile, tile), tile)
            spectrum[rows, :] = jnp.dot(
                table_f[rows, :], half[...], preferred_element_type=jnp.float32
            )

    def inverse(turn, ref, tile_start):
        returned[...] = jnp.dot(
            table_i[pl.ds(tile_start, tile), :], shifted[ref], preferred_element_type=jnp.float32
        ).astype(jnp.bfloat16)
        for which in range(2):
            for side in range(2):
                refocused[turn, ref, :, lanes(which, side)] = jnp.dot(
                    returned[:, lanes(which, side)], table_z[...],
                    preferred_element_type=jnp.float32,
                )

    def send_group(d, tile_start, index):
        for each in range(group // share_rows):
            to = (tile_start + index * group) // share_rows + each
            hop = lax.rem(to - me + devices, devices)

            @pl.when(hop != 0)
            def _():
                send_cross(d, hop).start()

    own_tile = me * share_rows // tile
    own_group = lax.rem(me * share_rows, tile) // group

    def turn_index(number):
        return lax.rem(own_group + 1 + number, groups)

    def mix_tile(d, turn, tile_start):
        @pl.loop(0, groups)
        def _(number):
            for each in range(group // chunk):
                inside = pl.multiple_of(turn_index(number) * group + each * chunk, chunk)
                mix(d, turn, inside, pl.multiple_of(tile_start + inside, chunk))

            @pl.when(number > 0)
            def _():
                send_group(d, tile_start, turn_index(number - 1))

        send_group(d, tile_start, turn_index(groups - 1))

    def lag_table():
        lag_count = weights.shape[1]
        offsets = (
            lax.broadcasted_iota(jnp.int32, (1, lag_count), 1) - lag_count // 2
        ).astype(jnp.float32)

        @pl.loop(0, devices)
        def _(slot):
            turned = bins[slot].astype(jnp.float32) * offsets
            phase_rows[pl.ds(2 * slot, 1), :] = turned
            phase_rows[pl.ds(2 * slot + 1, 1), :] = turned

        counts = phase_rows[...]
        wraps = jnp.floor((counts + 0.5) * (1.0 / period_bins))
        sine, cosine = sin_cos(
            (counts - wraps * period_bins) * (math.pi / period_bins) - 0.5 * math.pi
        )
        odd = lax.broadcasted_iota(jnp.int32, counts.shape, 0) % 2 == 1
        weights[...] = jnp.where(odd, -sine, cosine).astype(jnp.bfloat16)

    def mix_piece(d, half, mask):
        block = mate(mask)
        turn = (block * share_rows) // tile
        turn = turn + jnp.where(half == core, 0, tiles // 2)
        inside = lax.rem(block * share_rows, tile)
        to = half * chips + block
        for each in range(share_rows // chunk):
            mix(
                d, turn, pl.multiple_of(inside + each * chunk, chunk),
                pl.multiple_of(to * share_rows + each * chunk, chunk),
            )
        hop = lax.rem(to - me + devices, devices)

        @pl.when(hop != 0)
        def _():
            send_cross(d, hop).start()

    def mix_pieces(d, first, end):
        @pl.loop(first, end)
        def _(mask):
            gather(d, mask).wait()
            swap_piece(d, mask).start()
            mix_piece(d, core, mask)
            swap_piece(d, mask - 1).wait()
            mix_piece(d, other, mask - 1)

    def mix_last_piece(d):
        swap_piece(d, chips - 1).wait()
        mix_piece(d, other, chips - 1)

    first_tiles = (core * (tiles // 2),) + (own_tile + 1,) * (depths - 1)
    for d in range(depths):
        tile_starts = [
            pl.multiple_of(lax.rem(first_tiles[d] + turn, tiles) * tile, tile)
            for turn in range(tiles)
        ]
        if d == 0:
            fill_tables()
            loads[1].wait()
            loads[2].wait()
            forward_y(0, source)
            begin_scatter(0)
            for later in range(1, depths):
                begin_near_scatter(later)
            loads[3].wait()
            forward_y(1, receiver)
            loads[4].wait()
            forward_x()
            for ref in range(3):
                phase_table(0, ref)
                shift(0, ref)
            loads[6].wait()
            loads[7].wait()
            for turn in range(tiles // 2):
                for ref in range(3):
                    inverse(turn, ref, tile_starts[turn])
            for later in range(1, depths):
                begin_trade(later)
            begin_gather(0)
            loads[5].wait()
            if pieced:
                swap_piece(0, 0).start()
                mix_piece(0, core, 0)
            for turn in range(tiles // 2, tiles):
                for ref in range(3):
                    inverse(turn, ref, tile_starts[turn])
            for later in range(1, depths):
                for ref in range(3):
                    phase_table(later, ref)
            if pieced:
                mix_pieces(0, 1, sides)
            for later in range(1, depths):
                begin_near_gather(later)
            if pieced:
                mix_pieces(0, sides, chips)
                mix_last_piece(0)
            else:
                begin_last(0)
                for turn in range(tiles // 2):
                    mix_tile(0, turn, tile_starts[turn])
                swap_last(0).wait()
                for turn in range(tiles // 2, tiles):
                    mix_tile(0, turn, tile_starts[turn])
        else:
            forward_y(0, fields.at[0])
            forward_y(1, fields.at[1])
            forward_x()
            begin_near_last(d)
            for ref in range(3):
                shift(d, ref)
            for turn in range(tiles):
                for ref in range(3):
                    inverse(turn, ref, tile_starts[turn])
                if turn == 0:
                    swap_last(d).wait()
                mix_tile(d, turn, tile_starts[turn])
        received[d, me] = cross[d, me]
    lag_table()
    for d in range(depths):
        @pl.loop(1, devices)
        def _(hop):
            send_cross(d, hop).wait()


def cross_spectra(
    devices, bins, gaps, slab_map, corner, source, receiver, slabs, bracket
):
    depths, rows_x, cols_y = bracket.shape
    slab_count, rows_all, cols_all = slabs.shape
    chips = devices // 2
    share_rows = rows_x // devices
    table_f, table_i = real_transform(rows_x)
    table_y, table_z = (table.T for table in real_transform(cols_y))
    vmem = pl.BlockSpec(memory_space=pltpu.VMEM)
    flops = 8 * rows_x * (rows_x + cols_y) * 4 * cols_y * depths
    dma = pltpu.SemaphoreType.DMA
    held = (depths, chips, share_rows, cols_y)
    field = pltpu.VMEM((2, rows_x, cols_y), jnp.bfloat16)
    return pl.pallas_call(
        functools.partial(window_kernel, devices),
        out_shape=(
            jax.ShapeDtypeStruct((depths, devices, 2, share_rows, cols_y), jnp.bfloat16),
            jax.ShapeDtypeStruct((2 * devices, LAGS), jnp.bfloat16),
        ),
        in_specs=[pl.BlockSpec(memory_space=pltpu.SMEM)] * 4
        + [pl.BlockSpec(memory_space=pltpu.HBM)] * 8,
        out_specs=(vmem, vmem),
        scratch_shapes=[
            pltpu.VMEM(slabs.shape, jnp.bfloat16),
            field,
            pltpu.VMEM(table_y.shape, jnp.bfloat16),
            field,
            pltpu.VMEM(table_f.shape, jnp.bfloat16),
            pltpu.VMEM(table_i.shape, jnp.bfloat16),
            pltpu.VMEM(bracket.shape, jnp.int32),
            pltpu.VMEM(table_z.shape, jnp.bfloat16),
            pltpu.VMEM((rows_x, 4 * cols_y), jnp.bfloat16),
            pltpu.VMEM((rows_x, 4 * cols_y), jnp.float32),
            pltpu.VMEM((rows_x // 2 + strip, cols_y // 2), jnp.float32),
            pltpu.VMEM((2, rows_x // 2 + strip, cols_y // 2), jnp.float32),
            pltpu.VMEM((depths, 3, 2, rows_x // 2 + strip, cols_y), jnp.float32),
            pltpu.VMEM((3, rows_x, 4 * cols_y), jnp.bfloat16),
            pltpu.VMEM((tile, 4 * cols_y), jnp.bfloat16),
            pltpu.VMEM((rows_x // tile, 3, tile, 4 * cols_y), jnp.float32),
            pltpu.VMEM((2, 2, rows_x, cols_y), jnp.bfloat16),
            pltpu.VMEM((depths, devices, 2, share_rows, cols_y), jnp.bfloat16),
            pltpu.VMEM((rows_all, cols_y), jnp.bfloat16),
            pltpu.VMEM((depths, 2, chips, share_rows, cols_y), jnp.bfloat16),
            pltpu.VMEM(held, jnp.bfloat16),
            pltpu.VMEM(held, jnp.bfloat16),
            pltpu.VMEM(held, jnp.bfloat16),
            pltpu.VMEM((depths, 2, share_rows, cols_y), jnp.bfloat16),
            pltpu.VMEM((depths, share_rows, cols_y), jnp.bfloat16),
            pltpu.VMEM((depths, 2, chips, share_rows, cols_y), jnp.bfloat16),
            pltpu.VMEM((2 * devices, LAGS), jnp.float32),
            dma((8,)),
            dma((depths, 4)),
            dma((depths, 2, chips)),
            dma((depths, 2, chips)),
            dma((2, chips)),
            dma((depths, 2, devices)),
        ],
        cost_estimate=pl.CostEstimate(
            flops=flops, bytes_accessed=8 * 1024 * 1024, transcendentals=0
        ),
        compiler_params=pltpu.CompilerParams(
            collective_id=0, has_side_effects=True, vmem_limit_bytes=44 * 1024 * 1024
        ),
    )(
        *[
            pltpu.with_memory_space_constraint(value, pltpu.HBM)
            for value in (
                bins, gaps, slab_map, corner, slabs, source, jnp.asarray(table_y), receiver,
                jnp.asarray(table_f), jnp.asarray(table_i), bracket, jnp.asarray(table_z),
            )
        ]
    )


def image_kernel(scale, crosses, weights, out, held, sems):
    depths, slots, _, rows, cols_y = crosses.shape
    step = min(16, rows)
    part = min(4, step)
    count = depths * (rows // step)

    def block(number, place):
        d = number // (rows // step)
        start = lax.rem(number, rows // step) * step + place * part
        return d, pl.ds(start, part)

    def write(number, place):
        d, local = block(number, place)
        return pltpu.make_async_copy(
            held.at[d, local], out.at[d, local], sems.at[number, place]
        )

    @pl.loop(0, count)
    def _(number):
        d = number // (rows // step)
        start = pl.multiple_of(lax.rem(number, rows // step) * step, step)
        values = crosses[d, :, :, pl.ds(start, step), :]
        values = values.astype(jnp.float32).reshape(2 * slots, step, cols_y)
        values = jnp.swapaxes(values, 0, 1).astype(jnp.bfloat16)
        for row in range(step):
            held[d, start + row] = scale * lax.dot_general(
                values[row], weights[...], (((0,), (0,)), ((), ())),
                preferred_element_type=jnp.float32,
            )
            if row % part == part - 1:
                write(number, row // part).start()

    @pl.loop(0, count)
    def _(number):
        for place in range(step // part):
            write(number, place).wait()


def lag_image(crosses, weights):
    depths, slots, _, rows, cols_y = crosses.shape
    lag_count = weights.shape[1]
    step = min(16, rows)
    whole = pl.BlockSpec(memory_space=pltpu.VMEM)
    image = (depths, rows, cols_y, lag_count)
    return pl.pallas_call(
        functools.partial(image_kernel, slots ** (-0.5)),
        out_shape=jax.ShapeDtypeStruct(image, jnp.float32),
        in_specs=[whole, whole],
        out_specs=pl.BlockSpec(memory_space=pltpu.HBM),
        scratch_shapes=[
            pltpu.VMEM(image, jnp.float32),
            pltpu.SemaphoreType.DMA((depths * (rows // step), step // min(4, step))),
        ],
        compiler_params=pltpu.CompilerParams(vmem_limit_bytes=32 * 1024 * 1024),
    )(crosses, weights)


def shards(
    devices,
    source_field,
    receiver_field,
    slowness_slabs,
    slab_map,
    reference_gaps,
    reference_index,
    frequency_bins,
    shot_corner,
):
    crosses, weights = cross_spectra(
        devices, frequency_bins, reference_gaps, slab_map, shot_corner, source_field[:, 0],
        receiver_field[:, 0], slowness_slabs, reference_index,
    )
    return lag_image(crosses, weights)


def solution(mesh):
    placed = (
        P("grp", "freq", None, None),
        P("grp", "freq", None, None),
        P(("grp", "freq"), None, None),
        P("grp"),
        P("grp", None),
        P("grp", None, None),
        P(),
        P("grp"),
    )
    return jax.shard_map(
        functools.partial(shards, mesh.shape["freq"]),
        mesh=mesh,
        in_specs=placed,
        out_specs=P("grp", "freq", None, None),
        check_vma=False,
    )
```

```python
import functools
import math

import jax
import jax.numpy as jnp
import numpy as np
from jax import lax
from jax.experimental import pallas as pl
from jax.experimental.pallas import tpu as pltpu
from jax.sharding import PartitionSpec as P

LAGS = 256

cell_width = 0.0125
layer_thick = 0.0125
bin_hertz = 0.5
period_bins = 500
slow_base = 0.3
chunk = 16
tile = 256
strip = 64


def parts_of(length):
    steps = np.arange(length, dtype=np.int64)
    phases = np.mod(steps[:, None] * steps[None, :], length).astype(np.float32)
    angles = phases * np.float32(2.0 * math.pi / length)
    scale = np.float32(1.0 / math.sqrt(length))
    return np.cos(angles) * scale, np.sin(angles) * scale


def real_transform(length):
    cosine, sine = (part.astype(jnp.bfloat16) for part in parts_of(length))
    half = length // 2
    basis = np.concatenate([cosine[: half + 1], sine[1:half]], axis=0)
    twice = np.full((length, 1), 2.0, np.float32)
    twice[0] = twice[half] = 1.0
    return (basis.astype(np.float32) * twice).astype(jnp.bfloat16), basis.T


def sin_cos(half_angle):
    square = half_angle * half_angle
    sine = half_angle + half_angle * square * (
        -1.6666656999673e-1
        + square * (8.3330149027548e-3 + square * (-1.9806441580e-4 + square * 2.5996687760e-6))
    )
    cosine = 1.0 + square * (
        -4.9999999543840e-1
        + square * (
            4.1666640465459e-2
            + square * (-1.3888399836750e-3 + square * (2.4761687147e-5 + square * -2.6073429763e-7))
        )
    )
    twice = sine + sine
    return -(twice * cosine), twice * sine - 1.0


def window_kernel(
    devices, bins, gaps, slab_map, corner, slab_in, source_in, table_y_in, receiver_in,
    table_f_in, table_i_in, bracket_in, table_z_in,
    received, weights,
    slab, source, table_y, receiver, table_f, table_i, bracket, table_z,
    half, spectrum, squares, edge, phases, shifted, returned, refocused, fields, cross,
    wide, windows, pair, part, parts, traded, total, slow, phase_rows,
    load_sems, pair_sems, scatter_sems, gather_sems, piece_sems, cross_sems,
):
    depths, rows_x, cols_y = bracket.shape
    slab_count, rows_all, cols_all = slab.shape
    chips = devices // 2
    me = lax.axis_index("freq")
    grp = lax.axis_index("grp")
    core = lax.rem(me, 2)
    chip = me // 2
    other = 1 - core
    share_rows = rows_x // devices
    signs = (1.0, -1.0)
    middle = rows_x // 2
    tiles = rows_x // tile
    group = max(share_rows, chunk)
    groups = tile // group
    angular = bins[me].astype(jnp.float32) * (2.0 * math.pi * bin_hertz)
    references = []
    for d in range(depths):
        first = gaps[d, 0]
        second = first + gaps[d, 1]
        third = second + gaps[d, 2]
        references.append((slow_base + first, slow_base + second, slow_base + third))

    loads = [
        pltpu.make_async_copy(far, near, load_sems.at[place])
        for place, (far, near) in enumerate((
            (slab_in, slab), (source_in, source), (table_y_in, table_y), (receiver_in, receiver),
            (table_f_in, table_f), (bracket_in, bracket), (table_i_in, table_i), (table_z_in, table_z),
        ))
    ]

    def lanes(which, side):
        return pl.ds((2 * which + side) * cols_y, cols_y)

    def remote(source_ref, target_ref, sems, place):
        return pltpu.make_async_remote_copy(
            src_ref=source_ref, dst_ref=target_ref, send_sem=sems[0], recv_sem=sems[1],
            device_id=(grp, place), device_id_type=pl.DeviceIdType.MESH,
        )

    levels = chips.bit_length() - 1
    pieced = share_rows >= chunk

    def mate(mask):
        place = 0 * chip
        for level in range(levels):
            flipped = lax.rem(chip // 2**level + mask // 2**level, 2)
            place = place + flipped * 2**level
        return place

    def swap_first(d):
        return remote(
            windows.at[d, other], pair.at[d], (pair_sems.at[d, 0], pair_sems.at[d, 1]),
            chip * 2 + other,
        )

    def scatter(d, mask):
        return remote(
            part.at[d, mate(mask)], parts.at[d, mask],
            (scatter_sems.at[d, 0, mask], scatter_sems.at[d, 1, mask]), mate(mask) * 2 + core,
        )

    def gather(d, mask):
        return remote(
            total.at[d], slow.at[d, core, chip],
            (gather_sems.at[d, 0, mask], gather_sems.at[d, 1, mask]), mate(mask) * 2 + core,
        )

    def swap_piece(d, mask):
        piece = slow.at[d, core, mate(mask)]
        return remote(
            piece, piece, (piece_sems.at[0, mask], piece_sems.at[1, mask]), chip * 2 + other
        )

    def swap_last(d):
        return remote(
            slow.at[d, core], slow.at[d, core], (pair_sems.at[d, 2], pair_sems.at[d, 3]),
            chip * 2 + other,
        )

    def send_cross(d, hop):
        to = lax.rem(me + hop, devices)
        return remote(
            cross.at[d, to], received.at[d, me],
            (cross_sems.at[d, 0, hop], cross_sems.at[d, 1, hop]), to,
        )

    sides = chips // 2
    low = lax.rem(chip, sides)
    pairs = pl.ds(2 * low, 2)
    near_start = chip - low

    def near_mate(mask):
        return lax.rem(mate(mask), sides)

    def near_scatter(d, mask):
        return remote(
            part.at[d, pl.ds(2 * near_mate(mask), 2)], parts.at[d, pl.ds(2 * mask, 2)],
            (scatter_sems.at[d, 0, mask], scatter_sems.at[d, 1, mask]),
            (near_start + near_mate(mask)) * 2 + core,
        )

    def trade(d):
        return remote(
            parts.at[d, pl.ds(0, 2)], traded.at[d],
            (scatter_sems.at[d, 0, 0], scatter_sems.at[d, 1, 0]),
            (sides - near_start + low) * 2 + core,
        )

    def near_gather(d, mask):
        return remote(
            slow.at[d, core, pairs], slow.at[d, core, pairs],
            (gather_sems.at[d, 0, mask], gather_sems.at[d, 1, mask]),
            (near_start + near_mate(mask)) * 2 + core,
        )

    def begin_near_scatter(d):
        swap_first(d).wait()
        part[d] = windows[d, core] + pair[d]

        @pl.loop(1, sides)
        def _(step):
            near_scatter(d, sides - step).start()

    def begin_trade(d):
        @pl.loop(1, sides)
        def _(mask):
            near_scatter(d, mask).wait()

        summed = part[d, pairs]
        for mask in range(1, sides):
            summed = summed + parts[d, pl.ds(2 * mask, 2)]
        parts[d, pl.ds(0, 2)] = summed
        trade(d).start()

    def begin_near_gather(d):
        trade(d).wait()
        slow[d, core, pairs] = parts[d, pl.ds(0, 2)] + traded[d]

        @pl.loop(1, sides)
        def _(step):
            near_gather(d, sides - step).start()

    def begin_near_last(d):
        @pl.loop(1, sides)
        def _(mask):
            near_gather(d, mask).wait()

        swap_last(d).start()

    def begin_scatter(d):
        swap_first(d).wait()
        part[d] = windows[d, core] + pair[d]

        @pl.loop(1, chips)
        def _(step):
            scatter(d, chips - step).start()

    def begin_gather(d):
        @pl.loop(1, chips)
        def _(hop):
            scatter(d, hop).wait()

        summed = part[d, chip]
        for hop in range(1, chips):
            summed = summed + parts[d, hop]
        total[d] = summed
        slow[d, core, chip] = summed

        @pl.loop(1, chips)
        def _(step):
            gather(d, chips - step).start()

    def begin_last(d):
        @pl.loop(1, chips)
        def _(hop):
            gather(d, hop).wait()

        swap_last(d).start()

    barrier = pltpu.get_barrier_semaphore()

    @pl.loop(1, devices)
    def _(hop):
        pl.semaphore_signal(
            barrier, inc=1, device_id=(grp, lax.rem(me + hop, devices)),
            device_id_type=pl.DeviceIdType.MESH,
        )

    loads[0].start()

    def one_hot(sizes, offset):
        ahead = lax.broadcasted_iota(jnp.int32, sizes, 0) - lax.broadcasted_iota(
            jnp.int32, sizes, 1
        )
        return jnp.where(ahead == offset, 1.0, 0.0).astype(jnp.bfloat16)

    def cut_slab(which):
        pick = one_hot((cols_all, cols_y), corner[1])
        for start in range(0, rows_all, tile):
            size = min(tile, rows_all - start)
            wide[pl.ds(start, size), :] = jnp.dot(
                slab[which, pl.ds(start, size), :], pick, preferred_element_type=jnp.float32
            ).astype(jnp.bfloat16)

    def put_windows(steps):
        kept = []
        for d in steps:
            apart = jnp.abs(lax.div(slab_map[d], slab_count) - me)
            kept.append((1 - jnp.minimum(apart, 1)).astype(jnp.float32))
        reach = tile + rows_all - rows_x
        pick = one_hot((tile, reach), -corner[0])
        for start in range(0, rows_x, tile):
            values = jnp.dot(
                pick, wide[pl.ds(start, reach), :], preferred_element_type=jnp.float32
            )
            for d, keep in zip(steps, kept):
                held = (values * keep).astype(jnp.bfloat16)
                for piece in range(tile // share_rows):
                    block = start // share_rows + piece
                    windows[d, block // chips, block % chips] = held[
                        piece * share_rows : (piece + 1) * share_rows
                    ]

    half_y = cols_y // 2
    unit = 0.5 * layer_thick
    step_x = unit * 2.0 * math.pi / (rows_x * cell_width)
    step_y = unit * 2.0 * math.pi / (cols_y * cell_width)
    strips = middle // strip + 1
    counted = lax.broadcasted_iota(jnp.int32, (strip, half_y), 0)
    columns = lax.broadcasted_iota(jnp.int32, (strip, half_y), 1)

    def strip_rows(number):
        return pl.ds(pl.multiple_of(number * strip, strip), strip)

    def reach_of(d, ref):
        return angular * references[d][ref] * unit

    def turn_of(reach, square):
        radicand = reach * reach - square
        size = jnp.abs(radicand)
        depth = size * lax.rsqrt(jnp.maximum(size, 1e-30))
        moving = radicand > 0.0
        fading = jnp.exp(jnp.where(moving, 0.0, -2.0 * depth))
        sine, cosine = sin_cos(jnp.where(moving, depth, 0.0) + (0.5 * math.pi - reach))
        return fading * cosine, fading * sine

    def fill_tables():
        reach = jnp.zeros((strip, half_y), jnp.float32)
        for d in range(depths):
            for ref in range(3):
                reach = jnp.where(columns == 3 * d + ref, reach_of(d, ref), reach)

        @pl.loop(0, strips)
        def _(number):
            rows = strip_rows(number)
            index = counted + number * strip
            magnitude = jnp.where(index <= middle, index, index - middle)
            wave_x = magnitude.astype(jnp.float32) * step_x
            wave_y = columns.astype(jnp.float32) * step_y
            squares[rows, :] = wave_x * wave_x + wave_y * wave_y
            real, imag = turn_of(reach, wave_x * wave_x + (half_y * step_y) ** 2)
            edge[0, rows, :] = real
            edge[1, rows, :] = imag

    fill_tables()
    loads[0].wait()
    for load in loads[1:]:
        load.start()
    if slab_count == 1:
        cut_slab(0)
        put_windows(range(depths))
    else:
        for d in range(depths):
            cut_slab(lax.rem(slab_map[d], slab_count))
            put_windows((d,))
    pl.semaphore_wait(barrier, devices - 1)
    for d in range(depths):
        swap_first(d).start()

    def phase_table(d, ref):
        @pl.loop(0, strips)
        def _(number):
            rows = strip_rows(number)
            for part, values in enumerate(turn_of(reach_of(d, ref), squares[rows, :])):
                phases[d, ref, part, rows, :half_y] = values
                last = pltpu.roll(edge[part, rows, :], (half_y - 3 * d - ref) % half_y, 1)
                phases[d, ref, part, rows, half_y:] = jnp.where(columns == 0, last, values)

    def apply_phase(d, ref, start, place):
        rows = pl.ds(start, chunk)
        cosine = phases[d, ref, 0, pl.ds(place, chunk), :]
        sine = phases[d, ref, 1, pl.ds(place, chunk), :]
        for which in range(2):
            turned = signs[which] * sine
            real = spectrum[rows, lanes(which, 0)]
            imag = spectrum[rows, lanes(which, 1)]
            shifted[ref, rows, lanes(which, 0)] = (cosine * real - turned * imag).astype(
                jnp.bfloat16
            )
            shifted[ref, rows, lanes(which, 1)] = (cosine * imag + turned * real).astype(
                jnp.bfloat16
            )

    def shift_chunk(d, ref, start):
        apply_phase(d, ref, start, start)
        apply_phase(d, ref, pl.multiple_of(middle + start, chunk), start)

    def shift_edge(d, ref):
        apply_phase(d, ref, 0, 0)
        apply_phase(d, ref, middle, middle)

    def shift(d, ref):
        @pl.loop(1, middle // chunk)
        def _(number):
            shift_chunk(d, ref, pl.multiple_of(number * chunk, chunk))

        shift_edge(d, ref)

    def slow_rows(d, start):
        if share_rows >= chunk:
            block = start // share_rows
            inner = pl.multiple_of(lax.rem(start, share_rows), chunk)
            return slow[d, block // chips, lax.rem(block, chips), pl.ds(inner, chunk), :].astype(
                jnp.float32
            )
        pieces = []
        for piece in range(chunk // share_rows):
            block = start // share_rows + piece
            pieces.append(
                slow[d, block // chips, lax.rem(block, chips)].astype(jnp.float32)
            )
        return jnp.concatenate(pieces, axis=0)

    def store_cross(d, start, which, values):
        if share_rows >= chunk:
            inner = pl.multiple_of(lax.rem(start, share_rows), chunk)
            cross[d, start // share_rows, which, pl.ds(inner, chunk), :] = values.astype(
                jnp.bfloat16
            )
        else:
            for piece in range(chunk // share_rows):
                cross[d, start // share_rows + piece, which] = values[
                    piece * share_rows : (piece + 1) * share_rows
                ].astype(jnp.bfloat16)

    def mix(d, turn, inside, start):
        local = pl.ds(inside, chunk)
        rows = pl.ds(start, chunk)
        slowness = slow_rows(d, start)
        lower = bracket[d, rows, :] == 0
        slow_low = jnp.where(lower, references[d][0], references[d][1])
        slow_scale = jnp.where(
            lower, 1.0 / (references[d][1] - references[d][0]),
            1.0 / (references[d][2] - references[d][1]),
        )
        weight = jnp.clip((slowness - slow_low) * slow_scale, 0.0, 1.0)
        sine, cosine = sin_cos((angular * unit) * slowness - 0.5 * math.pi)
        rounded = []
        for which in range(2):
            mixed = []
            for side in range(2):
                first = refocused[turn, 0, local, lanes(which, side)]
                second = refocused[turn, 1, local, lanes(which, side)]
                third = refocused[turn, 2, local, lanes(which, side)]
                low = jnp.where(lower, first, second)
                high = jnp.where(lower, second, third)
                mixed.append((1.0 - weight) * low + weight * high)
            turned = signs[which] * sine
            real = (cosine * mixed[0] - turned * mixed[1]).astype(jnp.bfloat16)
            imag = (turned * mixed[0] + cosine * mixed[1]).astype(jnp.bfloat16)
            if d < depths - 1:
                fields[which, 0, rows, :] = real
                fields[which, 1, rows, :] = imag
            rounded.append((real.astype(jnp.float32), imag.astype(jnp.float32)))
        (sr, si), (rr, ri) = rounded
        store_cross(d, start, 0, sr * rr + si * ri)
        store_cross(d, start, 1, sr * ri - si * rr)

    def forward_y(which, field):
        for side in range(2):
            for start in range(0, rows_x, tile):
                rows = pl.ds(start, tile)
                half[rows, lanes(which, side)] = jnp.dot(
                    field[side, rows, :], table_y[...], preferred_element_type=jnp.float32
                ).astype(jnp.bfloat16)

    def forward_x():
        @pl.loop(0, rows_x // tile)
        def _(number):
            rows = pl.ds(pl.multiple_of(number * tile, tile), tile)
            spectrum[rows, :] = jnp.dot(
                table_f[rows, :], half[...], preferred_element_type=jnp.float32
            )

    def inverse(turn, ref, tile_start):
        returned[...] = jnp.dot(
            table_i[pl.ds(tile_start, tile), :], shifted[ref], preferred_element_type=jnp.float32
        ).astype(jnp.bfloat16)
        for which in range(2):
            for side in range(2):
                refocused[turn, ref, :, lanes(which, side)] = jnp.dot(
                    returned[:, lanes(which, side)], table_z[...],
                    preferred_element_type=jnp.float32,
                )

    def send_group(d, tile_start, index):
        for each in range(group // share_rows):
            to = (tile_start + index * group) // share_rows + each
            hop = lax.rem(to - me + devices, devices)

            @pl.when(hop != 0)
            def _():
                send_cross(d, hop).start()

    own_tile = me * share_rows // tile
    own_group = lax.rem(me * share_rows, tile) // group

    def turn_index(number):
        return lax.rem(own_group + 1 + number, groups)

    def mix_tile(d, turn, tile_start):
        @pl.loop(0, groups)
        def _(number):
            for each in range(group // chunk):
                inside = pl.multiple_of(turn_index(number) * group + each * chunk, chunk)
                mix(d, turn, inside, pl.multiple_of(tile_start + inside, chunk))

            @pl.when(number > 0)
            def _():
                send_group(d, tile_start, turn_index(number - 1))

        send_group(d, tile_start, turn_index(groups - 1))

    def lag_table():
        lag_count = weights.shape[1]
        offsets = (
            lax.broadcasted_iota(jnp.int32, (1, lag_count), 1) - lag_count // 2
        ).astype(jnp.float32)

        @pl.loop(0, devices)
        def _(slot):
            turned = bins[slot].astype(jnp.float32) * offsets
            phase_rows[pl.ds(2 * slot, 1), :] = turned
            phase_rows[pl.ds(2 * slot + 1, 1), :] = turned

        counts = phase_rows[...]
        wraps = jnp.floor((counts + 0.5) * (1.0 / period_bins))
        sine, cosine = sin_cos(
            (counts - wraps * period_bins) * (math.pi / period_bins) - 0.5 * math.pi
        )
        odd = lax.broadcasted_iota(jnp.int32, counts.shape, 0) % 2 == 1
        weights[...] = jnp.where(odd, -sine, cosine).astype(jnp.bfloat16)

    def mix_piece(d, half, mask):
        block = mate(mask)
        turn = (block * share_rows) // tile
        turn = turn + jnp.where(half == core, 0, tiles // 2)
        inside = lax.rem(block * share_rows, tile)
        to = half * chips + block
        for each in range(share_rows // chunk):
            mix(
                d, turn, pl.multiple_of(inside + each * chunk, chunk),
                pl.multiple_of(to * share_rows + each * chunk, chunk),
            )
        hop = lax.rem(to - me + devices, devices)

        @pl.when(hop != 0)
        def _():
            send_cross(d, hop).start()

    def mix_pieces(d, first, end):
        @pl.loop(first, end)
        def _(mask):
            gather(d, mask).wait()
            swap_piece(d, mask).start()
            mix_piece(d, core, mask)
            swap_piece(d, mask - 1).wait()
            mix_piece(d, other, mask - 1)

    def mix_last_piece(d):
        swap_piece(d, chips - 1).wait()
        mix_piece(d, other, chips - 1)

    first_tiles = (core * (tiles // 2),) + (own_tile + 1,) * (depths - 1)
    for d in range(depths):
        tile_starts = [
            pl.multiple_of(lax.rem(first_tiles[d] + turn, tiles) * tile, tile)
            for turn in range(tiles)
        ]
        if d == 0:
            begin_scatter(0)
            loads[1].wait()
            loads[2].wait()
            forward_y(0, source)
            for later in range(1, depths):
                begin_near_scatter(later)
            loads[3].wait()
            forward_y(1, receiver)
            loads[4].wait()
            forward_x()
            for ref in range(3):
                phase_table(0, ref)
                shift(0, ref)
            loads[6].wait()
            loads[7].wait()
            for turn in range(tiles // 2):
                for ref in range(3):
                    inverse(turn, ref, tile_starts[turn])
            for later in range(1, depths):
                begin_trade(later)
            begin_gather(0)
            loads[5].wait()
            if pieced:
                swap_piece(0, 0).start()
                mix_piece(0, core, 0)
            for turn in range(tiles // 2, tiles):
                for ref in range(3):
                    inverse(turn, ref, tile_starts[turn])
            for later in range(1, depths):
                for ref in range(3):
                    phase_table(later, ref)
            if pieced:
                mix_pieces(0, 1, sides)
            for later in range(1, depths):
                begin_near_gather(later)
            if pieced:
                mix_pieces(0, sides, chips)
                mix_last_piece(0)
            else:
                begin_last(0)
                for turn in range(tiles // 2):
                    mix_tile(0, turn, tile_starts[turn])
                swap_last(0).wait()
                for turn in range(tiles // 2, tiles):
                    mix_tile(0, turn, tile_starts[turn])
        else:
            forward_y(0, fields.at[0])
            forward_y(1, fields.at[1])
            forward_x()
            begin_near_last(d)
            for ref in range(3):
                shift(d, ref)
            for turn in range(tiles):
                for ref in range(3):
                    inverse(turn, ref, tile_starts[turn])
                if turn == 0:
                    swap_last(d).wait()
                mix_tile(d, turn, tile_starts[turn])
        received[d, me] = cross[d, me]
    lag_table()
    for d in range(depths):
        @pl.loop(1, devices)
        def _(hop):
            send_cross(d, hop).wait()


def cross_spectra(
    devices, bins, gaps, slab_map, corner, source, receiver, slabs, bracket
):
    depths, rows_x, cols_y = bracket.shape
    slab_count, rows_all, cols_all = slabs.shape
    chips = devices // 2
    share_rows = rows_x // devices
    table_f, table_i = real_transform(rows_x)
    table_y, table_z = (table.T for table in real_transform(cols_y))
    vmem = pl.BlockSpec(memory_space=pltpu.VMEM)
    flops = 8 * rows_x * (rows_x + cols_y) * 4 * cols_y * depths
    dma = pltpu.SemaphoreType.DMA
    held = (depths, chips, share_rows, cols_y)
    field = pltpu.VMEM((2, rows_x, cols_y), jnp.bfloat16)
    return pl.pallas_call(
        functools.partial(window_kernel, devices),
        out_shape=(
            jax.ShapeDtypeStruct((depths, devices, 2, share_rows, cols_y), jnp.bfloat16),
            jax.ShapeDtypeStruct((2 * devices, LAGS), jnp.bfloat16),
        ),
        in_specs=[pl.BlockSpec(memory_space=pltpu.SMEM)] * 4
        + [pl.BlockSpec(memory_space=pltpu.HBM)] * 8,
        out_specs=(vmem, vmem),
        scratch_shapes=[
            pltpu.VMEM(slabs.shape, jnp.bfloat16),
            field,
            pltpu.VMEM(table_y.shape, jnp.bfloat16),
            field,
            pltpu.VMEM(table_f.shape, jnp.bfloat16),
            pltpu.VMEM(table_i.shape, jnp.bfloat16),
            pltpu.VMEM(bracket.shape, jnp.int32),
            pltpu.VMEM(table_z.shape, jnp.bfloat16),
            pltpu.VMEM((rows_x, 4 * cols_y), jnp.bfloat16),
            pltpu.VMEM((rows_x, 4 * cols_y), jnp.float32),
            pltpu.VMEM((rows_x // 2 + strip, cols_y // 2), jnp.float32),
            pltpu.VMEM((2, rows_x // 2 + strip, cols_y // 2), jnp.float32),
            pltpu.VMEM((depths, 3, 2, rows_x // 2 + strip, cols_y), jnp.float32),
            pltpu.VMEM((3, rows_x, 4 * cols_y), jnp.bfloat16),
            pltpu.VMEM((tile, 4 * cols_y), jnp.bfloat16),
            pltpu.VMEM((rows_x // tile, 3, tile, 4 * cols_y), jnp.float32),
            pltpu.VMEM((2, 2, rows_x, cols_y), jnp.bfloat16),
            pltpu.VMEM((depths, devices, 2, share_rows, cols_y), jnp.bfloat16),
            pltpu.VMEM((rows_all, cols_y), jnp.bfloat16),
            pltpu.VMEM((depths, 2, chips, share_rows, cols_y), jnp.bfloat16),
            pltpu.VMEM(held, jnp.bfloat16),
            pltpu.VMEM(held, jnp.bfloat16),
            pltpu.VMEM(held, jnp.bfloat16),
            pltpu.VMEM((depths, 2, share_rows, cols_y), jnp.bfloat16),
            pltpu.VMEM((depths, share_rows, cols_y), jnp.bfloat16),
            pltpu.VMEM((depths, 2, chips, share_rows, cols_y), jnp.bfloat16),
            pltpu.VMEM((2 * devices, LAGS), jnp.float32),
            dma((8,)),
            dma((depths, 4)),
            dma((depths, 2, chips)),
            dma((depths, 2, chips)),
            dma((2, chips)),
            dma((depths, 2, devices)),
        ],
        cost_estimate=pl.CostEstimate(
            flops=flops, bytes_accessed=8 * 1024 * 1024, transcendentals=0
        ),
        compiler_params=pltpu.CompilerParams(
            collective_id=0, has_side_effects=True, vmem_limit_bytes=44 * 1024 * 1024
        ),
    )(
        *[
            pltpu.with_memory_space_constraint(value, pltpu.HBM)
            for value in (
                bins, gaps, slab_map, corner, slabs, source, jnp.asarray(table_y), receiver,
                jnp.asarray(table_f), jnp.asarray(table_i), bracket, jnp.asarray(table_z),
            )
        ]
    )


def image_kernel(scale, crosses, weights, out, held, sems):
    depths, slots, _, rows, cols_y = crosses.shape
    step = min(16, rows)
    part = min(4, step)
    count = depths * (rows // step)

    def block(number, place):
        d = number // (rows // step)
        start = lax.rem(number, rows // step) * step + place * part
        return d, pl.ds(start, part)

    def write(number, place):
        d, local = block(number, place)
        return pltpu.make_async_copy(
            held.at[d, local], out.at[d, local], sems.at[number, place]
        )

    @pl.loop(0, count)
    def _(number):
        d = number // (rows // step)
        start = pl.multiple_of(lax.rem(number, rows // step) * step, step)
        values = crosses[d, :, :, pl.ds(start, step), :]
        values = values.astype(jnp.float32).reshape(2 * slots, step, cols_y)
        values = jnp.swapaxes(values, 0, 1).astype(jnp.bfloat16)
        for row in range(step):
            held[d, start + row] = scale * lax.dot_general(
                values[row], weights[...], (((0,), (0,)), ((), ())),
                preferred_element_type=jnp.float32,
            )
            if row % part == part - 1:
                write(number, row // part).start()

    @pl.loop(0, count)
    def _(number):
        for place in range(step // part):
            write(number, place).wait()


def lag_image(crosses, weights):
    depths, slots, _, rows, cols_y = crosses.shape
    lag_count = weights.shape[1]
    step = min(16, rows)
    whole = pl.BlockSpec(memory_space=pltpu.VMEM)
    image = (depths, rows, cols_y, lag_count)
    return pl.pallas_call(
        functools.partial(image_kernel, slots ** (-0.5)),
        out_shape=jax.ShapeDtypeStruct(image, jnp.float32),
        in_specs=[whole, whole],
        out_specs=pl.BlockSpec(memory_space=pltpu.HBM),
        scratch_shapes=[
            pltpu.VMEM(image, jnp.float32),
            pltpu.SemaphoreType.DMA((depths * (rows // step), step // min(4, step))),
        ],
        compiler_params=pltpu.CompilerParams(vmem_limit_bytes=32 * 1024 * 1024),
    )(crosses, weights)


def shards(
    devices,
    source_field,
    receiver_field,
    slowness_slabs,
    slab_map,
    reference_gaps,
    reference_index,
    frequency_bins,
    shot_corner,
):
    crosses, weights = cross_spectra(
        devices, frequency_bins, reference_gaps, slab_map, shot_corner, source_field[:, 0],
        receiver_field[:, 0], slowness_slabs, reference_index,
    )
    return lag_image(crosses, weights)


def solution(mesh):
    placed = (
        P("grp", "freq", None, None),
        P("grp", "freq", None, None),
        P(("grp", "freq"), None, None),
        P("grp"),
        P("grp", None),
        P("grp", None, None),
        P(),
        P("grp"),
    )
    return jax.shard_map(
        functools.partial(shards, mesh.shape["freq"]),
        mesh=mesh,
        in_specs=placed,
        out_specs=P("grp", "freq", None, None),
        check_vma=False,
    )
```

```python
import functools
import math

import jax
import jax.numpy as jnp
import numpy as np
from jax import lax
from jax.experimental import pallas as pl
from jax.experimental.pallas import tpu as pltpu
from jax.sharding import PartitionSpec as P

LAGS = 256

cell_width = 0.0125
layer_thick = 0.0125
bin_hertz = 0.5
period_bins = 500
slow_base = 0.3
chunk = 16
tile = 256
strip = 64


def parts_of(length):
    steps = np.arange(length, dtype=np.int64)
    phases = np.mod(steps[:, None] * steps[None, :], length).astype(np.float32)
    angles = phases * np.float32(2.0 * math.pi / length)
    scale = np.float32(1.0 / math.sqrt(length))
    return np.cos(angles) * scale, np.sin(angles) * scale


def real_transform(length):
    cosine, sine = (part.astype(jnp.bfloat16) for part in parts_of(length))
    half = length // 2
    basis = np.concatenate([cosine[: half + 1], sine[1:half]], axis=0)
    twice = np.full((length, 1), 2.0, np.float32)
    twice[0] = twice[half] = 1.0
    return (basis.astype(np.float32) * twice).astype(jnp.bfloat16), basis.T


def sin_cos(half_angle):
    square = half_angle * half_angle
    sine = half_angle + half_angle * square * (
        -1.6666656999673e-1
        + square * (8.3330149027548e-3 + square * (-1.9806441580e-4 + square * 2.5996687760e-6))
    )
    cosine = 1.0 + square * (
        -4.9999999543840e-1
        + square * (
            4.1666640465459e-2
            + square * (-1.3888399836750e-3 + square * (2.4761687147e-5 + square * -2.6073429763e-7))
        )
    )
    twice = sine + sine
    return -(twice * cosine), twice * sine - 1.0


def window_kernel(
    devices, bins, gaps, slab_map, corner, slab_in, source_in, table_y_in, receiver_in,
    table_f_in, table_i_in, bracket_in, table_z_in,
    received, weights,
    slab, source, table_y, receiver, table_f, table_i, bracket, table_z,
    half, spectrum, squares, edge, phases, shifted, returned, refocused, fields, cross,
    wide, windows, pair, part, parts, traded, total, slow, phase_rows,
    load_sems, pair_sems, scatter_sems, gather_sems, piece_sems, cross_sems,
):
    depths, rows_x, cols_y = bracket.shape
    slab_count, rows_all, cols_all = slab.shape
    chips = devices // 2
    me = lax.axis_index("freq")
    grp = lax.axis_index("grp")
    core = lax.rem(me, 2)
    chip = me // 2
    other = 1 - core
    share_rows = rows_x // devices
    signs = (1.0, -1.0)
    middle = rows_x // 2
    tiles = rows_x // tile
    group = max(share_rows, chunk)
    groups = tile // group
    angular = bins[me].astype(jnp.float32) * (2.0 * math.pi * bin_hertz)
    references = []
    for d in range(depths):
        first = gaps[d, 0]
        second = first + gaps[d, 1]
        third = second + gaps[d, 2]
        references.append((slow_base + first, slow_base + second, slow_base + third))

    loads = [
        pltpu.make_async_copy(far, near, load_sems.at[place])
        for place, (far, near) in enumerate((
            (slab_in, slab), (source_in, source), (table_y_in, table_y), (receiver_in, receiver),
            (table_f_in, table_f), (bracket_in, bracket), (table_i_in, table_i), (table_z_in, table_z),
        ))
    ]

    def lanes(which, side):
        return pl.ds((2 * which + side) * cols_y, cols_y)

    def remote(source_ref, target_ref, sems, place):
        return pltpu.make_async_remote_copy(
            src_ref=source_ref, dst_ref=target_ref, send_sem=sems[0], recv_sem=sems[1],
            device_id=(grp, place), device_id_type=pl.DeviceIdType.MESH,
        )

    levels = chips.bit_length() - 1
    pieced = share_rows >= chunk

    def mate(mask):
        place = 0 * chip
        for level in range(levels):
            flipped = lax.rem(chip // 2**level + mask // 2**level, 2)
            place = place + flipped * 2**level
        return place

    def swap_first(d):
        return remote(
            windows.at[d, other], pair.at[d], (pair_sems.at[d, 0], pair_sems.at[d, 1]),
            chip * 2 + other,
        )

    def scatter(d, mask):
        return remote(
            part.at[d, mate(mask)], parts.at[d, mask],
            (scatter_sems.at[d, 0, mask], scatter_sems.at[d, 1, mask]), mate(mask) * 2 + core,
        )

    def gather(d, mask):
        return remote(
            total.at[d], slow.at[d, core, chip],
            (gather_sems.at[d, 0, mask], gather_sems.at[d, 1, mask]), mate(mask) * 2 + core,
        )

    def swap_piece(d, mask):
        piece = slow.at[d, core, mate(mask)]
        return remote(
            piece, piece, (piece_sems.at[0, mask], piece_sems.at[1, mask]), chip * 2 + other
        )

    def swap_last(d):
        return remote(
            slow.at[d, core], slow.at[d, core], (pair_sems.at[d, 2], pair_sems.at[d, 3]),
            chip * 2 + other,
        )

    def send_cross(d, hop):
        to = lax.rem(me + hop, devices)
        return remote(
            cross.at[d, to], received.at[d, me],
            (cross_sems.at[d, 0, hop], cross_sems.at[d, 1, hop]), to,
        )

    sides = chips // 2
    low = lax.rem(chip, sides)
    pairs = pl.ds(2 * low, 2)
    near_start = chip - low

    def near_mate(mask):
        return lax.rem(mate(mask), sides)

    def near_scatter(d, mask):
        return remote(
            part.at[d, pl.ds(2 * near_mate(mask), 2)], parts.at[d, pl.ds(2 * mask, 2)],
            (scatter_sems.at[d, 0, mask], scatter_sems.at[d, 1, mask]),
            (near_start + near_mate(mask)) * 2 + core,
        )

    def trade(d):
        return remote(
            parts.at[d, pl.ds(0, 2)], traded.at[d],
            (scatter_sems.at[d, 0, 0], scatter_sems.at[d, 1, 0]),
            (sides - near_start + low) * 2 + core,
        )

    def near_gather(d, mask):
        return remote(
            slow.at[d, core, pairs], slow.at[d, core, pairs],
            (gather_sems.at[d, 0, mask], gather_sems.at[d, 1, mask]),
            (near_start + near_mate(mask)) * 2 + core,
        )

    def begin_near_scatter(d):
        swap_first(d).wait()
        part[d] = windows[d, core] + pair[d]

        @pl.loop(1, sides)
        def _(step):
            near_scatter(d, sides - step).start()

    def begin_trade(d):
        @pl.loop(1, sides)
        def _(mask):
            near_scatter(d, mask).wait()

        summed = part[d, pairs]
        for mask in range(1, sides):
            summed = summed + parts[d, pl.ds(2 * mask, 2)]
        parts[d, pl.ds(0, 2)] = summed
        trade(d).start()

    def begin_near_gather(d):
        trade(d).wait()
        slow[d, core, pairs] = parts[d, pl.ds(0, 2)] + traded[d]

        @pl.loop(1, sides)
        def _(step):
            near_gather(d, sides - step).start()

    def begin_near_last(d):
        @pl.loop(1, sides)
        def _(mask):
            near_gather(d, mask).wait()

        swap_last(d).start()

    def begin_scatter(d):
        swap_first(d).wait()
        part[d] = windows[d, core] + pair[d]

        @pl.loop(1, chips)
        def _(step):
            scatter(d, chips - step).start()

    def begin_gather(d):
        @pl.loop(1, chips)
        def _(hop):
            scatter(d, hop).wait()

        summed = part[d, chip]
        for hop in range(1, chips):
            summed = summed + parts[d, hop]
        total[d] = summed
        slow[d, core, chip] = summed

        @pl.loop(1, chips)
        def _(step):
            gather(d, chips - step).start()

    def begin_last(d):
        @pl.loop(1, chips)
        def _(hop):
            gather(d, hop).wait()

        swap_last(d).start()

    barrier = pltpu.get_barrier_semaphore()

    @pl.loop(1, devices)
    def _(hop):
        pl.semaphore_signal(
            barrier, inc=1, device_id=(grp, lax.rem(me + hop, devices)),
            device_id_type=pl.DeviceIdType.MESH,
        )

    loads[0].start()

    def one_hot(sizes, offset):
        ahead = lax.broadcasted_iota(jnp.int32, sizes, 0) - lax.broadcasted_iota(
            jnp.int32, sizes, 1
        )
        return jnp.where(ahead == offset, 1.0, 0.0).astype(jnp.bfloat16)

    def cut_slab(which):
        pick = one_hot((cols_all, cols_y), corner[1])
        for start in range(0, rows_all, tile):
            size = min(tile, rows_all - start)
            wide[pl.ds(start, size), :] = jnp.dot(
                slab[which, pl.ds(start, size), :], pick, preferred_element_type=jnp.float32
            ).astype(jnp.bfloat16)

    def put_windows(steps):
        kept = []
        for d in steps:
            apart = jnp.abs(lax.div(slab_map[d], slab_count) - me)
            kept.append((1 - jnp.minimum(apart, 1)).astype(jnp.float32))
        reach = tile + rows_all - rows_x
        pick = one_hot((tile, reach), -corner[0])
        for start in range(0, rows_x, tile):
            values = jnp.dot(
                pick, wide[pl.ds(start, reach), :], preferred_element_type=jnp.float32
            )
            for d, keep in zip(steps, kept):
                held = (values * keep).astype(jnp.bfloat16)
                for piece in range(tile // share_rows):
                    block = start // share_rows + piece
                    windows[d, block // chips, block % chips] = held[
                        piece * share_rows : (piece + 1) * share_rows
                    ]

    loads[0].wait()
    for load in loads[1:]:
        load.start()
    if slab_count == 1:
        cut_slab(0)
        put_windows(range(depths))
    else:
        for d in range(depths):
            cut_slab(lax.rem(slab_map[d], slab_count))
            put_windows((d,))
    pl.semaphore_wait(barrier, devices - 1)
    for d in range(depths):
        swap_first(d).start()

    half_y = cols_y // 2
    unit = 0.5 * layer_thick
    step_x = unit * 2.0 * math.pi / (rows_x * cell_width)
    step_y = unit * 2.0 * math.pi / (cols_y * cell_width)
    strips = middle // strip + 1
    counted = lax.broadcasted_iota(jnp.int32, (strip, half_y), 0)
    columns = lax.broadcasted_iota(jnp.int32, (strip, half_y), 1)

    def strip_rows(number):
        return pl.ds(pl.multiple_of(number * strip, strip), strip)

    def reach_of(d, ref):
        return angular * references[d][ref] * unit

    def turn_of(reach, square):
        radicand = reach * reach - square
        size = jnp.abs(radicand)
        depth = size * lax.rsqrt(jnp.maximum(size, 1e-30))
        moving = radicand > 0.0
        fading = jnp.exp(jnp.where(moving, 0.0, -2.0 * depth))
        sine, cosine = sin_cos(jnp.where(moving, depth, 0.0) + (0.5 * math.pi - reach))
        return fading * cosine, fading * sine

    def fill_tables():
        reach = jnp.zeros((strip, half_y), jnp.float32)
        for d in range(depths):
            for ref in range(3):
                reach = jnp.where(columns == 3 * d + ref, reach_of(d, ref), reach)

        @pl.loop(0, strips)
        def _(number):
            rows = strip_rows(number)
            index = counted + number * strip
            magnitude = jnp.where(index <= middle, index, index - middle)
            wave_x = magnitude.astype(jnp.float32) * step_x
            wave_y = columns.astype(jnp.float32) * step_y
            squares[rows, :] = wave_x * wave_x + wave_y * wave_y
            real, imag = turn_of(reach, wave_x * wave_x + (half_y * step_y) ** 2)
            edge[0, rows, :] = real
            edge[1, rows, :] = imag

    def phase_table(d, ref):
        @pl.loop(0, strips)
        def _(number):
            rows = strip_rows(number)
            for part, values in enumerate(turn_of(reach_of(d, ref), squares[rows, :])):
                phases[d, ref, part, rows, :half_y] = values
                last = pltpu.roll(edge[part, rows, :], (half_y - 3 * d - ref) % half_y, 1)
                phases[d, ref, part, rows, half_y:] = jnp.where(columns == 0, last, values)

    def apply_phase(d, ref, start, place):
        rows = pl.ds(start, chunk)
        cosine = phases[d, ref, 0, pl.ds(place, chunk), :]
        sine = phases[d, ref, 1, pl.ds(place, chunk), :]
        for which in range(2):
            turned = signs[which] * sine
            real = spectrum[rows, lanes(which, 0)]
            imag = spectrum[rows, lanes(which, 1)]
            shifted[ref, rows, lanes(which, 0)] = (cosine * real - turned * imag).astype(
                jnp.bfloat16
            )
            shifted[ref, rows, lanes(which, 1)] = (cosine * imag + turned * real).astype(
                jnp.bfloat16
            )

    def shift_chunk(d, ref, start):
        apply_phase(d, ref, start, start)
        apply_phase(d, ref, pl.multiple_of(middle + start, chunk), start)

    def shift_edge(d, ref):
        apply_phase(d, ref, 0, 0)
        apply_phase(d, ref, middle, middle)

    def shift(d, ref):
        @pl.loop(1, middle // chunk)
        def _(number):
            shift_chunk(d, ref, pl.multiple_of(number * chunk, chunk))

        shift_edge(d, ref)

    def slow_rows(d, start):
        if share_rows >= chunk:
            block = start // share_rows
            inner = pl.multiple_of(lax.rem(start, share_rows), chunk)
            return slow[d, block // chips, lax.rem(block, chips), pl.ds(inner, chunk), :].astype(
                jnp.float32
            )
        pieces = []
        for piece in range(chunk // share_rows):
            block = start // share_rows + piece
            pieces.append(
                slow[d, block // chips, lax.rem(block, chips)].astype(jnp.float32)
            )
        return jnp.concatenate(pieces, axis=0)

    def store_cross(d, start, which, values):
        if share_rows >= chunk:
            inner = pl.multiple_of(lax.rem(start, share_rows), chunk)
            cross[d, start // share_rows, which, pl.ds(inner, chunk), :] = values.astype(
                jnp.bfloat16
            )
        else:
            for piece in range(chunk // share_rows):
                cross[d, start // share_rows + piece, which] = values[
                    piece * share_rows : (piece + 1) * share_rows
                ].astype(jnp.bfloat16)

    def mix(d, turn, inside, start):
        local = pl.ds(inside, chunk)
        rows = pl.ds(start, chunk)
        slowness = slow_rows(d, start)
        lower = bracket[d, rows, :] == 0
        slow_low = jnp.where(lower, references[d][0], references[d][1])
        slow_scale = jnp.where(
            lower, 1.0 / (references[d][1] - references[d][0]),
            1.0 / (references[d][2] - references[d][1]),
        )
        weight = jnp.clip((slowness - slow_low) * slow_scale, 0.0, 1.0)
        sine, cosine = sin_cos((angular * unit) * slowness - 0.5 * math.pi)
        rounded = []
        for which in range(2):
            mixed = []
            for side in range(2):
                first = refocused[turn, 0, local, lanes(which, side)]
                second = refocused[turn, 1, local, lanes(which, side)]
                third = refocused[turn, 2, local, lanes(which, side)]
                low = jnp.where(lower, first, second)
                high = jnp.where(lower, second, third)
                mixed.append((1.0 - weight) * low + weight * high)
            turned = signs[which] * sine
            real = (cosine * mixed[0] - turned * mixed[1]).astype(jnp.bfloat16)
            imag = (turned * mixed[0] + cosine * mixed[1]).astype(jnp.bfloat16)
            if d < depths - 1:
                fields[which, 0, rows, :] = real
                fields[which, 1, rows, :] = imag
            rounded.append((real.astype(jnp.float32), imag.astype(jnp.float32)))
        (sr, si), (rr, ri) = rounded
        store_cross(d, start, 0, sr * rr + si * ri)
        store_cross(d, start, 1, sr * ri - si * rr)

    def forward_y(which, field):
        for side in range(2):
            for start in range(0, rows_x, tile):
                rows = pl.ds(start, tile)
                half[rows, lanes(which, side)] = jnp.dot(
                    field[side, rows, :], table_y[...], preferred_element_type=jnp.float32
                ).astype(jnp.bfloat16)

    def forward_x():
        @pl.loop(0, rows_x // tile)
        def _(number):
            rows = pl.ds(pl.multiple_of(number * tile, tile), tile)
            spectrum[rows, :] = jnp.dot(
                table_f[rows, :], half[...], preferred_element_type=jnp.float32
            )

    def inverse(turn, ref, tile_start):
        returned[...] = jnp.dot(
            table_i[pl.ds(tile_start, tile), :], shifted[ref], preferred_element_type=jnp.float32
        ).astype(jnp.bfloat16)
        for which in range(2):
            for side in range(2):
                refocused[turn, ref, :, lanes(which, side)] = jnp.dot(
                    returned[:, lanes(which, side)], table_z[...],
                    preferred_element_type=jnp.float32,
                )

    def send_group(d, tile_start, index):
        for each in range(group // share_rows):
            to = (tile_start + index * group) // share_rows + each
            hop = lax.rem(to - me + devices, devices)

            @pl.when(hop != 0)
            def _():
                send_cross(d, hop).start()

    own_tile = me * share_rows // tile
    own_group = lax.rem(me * share_rows, tile) // group

    def turn_index(number):
        return lax.rem(own_group + 1 + number, groups)

    def mix_tile(d, turn, tile_start):
        @pl.loop(0, groups)
        def _(number):
            for each in range(group // chunk):
                inside = pl.multiple_of(turn_index(number) * group + each * chunk, chunk)
                mix(d, turn, inside, pl.multiple_of(tile_start + inside, chunk))

            @pl.when(number > 0)
            def _():
                send_group(d, tile_start, turn_index(number - 1))

        send_group(d, tile_start, turn_index(groups - 1))

    def lag_table():
        lag_count = weights.shape[1]
        offsets = (
            lax.broadcasted_iota(jnp.int32, (1, lag_count), 1) - lag_count // 2
        ).astype(jnp.float32)

        @pl.loop(0, devices)
        def _(slot):
            turned = bins[slot].astype(jnp.float32) * offsets
            phase_rows[pl.ds(2 * slot, 1), :] = turned
            phase_rows[pl.ds(2 * slot + 1, 1), :] = turned

        counts = phase_rows[...]
        wraps = jnp.floor((counts + 0.5) * (1.0 / period_bins))
        sine, cosine = sin_cos(
            (counts - wraps * period_bins) * (math.pi / period_bins) - 0.5 * math.pi
        )
        odd = lax.broadcasted_iota(jnp.int32, counts.shape, 0) % 2 == 1
        weights[...] = jnp.where(odd, -sine, cosine).astype(jnp.bfloat16)

    def mix_piece(d, half, mask):
        block = mate(mask)
        turn = (block * share_rows) // tile
        turn = turn + jnp.where(half == core, 0, tiles // 2)
        inside = lax.rem(block * share_rows, tile)
        to = half * chips + block
        for each in range(share_rows // chunk):
            mix(
                d, turn, pl.multiple_of(inside + each * chunk, chunk),
                pl.multiple_of(to * share_rows + each * chunk, chunk),
            )
        hop = lax.rem(to - me + devices, devices)

        @pl.when(hop != 0)
        def _():
            send_cross(d, hop).start()

    def mix_pieces(d, first, end):
        @pl.loop(first, end)
        def _(mask):
            gather(d, mask).wait()
            swap_piece(d, mask).start()
            mix_piece(d, core, mask)
            swap_piece(d, mask - 1).wait()
            mix_piece(d, other, mask - 1)

    def mix_last_piece(d):
        swap_piece(d, chips - 1).wait()
        mix_piece(d, other, chips - 1)

    first_tiles = (core * (tiles // 2),) + (own_tile + 1,) * (depths - 1)
    for d in range(depths):
        tile_starts = [
            pl.multiple_of(lax.rem(first_tiles[d] + turn, tiles) * tile, tile)
            for turn in range(tiles)
        ]
        if d == 0:
            begin_scatter(0)
            fill_tables()
            loads[1].wait()
            loads[2].wait()
            forward_y(0, source)
            for later in range(1, depths):
                begin_near_scatter(later)
            loads[3].wait()
            forward_y(1, receiver)
            loads[4].wait()
            forward_x()
            for ref in range(3):
                phase_table(0, ref)
                shift(0, ref)
            loads[6].wait()
            loads[7].wait()
            for turn in range(tiles // 2):
                for ref in range(3):
                    inverse(turn, ref, tile_starts[turn])
            for later in range(1, depths):
                begin_trade(later)
            begin_gather(0)
            loads[5].wait()
            if pieced:
                swap_piece(0, 0).start()
                mix_piece(0, core, 0)
            for turn in range(tiles // 2, tiles):
                for ref in range(3):
                    inverse(turn, ref, tile_starts[turn])
            for later in range(1, depths):
                for ref in range(3):
                    phase_table(later, ref)
            if pieced:
                mix_pieces(0, 1, sides)
            for later in range(1, depths):
                begin_near_gather(later)
            if pieced:
                mix_pieces(0, sides, chips)
                mix_last_piece(0)
            else:
                begin_last(0)
                for turn in range(tiles // 2):
                    mix_tile(0, turn, tile_starts[turn])
                swap_last(0).wait()
                for turn in range(tiles // 2, tiles):
                    mix_tile(0, turn, tile_starts[turn])
        else:
            forward_y(0, fields.at[0])
            forward_y(1, fields.at[1])
            forward_x()
            begin_near_last(d)
            for ref in range(3):
                shift(d, ref)
            for turn in range(tiles):
                for ref in range(3):
                    inverse(turn, ref, tile_starts[turn])
                if turn == 0:
                    swap_last(d).wait()
                mix_tile(d, turn, tile_starts[turn])
        received[d, me] = cross[d, me]
    lag_table()
    for d in range(depths):
        @pl.loop(1, devices)
        def _(hop):
            send_cross(d, hop).wait()


def cross_spectra(
    devices, bins, gaps, slab_map, corner, source, receiver, slabs, bracket
):
    depths, rows_x, cols_y = bracket.shape
    slab_count, rows_all, cols_all = slabs.shape
    chips = devices // 2
    share_rows = rows_x // devices
    table_f, table_i = real_transform(rows_x)
    table_y, table_z = (table.T for table in real_transform(cols_y))
    vmem = pl.BlockSpec(memory_space=pltpu.VMEM)
    flops = 8 * rows_x * (rows_x + cols_y) * 4 * cols_y * depths
    dma = pltpu.SemaphoreType.DMA
    held = (depths, chips, share_rows, cols_y)
    field = pltpu.VMEM((2, rows_x, cols_y), jnp.bfloat16)
    return pl.pallas_call(
        functools.partial(window_kernel, devices),
        out_shape=(
            jax.ShapeDtypeStruct((depths, devices, 2, share_rows, cols_y), jnp.bfloat16),
            jax.ShapeDtypeStruct((2 * devices, LAGS), jnp.bfloat16),
        ),
        in_specs=[pl.BlockSpec(memory_space=pltpu.SMEM)] * 4
        + [pl.BlockSpec(memory_space=pltpu.HBM)] * 8,
        out_specs=(vmem, vmem),
        scratch_shapes=[
            pltpu.VMEM(slabs.shape, jnp.bfloat16),
            field,
            pltpu.VMEM(table_y.shape, jnp.bfloat16),
            field,
            pltpu.VMEM(table_f.shape, jnp.bfloat16),
            pltpu.VMEM(table_i.shape, jnp.bfloat16),
            pltpu.VMEM(bracket.shape, jnp.int32),
            pltpu.VMEM(table_z.shape, jnp.bfloat16),
            pltpu.VMEM((rows_x, 4 * cols_y), jnp.bfloat16),
            pltpu.VMEM((rows_x, 4 * cols_y), jnp.float32),
            pltpu.VMEM((rows_x // 2 + strip, cols_y // 2), jnp.float32),
            pltpu.VMEM((2, rows_x // 2 + strip, cols_y // 2), jnp.float32),
            pltpu.VMEM((depths, 3, 2, rows_x // 2 + strip, cols_y), jnp.float32),
            pltpu.VMEM((3, rows_x, 4 * cols_y), jnp.bfloat16),
            pltpu.VMEM((tile, 4 * cols_y), jnp.bfloat16),
            pltpu.VMEM((rows_x // tile, 3, tile, 4 * cols_y), jnp.float32),
            pltpu.VMEM((2, 2, rows_x, cols_y), jnp.bfloat16),
            pltpu.VMEM((depths, devices, 2, share_rows, cols_y), jnp.bfloat16),
            pltpu.VMEM((rows_all, cols_y), jnp.bfloat16),
            pltpu.VMEM((depths, 2, chips, share_rows, cols_y), jnp.bfloat16),
            pltpu.VMEM(held, jnp.bfloat16),
            pltpu.VMEM(held, jnp.bfloat16),
            pltpu.VMEM(held, jnp.bfloat16),
            pltpu.VMEM((depths, 2, share_rows, cols_y), jnp.bfloat16),
            pltpu.VMEM((depths, share_rows, cols_y), jnp.bfloat16),
            pltpu.VMEM((depths, 2, chips, share_rows, cols_y), jnp.bfloat16),
            pltpu.VMEM((2 * devices, LAGS), jnp.float32),
            dma((8,)),
            dma((depths, 4)),
            dma((depths, 2, chips)),
            dma((depths, 2, chips)),
            dma((2, chips)),
            dma((depths, 2, devices)),
        ],
        cost_estimate=pl.CostEstimate(
            flops=flops, bytes_accessed=8 * 1024 * 1024, transcendentals=0
        ),
        compiler_params=pltpu.CompilerParams(
            collective_id=0, has_side_effects=True, vmem_limit_bytes=44 * 1024 * 1024
        ),
    )(
        *[
            pltpu.with_memory_space_constraint(value, pltpu.HBM)
            for value in (
                bins, gaps, slab_map, corner, slabs, source, jnp.asarray(table_y), receiver,
                jnp.asarray(table_f), jnp.asarray(table_i), bracket, jnp.asarray(table_z),
            )
        ]
    )


def image_kernel(scale, crosses, weights, out, held, sems):
    depths, slots, _, rows, cols_y = crosses.shape
    step = min(16, rows)
    part = min(4, step)
    count = depths * (rows // step)

    def block(number, place):
        d = number // (rows // step)
        start = lax.rem(number, rows // step) * step + place * part
        return d, pl.ds(start, part)

    def write(number, place):
        d, local = block(number, place)
        return pltpu.make_async_copy(
            held.at[d, local], out.at[d, local], sems.at[number, place]
        )

    @pl.loop(0, count)
    def _(number):
        d = number // (rows // step)
        start = pl.multiple_of(lax.rem(number, rows // step) * step, step)
        values = crosses[d, :, :, pl.ds(start, step), :]
        values = values.astype(jnp.float32).reshape(2 * slots, step, cols_y)
        values = jnp.swapaxes(values, 0, 1).astype(jnp.bfloat16)
        for row in range(step):
            held[d, start + row] = scale * lax.dot_general(
                values[row], weights[...], (((0,), (0,)), ((), ())),
                preferred_element_type=jnp.float32,
            )
            if row % part == part - 1:
                write(number, row // part).start()

    @pl.loop(0, count)
    def _(number):
        for place in range(step // part):
            write(number, place).wait()


def lag_image(crosses, weights):
    depths, slots, _, rows, cols_y = crosses.shape
    lag_count = weights.shape[1]
    step = min(16, rows)
    whole = pl.BlockSpec(memory_space=pltpu.VMEM)
    image = (depths, rows, cols_y, lag_count)
    return pl.pallas_call(
        functools.partial(image_kernel, slots ** (-0.5)),
        out_shape=jax.ShapeDtypeStruct(image, jnp.float32),
        in_specs=[whole, whole],
        out_specs=pl.BlockSpec(memory_space=pltpu.HBM),
        scratch_shapes=[
            pltpu.VMEM(image, jnp.float32),
            pltpu.SemaphoreType.DMA((depths * (rows // step), step // min(4, step))),
        ],
        compiler_params=pltpu.CompilerParams(vmem_limit_bytes=32 * 1024 * 1024),
    )(crosses, weights)


def shards(
    devices,
    source_field,
    receiver_field,
    slowness_slabs,
    slab_map,
    reference_gaps,
    reference_index,
    frequency_bins,
    shot_corner,
):
    crosses, weights = cross_spectra(
        devices, frequency_bins, reference_gaps, slab_map, shot_corner, source_field[:, 0],
        receiver_field[:, 0], slowness_slabs, reference_index,
    )
    return lag_image(crosses, weights)


def solution(mesh):
    placed = (
        P("grp", "freq", None, None),
        P("grp", "freq", None, None),
        P(("grp", "freq"), None, None),
        P("grp"),
        P("grp", None),
        P("grp", None, None),
        P(),
        P("grp"),
    )
    return jax.shard_map(
        functools.partial(shards, mesh.shape["freq"]),
        mesh=mesh,
        in_specs=placed,
        out_specs=P("grp", "freq", None, None),
        check_vma=False,
    )
```
